512 devices in a mesh: lat: 16 (over x, z_hi, core), lon: 32 (over y, z_lo).
Axes of the slice: x: 4, y: 8, z: 8 (z_hi: 2, z_lo: 4; z = z_hi * 4 + z_lo), core: 2. Of those that a mesh axis runs over, the one named last changes fastest.
Arguments:
- inputs_below: bfloat16 [64, 128, 4096], P(None, 'lat', 'lon'), may hold values from -6 to 6
- hidden_prev: bfloat16 [64, 128, 4096], P(None, 'lat', 'lon'), may hold values from -0.8984375 to 0.8984375
- cell_prev: float32 [64, 128, 4096], P(None, 'lat', 'lon'), may hold values from -5 to 5
- kernel_weights: bfloat16 [9, 256, 128], replicated, may hold values from -0.1875 to 0.1875
- gate_bias: float32 [256], replicated, may hold values from -4 to 4
- readout: float32 [64], replicated, may hold values from -0.75 to 0.75
- target_field: float32 [128, 4096], P('lat', 'lon'), may hold values from -6 to 6
- land_mask: int32 [128, 4096], P('lat', 'lon'), may hold values 0 or 1
- fire_mask: int32 [128, 4096], P('lat', 'lon'), may hold values 0 or 1
- hidden_grad: bfloat16 [64, 128, 4096], P(None, 'lat', 'lon'), may hold values from -10 to 10
Outputs:
- hidden_next: bfloat16 [64, 128, 4096], P(None, 'lat', 'lon')
- cell_next: float32 [64, 128, 4096], P(None, 'lat', 'lon')
- grad_inputs: bfloat16 [64, 128, 4096], P(None, 'lat', 'lon')
- grad_hidden: bfloat16 [64, 128, 4096], P(None, 'lat', 'lon')
- grad_cell: float32 [64, 128, 4096], P(None, 'lat', 'lon')
- grad_kernel: float32 [9, 256, 128], replicated
- grad_bias: float32 [256], replicated
The draws below stay inside these ranges and needn't reach their ends.
Inputs may be any that keep to these rules, and one draw needn't show every extreme that they name: `land_mask`: 1 marks land cells, 0 sea cells. `fire_mask`: 1 marks cells where fire danger is observed.
All inputs are finite; a program needn't handle non-finite values. No bound on the sum of `land_mask` or of `fire_mask` on one device may be relied on, other than what follows from the above.
Results may differ from the reference program's by a relative error of at most 0.0049.
Values may be sent and summed in bfloat16 or wider, within the bound.
A program may use at most 64 MiB of HBM per device.

```python
import math
import jax
import jax.numpy as jnp
from jax import lax

CIN = 64
HID = 64
GATES = 256
NLAT = 128
NLON = 4096


def plant(entries, stream_key, low, top_value):
    extent = entries.shape
    index_at = [jax.random.randint(jax.random.fold_in(stream_key, axis), (), 0, extent[axis]) for axis in range(len(extent))]
    entries = entries.at[tuple(index_at)].set(low)
    longest = extent.index(max(extent))
    index_at[longest] = (index_at[longest] + 1) % extent[longest]
    return entries.at[tuple(index_at)].set(top_value)


def steps_of(key, dims, split, least, high):
    factor_of, own = 1.0, jax.random.fold_in(key, 6)
    for axis_at, parts in split:
        draws = jnp.exp(jax.random.uniform(jax.random.fold_in(own, axis_at), (parts,), jnp.float32, least / len(split), high / len(split)))
        factor_of = factor_of * jnp.repeat(draws, dims[axis_at] // parts).reshape([-1 if axis == axis_at else 1 for axis in range(len(dims))])
    return factor_of


def noise(stream_key, shape, scale, bound, pieces=(), kind=jnp.bfloat16):
    array = scale * jax.random.normal(stream_key, shape, jnp.float32)
    if pieces:
        array = array * steps_of(stream_key, shape, pieces, -0.22, 0.18)
    return jnp.clip(array, -bound, bound).astype(kind)


def setup_inputs(seed: int = 0) -> dict:
    key_list = jax.random.split(jax.random.key(seed), 11)
    inputs_below = noise(key_list[0], (CIN, NLAT, NLON), 1.0, 6.0, ((1, 16), (2, 32)))
    hidden_prev = jnp.clip(jax.random.uniform(key_list[1], (HID, NLAT, NLON), jnp.float32, -0.8984375, 0.8984375) * steps_of(key_list[1], (HID, NLAT, NLON), ((1, 16), (2, 32)), -0.4, 0.0), -0.8984375, 0.8984375).astype(jnp.bfloat16)
    cell_prev = noise(key_list[2], (HID, NLAT, NLON), 1.0, 5.0, ((1, 16), (2, 32)), jnp.float32)
    kernel_weights = noise(key_list[3], (9, GATES, CIN + HID), (9 * (CIN + HID)) ** -0.5, 0.1875)
    gate_bias = noise(key_list[4], (GATES,), 1.0, 4.0, (), jnp.float32)
    readout = noise(key_list[5], (HID,), HID ** -0.5, 0.75, (), jnp.float32)
    target_field = noise(key_list[6], (NLAT, NLON), 1.0, 6.0, ((0, 16), (1, 32)), jnp.float32)
    land_mask = plant((jax.random.randint(key_list[7], (NLAT, NLON), 0, 4) < 3).astype(jnp.int32), jax.random.fold_in(key_list[7], 1), 0, 1)
    fire_mask = plant((jax.random.randint(key_list[8], (NLAT, NLON), 0, 2) < 1).astype(jnp.int32), jax.random.fold_in(key_list[8], 1), 0, 1)
    hidden_grad = noise(key_list[9], (HID, NLAT, NLON), 2.0, 10.0, ((1, 16), (2, 32)))
    return {"inputs_below": inputs_below, "hidden_prev": hidden_prev, "cell_prev": cell_prev, "kernel_weights": kernel_weights, "gate_bias": gate_bias, "readout": readout, "target_field": target_field, "land_mask": land_mask, "fire_mask": fire_mask, "hidden_grad": hidden_grad}


def fold_pad(field):
    halfway = field.shape[2] // 2
    north_row = jnp.roll(field[:, :1], -halfway, axis=2)
    south_row = jnp.roll(field[:, -1:], -halfway, axis=2)
    banded = jnp.concatenate([north_row, field, south_row], axis=1)
    return jnp.concatenate([banded[:, :, -1:], banded, banded[:, :, :1]], axis=2)

def convolve(padded, kernel):
    channels = padded.shape[0]
    row_count = padded.shape[1] - 2
    col_count = padded.shape[2] - 2
    running = jnp.zeros((kernel.shape[1], row_count * col_count), jnp.float32)
    for position in range(9):
        lat_start = position // 3
        lon_start = position % 3
        window = padded[:, lat_start:lat_start + row_count, lon_start:lon_start + col_count].reshape(channels, row_count * col_count)
        running = running + jnp.dot(kernel[position], window, preferred_element_type=jnp.float32, precision=lax.Precision.HIGHEST)
    return running.reshape(kernel.shape[1], row_count, col_count)

def reference(inputs_below, hidden_prev, cell_prev, kernel_weights, gate_bias, readout, target_field, land_mask, fire_mask, hidden_grad):
    stacked = jnp.concatenate([inputs_below, hidden_prev], axis=0)
    padded = fold_pad(stacked)
    preact = convolve(padded, kernel_weights) + gate_bias[:, None, None]
    input_gate = jax.nn.sigmoid(preact[0:HID])
    forget_gate = jax.nn.sigmoid(preact[HID:2 * HID])
    output_gate = jax.nn.sigmoid(preact[2 * HID:3 * HID])
    candidate = jnp.tanh(preact[3 * HID:4 * HID])
    land_float = land_mask.astype(jnp.float32)[None]
    fire_float = fire_mask.astype(jnp.float32)
    cell_next = land_float * (forget_gate * cell_prev + input_gate * candidate)
    squashed = jnp.tanh(cell_next)
    hidden_next = (output_gate * squashed).astype(jnp.bfloat16)
    predicted = lax.optimization_barrier(jnp.sum(readout[:, None, None] * hidden_next.astype(jnp.float32), axis=0))
    total_grad = hidden_grad.astype(jnp.float32) + 2.0 * (fire_float * (predicted - target_field))[None] * readout[:, None, None]
    cell_grad = land_float * total_grad * output_gate * (1.0 - squashed * squashed)
    grad_cell = cell_grad * forget_gate
    pre_grad = jnp.concatenate([cell_grad * candidate * input_gate * (1.0 - input_gate), cell_grad * cell_prev * forget_gate * (1.0 - forget_gate), total_grad * squashed * output_gate * (1.0 - output_gate), cell_grad * input_gate * (1.0 - candidate * candidate)], axis=0)
    pre_low = pre_grad.astype(jnp.bfloat16)
    scaling = 1.0 / math.sqrt(NLAT * NLON)
    grad_bias = lax.optimization_barrier(jnp.sum(pre_grad, axis=(1, 2))) * scaling
    low_flat = pre_low.reshape(4 * HID, NLAT * NLON)
    kernel_grads = []
    for position in range(9):
        lat_start = position // 3
        lon_start = position % 3
        window = padded[:, lat_start:lat_start + NLAT, lon_start:lon_start + NLON].reshape(CIN + HID, NLAT * NLON)
        kernel_grads.append(jnp.dot(low_flat, window.T, preferred_element_type=jnp.float32))
    grad_kernel = jnp.stack(kernel_grads, axis=0) * scaling
    kernel_float = kernel_weights.astype(jnp.float32)

    def linear(values):
        return convolve(fold_pad(values), kernel_float)
    unused_out, pullback = jax.vjp(linear, stacked.astype(jnp.float32))
    field_grad = pullback(pre_low.astype(jnp.float32))[0]
    grad_inputs = field_grad[:CIN].astype(jnp.bfloat16)
    grad_hidden = field_grad[CIN:].astype(jnp.bfloat16)
    return (hidden_next, cell_next, grad_inputs, grad_hidden, grad_cell, grad_kernel, grad_bias)
```

```python
import functools
import math

import jax
import jax.numpy as jnp
from jax import lax
from jax.experimental import pallas as pl
from jax.experimental.pallas import tpu as pltpu
from jax.sharding import PartitionSpec as P

MESH = pl.DeviceIdType.MESH
F32 = jnp.float32
BF16 = jnp.bfloat16
ROWS = 8
COLS = 128
PADDED = ROWS + 2
STATE = 128
GATES = 256
HALF = GATES // 2
LANES = 128
VMEM_SPEC = pl.BlockSpec(memory_space=pltpu.VMEM)
VMEM_LIMIT = 48 * 1024 * 1024


class Place:
    def __init__(self, sizes):
        self.nx, self.ny, self.zh, self.zl = sizes
        self.nz = self.zh * self.zl
        self.nlat = self.nx * self.zh * 2
        self.nlon = self.ny * self.zl
        self.lat = lax.axis_index("lat")
        self.lon = lax.axis_index("lon")
        self.core = lax.rem(self.lat, 2)
        chip = self.lat // 2
        self.z_hi = lax.rem(chip, self.zh)
        self.x = chip // self.zh
        self.z_lo = lax.rem(self.lon, self.zl)
        self.y = self.lon // self.zl
        self.z = self.z_hi * self.zl + self.z_lo
        self.count = {"core": 2, "x": self.nx, "y": self.ny, "z": self.nz}
        self.index = {"core": self.core, "x": self.x, "y": self.y, "z": self.z}
        self.north = self.lat == 0
        self.south = self.lat == self.nlat - 1

    def at(self, x, y, z, core):
        lat = (x * self.zh + z // self.zl) * 2 + core
        lon = y * self.zl + lax.rem(z, self.zl)
        return (lat, lon)

    def peer(self, axis, steps):
        other = lax.rem(self.index[axis] + steps, self.count[axis])
        where = dict(self.index)
        where[axis] = other
        return self.at(where["x"], where["y"], where["z"], where["core"]), other

    def peers(self, axis):
        return [self.peer(axis, steps) for steps in range(1, self.count[axis])]

    def up(self):
        opposite = lax.rem(self.lon + self.nlon // 2, self.nlon)
        lat = jnp.where(self.north, 0, self.lat - 1)
        return (lat, jnp.where(self.north, opposite, self.lon))

    def down(self):
        opposite = lax.rem(self.lon + self.nlon // 2, self.nlon)
        lat = jnp.where(self.south, self.nlat - 1, self.lat + 1)
        return (lat, jnp.where(self.south, opposite, self.lon))

    def east(self):
        return (self.lat, lax.rem(self.lon + 1, self.nlon))

    def west(self):
        return (self.lat, lax.rem(self.lon + self.nlon - 1, self.nlon))

    def around(self):
        return [self.up(), self.down(), self.east(), self.west()]


def greet(devices):
    barrier = pltpu.get_barrier_semaphore()
    for device in devices:
        pl.semaphore_signal(barrier, inc=1, device_id=device, device_id_type=MESH)
    return barrier


def remote(source, target, send_sem, recv_sem, device):
    return pltpu.make_async_remote_copy(
        src_ref=source,
        dst_ref=target,
        send_sem=send_sem,
        recv_sem=recv_sem,
        device_id=device,
        device_id_type=MESH,
    )


def lane_ids(shape):
    return lax.broadcasted_iota(jnp.int32, shape, len(shape) - 1)


def rows_out(place, first, last, halo, send_sem, recv_sem):
    upper_slot = jnp.where(place.north, 0, 1)
    lower_slot = jnp.where(place.south, 1, 0)
    copies = [
        remote(first, halo.at[upper_slot], send_sem.at[0], recv_sem.at[upper_slot], place.up()),
        remote(last, halo.at[lower_slot], send_sem.at[1], recv_sem.at[lower_slot], place.down()),
    ]
    for copy in copies:
        copy.start()
    waits = [
        remote(first, halo.at[0], send_sem.at[0], recv_sem.at[0], place.up()),
        remote(last, halo.at[1], send_sem.at[1], recv_sem.at[1], place.down()),
    ]
    return copies, waits


def collect(total, row, position, shift, lanes):
    return jnp.where(lanes == position, pltpu.roll(row, shift % LANES, 1), total)


def cols_out(place, edges, sides, send_sem, recv_sem):
    copies = [
        remote(edges.at[0], sides.at[0], send_sem.at[0], recv_sem.at[0], place.east()),
        remote(edges.at[1], sides.at[1], send_sem.at[1], recv_sem.at[1], place.west()),
    ]
    for copy in copies:
        copy.start()
    return copies


def halo_kernel(sizes, below, hidden, rows, sides, wide, halo, edges, row_send, row_recv, col_send, col_recv):
    place = Place(sizes)
    barrier = greet(place.around())
    width = below.shape[0]
    wide[pl.ds(0, width * ROWS), :] = below[...].astype(F32).reshape(width * ROWS, COLS)
    wide[pl.ds(width * ROWS, width * ROWS), :] = hidden[...].astype(F32).reshape(width * ROWS, COLS)

    def row_of(r):
        return wide[pl.ds(r, STATE, stride=ROWS), :]

    for r in (0, ROWS - 1):
        rows[r + 1] = row_of(r).astype(BF16)
    pl.semaphore_wait(barrier, 4)
    copies, waits = rows_out(place, rows.at[1], rows.at[ROWS], halo, row_send, row_recv)
    lanes = lane_ids((STATE, COLS))
    east = jnp.zeros((STATE, COLS), F32)
    west = jnp.zeros((STATE, COLS), F32)
    for r in range(ROWS):
        value = row_of(r)
        if 0 < r < ROWS - 1:
            rows[r + 1] = value.astype(BF16)
        east = collect(east, value, r + 1, r + 2, lanes)
        west = collect(west, value, r + 1, r + 1, lanes)
    for slot, position in ((0, 0), (1, ROWS + 1)):
        waits[slot].wait_recv()
        value = halo[slot].astype(F32)
        rows[position] = halo[slot]
        east = collect(east, value, position, position + 1, lanes)
        west = collect(west, value, position, position, lanes)
    edges[0] = east.astype(BF16)
    edges[1] = west.astype(BF16)
    col_copies = cols_out(place, edges, sides, col_send, col_recv)
    for copy in copies:
        copy.wait_send()
    for copy in col_copies:
        copy.wait()


def spread(values, sides_low, sides_high, lanes, position):
    before = jnp.where(lanes == 0, pltpu.roll(sides_low, (-position) % LANES, 1), pltpu.roll(values, 1, 1))
    after = jnp.where(
        lanes == COLS - 1, pltpu.roll(sides_high, (COLS - 1 - position) % LANES, 1), pltpu.roll(values, COLS - 1, 1)
    )
    return before, after


def local_kernel(
    rows,
    sides,
    cell_prev,
    hidden_grad,
    weights,
    gate_bias,
    readout,
    target,
    land,
    fire,
    hidden_next,
    cell_next,
    grad_cell,
    kernel_part,
    bias_part,
    low_rows,
    low_edges,
    windows,
    wide_grad,
    wide_next,
):
    hid = hidden_next.shape[0]
    lanes = lane_ids((STATE, COLS))
    low_side = sides[0].astype(F32)
    high_side = sides[1].astype(F32)
    for position in range(PADDED):
        value = rows[position].astype(F32)
        before, after = spread(value, low_side, high_side, lanes, position)
        windows[position, 0:STATE] = before.astype(BF16)
        windows[position, STATE : 2 * STATE] = rows[position]
        windows[position, 2 * STATE : 3 * STATE] = after.astype(BF16)
    wide_grad[...] = hidden_grad[...].astype(F32).reshape(hid * ROWS, COLS)
    flat = jnp.concatenate([weights[t] for t in range(9)], axis=1)
    bias_cols = jnp.transpose(jnp.broadcast_to(gate_bias[...], (LANES, GATES)))
    read_cols = jnp.transpose(jnp.broadcast_to(readout[...], (LANES, LANES)))[0:hid]
    bias_sum = jnp.zeros((GATES, COLS), F32)
    gate_lanes = lane_ids((GATES, COLS))
    east = jnp.zeros((GATES, COLS), F32)
    west = jnp.zeros((GATES, COLS), F32)
    for pair in range(ROWS // 2):
        first = 2 * pair
        columns = jnp.concatenate(
            [windows[first + k : first + k + 3].reshape(9 * STATE, COLS) for k in range(2)], axis=1
        )
        both = jnp.dot(flat, columns, preferred_element_type=F32)
        for k in range(2):
            r = first + k
            preact = both[:, k * COLS : (k + 1) * COLS] + bias_cols
            input_gate = jax.nn.sigmoid(preact[0:hid])
            forget_gate = jax.nn.sigmoid(preact[hid : 2 * hid])
            output_gate = jax.nn.sigmoid(preact[2 * hid : 3 * hid])
            candidate = jnp.tanh(preact[3 * hid : 4 * hid])
            land_row = land[r : r + 1, :].astype(F32)
            fire_row = fire[r : r + 1, :].astype(F32)
            prev = cell_prev[pl.ds(r, hid, stride=ROWS), :]
            cell = land_row * (forget_gate * prev + input_gate * candidate)
            squashed = jnp.tanh(cell)
            hidden = (output_gate * squashed).astype(BF16).astype(F32)
            predicted = jnp.sum(read_cols * hidden, axis=0, keepdims=True)
            miss = 2.0 * (fire_row * (predicted - target[r : r + 1, :]))
            total_grad = wide_grad[pl.ds(r, hid, stride=ROWS), :] + miss * read_cols
            cell_grad = land_row * total_grad * output_gate * (1.0 - squashed * squashed)
            pre_grad = jnp.concatenate(
                [
                    cell_grad * candidate * input_gate * (1.0 - input_gate),
                    cell_grad * prev * forget_gate * (1.0 - forget_gate),
                    total_grad * squashed * output_gate * (1.0 - output_gate),
                    cell_grad * input_gate * (1.0 - candidate * candidate),
                ],
                axis=0,
            )
            cell_next[pl.ds(r, hid, stride=ROWS), :] = cell
            grad_cell[pl.ds(r, hid, stride=ROWS), :] = cell_grad * forget_gate
            wide_next[pl.ds(r, hid, stride=ROWS), :] = hidden
            bias_sum = bias_sum + pre_grad
            low = pre_grad.astype(BF16)
            low_rows[r] = low
            rounded = low.astype(F32)
            east = collect(east, rounded, r + 1, r + 2, gate_lanes)
            west = collect(west, rounded, r + 1, r + 1, gate_lanes)
    hidden_next[...] = wide_next[...].reshape(hid, ROWS, COLS).astype(BF16)
    low_edges[0] = east
    low_edges[1] = west
    bias_part[...] = lax.dot_general(
        jnp.ones((8, COLS), F32),
        bias_sum,
        (((1,), (1,)), ((), ())),
        precision=lax.Precision.HIGHEST,
        preferred_element_type=F32,
    )
    cells = jnp.concatenate([low_rows[r] for r in range(ROWS)], axis=1)
    for a in range(3):
        seen = jnp.concatenate([windows[r + a] for r in range(ROWS)], axis=1)
        part = lax.dot_general(cells, seen, (((1,), (1,)), ((), ())), preferred_element_type=F32)
        for b in range(3):
            kernel_part[3 * a + b] = part[:, b * STATE : (b + 1) * STATE]


ORDERS = (("y", "z", "x"), ("z", "x", "y"), ("x", "y", "z"))


def reduce_kernel(
    sizes,
    scaling,
    kernel_part,
    bias_part,
    low_rows,
    low_edges,
    kernel_sum,
    bias_sum,
    halo,
    sides,
    pair_in,
    owned,
    bias_at,
    edges,
    first_in,
    second_out,
    second_in,
    third,
    gathered,
    bias_bufs,
    row_send,
    row_recv,
    col_send,
    col_recv,
    sends,
    recvs,
    bias_send,
    bias_recv,
):
    place = Place(sizes)
    partner, _ = place.peer("core", 1)
    devices = [partner] + place.around()
    for axis in ("x", "y", "z"):
        devices += [device for device, _ in place.peers(axis)]
    barrier = greet(devices)
    mine = pl.multiple_of(place.core * HALF, HALF)
    theirs = pl.multiple_of((1 - place.core) * HALF, HALF)
    pending = []
    pl.semaphore_wait(barrier, len(devices))

    pair_copies = []
    for a in range(3):
        copy = remote(
            kernel_part.at[pl.ds(3 * a, 3), pl.ds(theirs, HALF), :],
            pair_in.at[a],
            sends.at[0, a, 0],
            recvs.at[0, a, 0],
            partner,
        )
        copy.start()
        pair_copies.append(copy)

    def bias_start(stage, axis, value):
        slot = place.index[axis]
        buf = bias_bufs[stage]
        buf[slot] = value
        copies = []
        for k, (device, _) in enumerate(place.peers(axis)):
            copy = remote(buf.at[slot], buf.at[slot], bias_send.at[stage, k], bias_recv.at[stage, k], device)
            copy.start()
            copies.append(copy)
        return copies

    def bias_finish(stage, axis, copies):
        buf = bias_bufs[stage]
        for copy in copies:
            copy.wait_recv()
        pending.extend(copies)
        total = buf[0]
        for k in range(1, place.count[axis]):
            total = total + buf[k]
        return total

    bias_copies = bias_start(0, "core", bias_part[...])
    row_copies, row_waits = rows_out(place, low_rows.at[0], low_rows.at[ROWS - 1], halo, row_send, row_recv)

    first_copies = []
    for a in range(3):
        pair_copies[a].wait_recv()
        for b in range(3):
            owned[a, b] = kernel_part[3 * a + b, pl.ds(mine, HALF), :] + pair_in[a, b]
        axis = ORDERS[a][0]
        rows1 = HALF // place.count[axis]
        copies = []
        for k, (device, other) in enumerate(place.peers(axis)):
            start = pl.multiple_of(other * rows1, rows1)
            copy = remote(
                owned.at[a, :, pl.ds(start, rows1), :],
                first_in[a].at[k],
                sends.at[1, a, k],
                recvs.at[1, a, k],
                device,
            )
            copy.start()
            copies.append(copy)
        first_copies.append(copies)
    pending.extend(pair_copies)

    bias = bias_finish(0, "core", bias_copies)
    bias_copies = bias_start(1, "x", bias)

    lanes = lane_ids((GATES, COLS))
    east, west = low_edges[0], low_edges[1]
    for slot, position in ((0, 0), (1, ROWS + 1)):
        row_waits[slot].wait_recv()
        value = halo[slot].astype(F32)
        east = collect(east, value, position, position + 1, lanes)
        west = collect(west, value, position, position, lanes)
    edges[0] = east.astype(BF16)
    edges[1] = west.astype(BF16)
    pending.extend(row_copies)
    col_copies = cols_out(place, edges, sides, col_send, col_recv)

    bias = bias_finish(1, "x", bias_copies)
    bias_copies = bias_start(2, "y", bias)

    second_copies = []
    for a in (2, 0, 1):
        axis1, axis2, _ = ORDERS[a]
        n1, n2 = place.count[axis1], place.count[axis2]
        rows1 = HALF // n1
        rows2 = rows1 // n2
        for copy in first_copies[a]:
            copy.wait_recv()
        pending.extend(first_copies[a])
        start = pl.multiple_of(place.index[axis1] * rows1, rows1)
        total = owned[a, :, pl.ds(start, rows1), :]
        for k in range(n1 - 1):
            total = total + first_in[a][k]
        for p in range(n2):
            second_out[a][p] = total[:, p * rows2 : (p + 1) * rows2, :]
        copies = []
        for k, (device, other) in enumerate(place.peers(axis2)):
            copy = remote(second_out[a].at[other], second_in[a].at[k], sends.at[2, a, k], recvs.at[2, a, k], device)
            copy.start()
            copies.append(copy)
        second_copies.append((a, copies))

    bias = bias_finish(2, "y", bias_copies)
    bias_copies = bias_start(3, "z", bias)

    third_copies = []
    for a, copies2 in second_copies:
        _, axis2, axis3 = ORDERS[a]
        for copy in copies2:
            copy.wait_recv()
        pending.extend(copies2)
        total = second_out[a][place.index[axis2]]
        for k in range(place.count[axis2] - 1):
            total = total + second_in[a][k]
        slot = place.index[axis3]
        third[a][slot] = total
        copies = []
        for k, (device, _) in enumerate(place.peers(axis3)):
            copy = remote(third[a].at[slot], third[a].at[slot], sends.at[3, a, k], recvs.at[3, a, k], device)
            copy.start()
            copies.append(copy)
        third_copies.append((a, copies))

    bias_sum[...] = bias_finish(3, "z", bias_copies) * scaling

    fourth_copies = []
    for a, copies3 in third_copies:
        _, axis2, axis3 = ORDERS[a]
        for copy in copies3:
            copy.wait_recv()
        pending.extend(copies3)
        total = third[a][0]
        for k in range(1, place.count[axis3]):
            total = total + third[a][k]
        slot = place.index[axis2]
        gathered[a][slot] = total * scaling
        copies = []
        for k, (device, _) in enumerate(place.peers(axis2)):
            copy = remote(gathered[a].at[slot], gathered[a].at[slot], sends.at[4, a, k], recvs.at[4, a, k], device)
            copy.start()
            copies.append(copy)
        fourth_copies.append((a, copies))

    fifth_copies = []
    for a, copies4 in fourth_copies:
        axis1, axis2, _ = ORDERS[a]
        rows1 = HALF // place.count[axis1]
        for copy in copies4:
            copy.wait_recv()
        pending.extend(copies4)
        start = pl.multiple_of(mine + place.index[axis1] * rows1, rows1)
        block = kernel_sum.at[pl.ds(3 * a, 3), pl.ds(start, rows1), :]
        block[...] = jnp.concatenate([gathered[a][p] for p in range(place.count[axis2])], axis=1)
        copies = []
        for k, (device, _) in enumerate(place.peers(axis1)):
            copy = remote(block, block, sends.at[5, a, k], recvs.at[5, a, k], device)
            copy.start()
            copies.append(copy)
        fifth_copies.append((a, copies))

    last_copies = []
    for a, copies5 in fifth_copies:
        for copy in copies5:
            copy.wait_recv()
        pending.extend(copies5)
        half = kernel_sum.at[pl.ds(3 * a, 3), pl.ds(mine, HALF), :]
        copy = remote(half, half, sends.at[6, a, 0], recvs.at[6, a, 0], partner)
        copy.start()
        last_copies.append(copy)
    for copy in last_copies:
        copy.wait_recv()
    pending.extend(last_copies)
    for copy in col_copies:
        copy.wait_recv()
    pending.extend(col_copies)
    for copy in pending:
        copy.wait_send()


def field_kernel(sizes, low_rows, halo, sides, weights, grad_inputs, grad_hidden, windows, turned, wide):
    place = Place(sizes)
    width = grad_inputs.shape[0]
    lanes = lane_ids((GATES, COLS))
    low_side = sides[0].astype(F32)
    high_side = sides[1].astype(F32)
    for position in range(PADDED):
        if position == 0:
            low = halo[0]
        elif position == PADDED - 1:
            low = halo[1]
        else:
            low = low_rows[position - 1]
        before, after = spread(low.astype(F32), low_side, high_side, lanes, position)
        windows[position, 0:GATES] = before.astype(BF16)
        windows[position, GATES : 2 * GATES] = low
        windows[position, 2 * GATES : 3 * GATES] = after.astype(BF16)
    for t in range(9):
        turned[t] = jnp.transpose(weights[t].astype(F32)).astype(BF16)
    flipped = jnp.concatenate([turned[8 - q] for q in range(9)], axis=1)
    for pair in range(ROWS // 2):
        first = 2 * pair
        blocks = []
        for k in range(2):
            r = first + k
            pieces = [windows[r + d] for d in range(3)]
            if r == 0:
                pieces[0] = jnp.zeros_like(pieces[0])
            if r == ROWS - 1:
                pieces[2] = jnp.zeros_like(pieces[2])
            blocks.append(jnp.concatenate(pieces, axis=0))
        both = jnp.dot(flipped, jnp.concatenate(blocks, axis=1), preferred_element_type=F32)
        for k in range(2):
            r = first + k
            value = both[:, k * COLS : (k + 1) * COLS]
            if r == 0:
                edge = [turned[jnp.where(place.north, 2 - q, 8 - q)] for q in range(3)]
                value = value + jnp.dot(jnp.concatenate(edge, axis=1), windows[0], preferred_element_type=F32)
            if r == ROWS - 1:
                edge = [turned[jnp.where(place.south, 8 - q, 2 - q)] for q in range(3)]
                value = value + jnp.dot(
                    jnp.concatenate(edge, axis=1), windows[PADDED - 1], preferred_element_type=F32
                )
            wide[pl.ds(r, STATE, stride=ROWS), :] = value
    grad_inputs[...] = wide[pl.ds(0, width * ROWS), :].reshape(width, ROWS, COLS).astype(BF16)
    grad_hidden[...] = wide[pl.ds(width * ROWS, width * ROWS), :].reshape(width, ROWS, COLS).astype(BF16)


def shape_of(shape, dtype):
    return jax.ShapeDtypeStruct(shape, dtype)


def body(
    sizes,
    inputs_below,
    hidden_prev,
    cell_prev,
    kernel_weights,
    gate_bias,
    readout,
    target_field,
    land_mask,
    fire_mask,
    hidden_grad,
):
    nx, ny, zh, zl = sizes
    count = {"x": nx, "y": ny, "z": zh * zl}
    hid = hidden_prev.shape[0]
    dma = pltpu.SemaphoreType.DMA
    rows, sides = pl.pallas_call(
        functools.partial(halo_kernel, sizes),
        out_shape=[shape_of((PADDED, STATE, COLS), BF16), shape_of((2, STATE, COLS), BF16)],
        in_specs=[VMEM_SPEC] * 2,
        out_specs=[VMEM_SPEC] * 2,
        scratch_shapes=[
            pltpu.VMEM((STATE * ROWS, COLS), F32),
            pltpu.VMEM((2, STATE, COLS), BF16),
            pltpu.VMEM((2, STATE, COLS), BF16),
            dma((2,)),
            dma((2,)),
            dma((2,)),
            dma((2,)),
        ],
        compiler_params=pltpu.CompilerParams(
            collective_id=0, has_side_effects=True, vmem_limit_bytes=VMEM_LIMIT
        ),
        name="state_halo",
    )(inputs_below, hidden_prev)

    hidden_next, cell_next, grad_cell, kernel_part, bias_part, low_rows, low_edges = pl.pallas_call(
        local_kernel,
        out_shape=[
            shape_of((hid, ROWS, COLS), BF16),
            shape_of((hid * ROWS, COLS), F32),
            shape_of((hid * ROWS, COLS), F32),
            shape_of((9, GATES, STATE), F32),
            shape_of((8, GATES), F32),
            shape_of((ROWS, GATES, COLS), BF16),
            shape_of((2, GATES, COLS), F32),
        ],
        in_specs=[VMEM_SPEC] * 10,
        out_specs=[VMEM_SPEC] * 7,
        scratch_shapes=[
            pltpu.VMEM((PADDED, 3 * STATE, COLS), BF16),
            pltpu.VMEM((hid * ROWS, COLS), F32),
            pltpu.VMEM((hid * ROWS, COLS), F32),
        ],
        compiler_params=pltpu.CompilerParams(vmem_limit_bytes=VMEM_LIMIT),
        name="cell_step",
    )(
        rows,
        sides,
        cell_prev.reshape(hid * ROWS, COLS),
        hidden_grad,
        kernel_weights,
        gate_bias.reshape(1, GATES),
        jnp.pad(readout, (0, LANES - hid)).reshape(1, LANES),
        target_field,
        land_mask,
        fire_mask,
    )

    scaling = 1.0 / math.sqrt(ROWS * nx * zh * 2 * COLS * ny * zl)
    most = max(nx, ny, zh * zl) - 1
    chunk = []
    for axis1, axis2, axis3 in ORDERS:
        rows1 = HALF // count[axis1]
        chunk.append((count[axis1], rows1, count[axis2], rows1 // count[axis2], count[axis3]))
    kernel_sum, bias_sum, low_halo, low_sides = pl.pallas_call(
        functools.partial(reduce_kernel, sizes, scaling),
        out_shape=[
            shape_of((9, GATES, STATE), F32),
            shape_of((8, GATES), F32),
            shape_of((2, GATES, COLS), BF16),
            shape_of((2, GATES, COLS), BF16),
        ],
        in_specs=[VMEM_SPEC] * 4,
        out_specs=[VMEM_SPEC] * 4,
        scratch_shapes=[
            pltpu.VMEM((3, 3, HALF, STATE), F32),
            pltpu.VMEM((3, 3, HALF, STATE), F32),
            pltpu.VMEM((8, GATES), F32),
            pltpu.VMEM((2, GATES, COLS), BF16),
            [pltpu.VMEM((n1 - 1, 3, r1, STATE), F32) for n1, r1, _, _, _ in chunk],
            [pltpu.VMEM((n2, 3, r2, STATE), F32) for _, _, n2, r2, _ in chunk],
            [pltpu.VMEM((n2 - 1, 3, r2, STATE), F32) for _, _, n2, r2, _ in chunk],
            [pltpu.VMEM((n3, 3, r2, STATE), F32) for _, _, _, r2, n3 in chunk],
            [pltpu.VMEM((n2, 3, r2, STATE), F32) for _, _, n2, r2, _ in chunk],
            [pltpu.VMEM((n, 8, GATES), F32) for n in (2, nx, ny, zh * zl)],
            dma((2,)),
            dma((2,)),
            dma((2,)),
            dma((2,)),
            dma((7, 3, most)),
            dma((7, 3, most)),
            dma((4, most)),
            dma((4, most)),
        ],
        compiler_params=pltpu.CompilerParams(
            collective_id=1, has_side_effects=True, vmem_limit_bytes=VMEM_LIMIT
        ),
        name="kernel_reduce",
    )(kernel_part, bias_part, low_rows, low_edges)

    grad_inputs, grad_hidden = pl.pallas_call(
        functools.partial(field_kernel, sizes),
        out_shape=[shape_of((hid, ROWS, COLS), BF16)] * 2,
        in_specs=[VMEM_SPEC] * 4,
        out_specs=[VMEM_SPEC] * 2,
        scratch_shapes=[
            pltpu.VMEM((PADDED, 3 * GATES, COLS), BF16),
            pltpu.VMEM((9, STATE, GATES), BF16),
            pltpu.VMEM((STATE * ROWS, COLS), F32),
        ],
        compiler_params=pltpu.CompilerParams(vmem_limit_bytes=VMEM_LIMIT),
        name="field_gradient",
    )(low_rows, low_halo, low_sides, kernel_weights)

    shape = (hid, ROWS, COLS)
    return (
        hidden_next,
        cell_next.reshape(shape),
        grad_inputs,
        grad_hidden,
        grad_cell.reshape(shape),
        kernel_sum,
        bias_sum[0],
    )


def solution(mesh):
    lat, lon = mesh.shape["lat"], mesh.shape["lon"]
    sizes = {(16, 32): (4, 8, 2, 4), (4, 4): (2, 2, 1, 2)}[(lat, lon)]
    cells = P(None, "lat", "lon")
    flat = P("lat", "lon")
    return jax.shard_map(
        functools.partial(body, sizes),
        mesh=mesh,
        in_specs=(cells, cells, cells, P(), P(), P(), flat, flat, flat, cells),
        out_specs=(cells, cells, cells, cells, cells, P(), P()),
        check_vma=False,
    )
```

```python
import functools
import math

import jax
import jax.numpy as jnp
from jax import lax
from jax.experimental import pallas as pl
from jax.experimental.pallas import tpu as pltpu
from jax.sharding import PartitionSpec as P

MESH = pl.DeviceIdType.MESH
F32 = jnp.float32
BF16 = jnp.bfloat16
ROWS = 8
COLS = 128
PADDED = ROWS + 2
STATE = 128
GATES = 256
HALF = GATES // 2
LANES = 128
VMEM_SPEC = pl.BlockSpec(memory_space=pltpu.VMEM)
VMEM_LIMIT = 48 * 1024 * 1024


class Place:
    def __init__(self, sizes):
        self.nx, self.ny, self.zh, self.zl = sizes
        self.nz = self.zh * self.zl
        self.nlat = self.nx * self.zh * 2
        self.nlon = self.ny * self.zl
        self.lat = lax.axis_index("lat")
        self.lon = lax.axis_index("lon")
        self.core = lax.rem(self.lat, 2)
        chip = self.lat // 2
        self.z_hi = lax.rem(chip, self.zh)
        self.x = chip // self.zh
        self.z_lo = lax.rem(self.lon, self.zl)
        self.y = self.lon // self.zl
        self.z = self.z_hi * self.zl + self.z_lo
        self.count = {"core": 2, "x": self.nx, "y": self.ny, "z": self.nz}
        self.index = {"core": self.core, "x": self.x, "y": self.y, "z": self.z}
        self.north = self.lat == 0
        self.south = self.lat == self.nlat - 1

    def at(self, x, y, z, core):
        lat = (x * self.zh + z // self.zl) * 2 + core
        lon = y * self.zl + lax.rem(z, self.zl)
        return (lat, lon)

    def peer(self, axis, steps):
        other = lax.rem(self.index[axis] + steps, self.count[axis])
        where = dict(self.index)
        where[axis] = other
        return self.at(where["x"], where["y"], where["z"], where["core"]), other

    def peers(self, axis):
        count = self.count[axis]
        order = sorted(range(1, count), key=lambda steps: min(steps, count - steps))
        return [(steps - 1, *self.peer(axis, steps)) for steps in order]

    def up(self):
        opposite = lax.rem(self.lon + self.nlon // 2, self.nlon)
        lat = jnp.where(self.north, 0, self.lat - 1)
        return (lat, jnp.where(self.north, opposite, self.lon))

    def down(self):
        opposite = lax.rem(self.lon + self.nlon // 2, self.nlon)
        lat = jnp.where(self.south, self.nlat - 1, self.lat + 1)
        return (lat, jnp.where(self.south, opposite, self.lon))

    def east(self):
        return (self.lat, lax.rem(self.lon + 1, self.nlon))

    def west(self):
        return (self.lat, lax.rem(self.lon + self.nlon - 1, self.nlon))

    def around(self):
        return [self.up(), self.down(), self.east(), self.west()]


def greet(devices):
    barrier = pltpu.get_barrier_semaphore()
    for device in devices:
        pl.semaphore_signal(barrier, inc=1, device_id=device, device_id_type=MESH)
    return barrier


def remote(source, target, send_sem, recv_sem, device):
    return pltpu.make_async_remote_copy(
        src_ref=source,
        dst_ref=target,
        send_sem=send_sem,
        recv_sem=recv_sem,
        device_id=device,
        device_id_type=MESH,
    )


def lane_ids(shape):
    return lax.broadcasted_iota(jnp.int32, shape, len(shape) - 1)


def rows_out(place, first, last, halo, send_sem, recv_sem):
    upper_slot = jnp.where(place.north, 0, 1)
    lower_slot = jnp.where(place.south, 1, 0)
    copies = [
        remote(first, halo.at[upper_slot], send_sem.at[0], recv_sem.at[upper_slot], place.up()),
        remote(last, halo.at[lower_slot], send_sem.at[1], recv_sem.at[lower_slot], place.down()),
    ]
    for copy in copies:
        copy.start()
    waits = [
        remote(first, halo.at[0], send_sem.at[0], recv_sem.at[0], place.up()),
        remote(last, halo.at[1], send_sem.at[1], recv_sem.at[1], place.down()),
    ]
    return copies, waits


def collect(total, row, position, shift, lanes):
    return jnp.where(lanes == position, pltpu.roll(row, shift % LANES, 1), total)


def cols_out(place, edges, sides, send_sem, recv_sem):
    copies = [
        remote(edges.at[0], sides.at[0], send_sem.at[0], recv_sem.at[0], place.east()),
        remote(edges.at[1], sides.at[1], send_sem.at[1], recv_sem.at[1], place.west()),
    ]
    for copy in copies:
        copy.start()
    return copies


def spread(values, sides_low, sides_high, lanes, position):
    before = jnp.where(lanes == 0, pltpu.roll(sides_low, (-position) % LANES, 1), pltpu.roll(values, 1, 1))
    after = jnp.where(
        lanes == COLS - 1, pltpu.roll(sides_high, (COLS - 1 - position) % LANES, 1), pltpu.roll(values, COLS - 1, 1)
    )
    return before, after


ORDERS = (("y", "x", "z"), ("z", "x", "y"), ("x", "y", "z"))
EARLY = ((1, 2), (3, 4), (5, 6))
LATE = (0, 7)


def step_kernel(
    sizes,
    scaling,
    below_hbm,
    hidden_hbm,
    cell_hbm,
    weights_hbm,
    gate_bias_hbm,
    readout_hbm,
    target_hbm,
    land_hbm,
    fire_hbm,
    hidden_grad_hbm,
    hidden_next,
    cell_next,
    grad_inputs,
    grad_hidden,
    grad_cell,
    kernel_low,
    bias_sum,
    below,
    hidden,
    cell_prev,
    weights,
    gate_bias,
    readout,
    target,
    land,
    fire,
    hidden_grad,
    wide,
    wide_grad,
    rows,
    halo,
    edges,
    sides,
    corner_edges,
    corners,
    windows,
    kernel_acc,
    turned,
    low_rows,
    low_halo,
    low_edges,
    low_sides,
    low_windows,
    pair_out,
    pair_in,
    owned,
    first_out,
    first_in,
    second_out,
    second_in,
    third,
    gathered,
    bias_bufs,
    load_sem,
    row_send,
    row_recv,
    col_send,
    col_recv,
    sends,
    recvs,
    bias_send,
    bias_recv,
):
    place = Place(sizes)
    hid = hidden_next.shape[0]
    width = grad_inputs.shape[0]
    partner, _ = place.peer("core", 1)
    devices = [partner] + place.around()
    for axis in ("x", "y", "z"):
        devices += [device for _, device, _ in place.peers(axis)]
    barrier = greet(devices)
    mine = pl.multiple_of(place.core * HALF, HALF)
    theirs = pl.multiple_of((1 - place.core) * HALF, HALF)
    pending = []

    sources = (below_hbm, hidden_hbm, weights_hbm, cell_hbm, hidden_grad_hbm, gate_bias_hbm, readout_hbm,
               target_hbm, land_hbm, fire_hbm)
    targets = (below, hidden, weights, cell_prev, hidden_grad, gate_bias, readout, target, land, fire)
    loads = [
        pltpu.make_async_copy(source, destination, load_sem.at[i])
        for i, (source, destination) in enumerate(zip(sources, targets))
    ]
    for load in loads:
        load.start()

    loads[0].wait()
    wide[pl.ds(0, width * ROWS), :] = below[...].astype(F32).reshape(width * ROWS, COLS)
    loads[1].wait()
    wide[pl.ds(width * ROWS, hid * ROWS), :] = hidden[...].astype(F32).reshape(hid * ROWS, COLS)

    def state_row(r):
        return wide[pl.ds(r, STATE, stride=ROWS), :]

    lanes = lane_ids((STATE, COLS))
    east = jnp.zeros((STATE, COLS), F32)
    west = jnp.zeros((STATE, COLS), F32)
    for r in range(ROWS):
        value = state_row(r)
        rows[r + 1] = value.astype(BF16)
        east = collect(east, value, r + 1, r + 2, lanes)
        west = collect(west, value, r + 1, r + 1, lanes)
    edges[0] = east.astype(BF16)
    edges[1] = west.astype(BF16)
    for load in loads[2:]:
        load.wait()
    for t in range(9):
        turned[t] = jnp.transpose(weights[t].astype(F32)).astype(BF16)
    wide_grad[...] = hidden_grad[...].astype(F32).reshape(hid * ROWS, COLS)
    bias_cols = jnp.transpose(jnp.broadcast_to(gate_bias[...], (LANES, GATES)))
    read_cols = jnp.transpose(jnp.broadcast_to(readout[...], (LANES, hid)))

    pl.semaphore_wait(barrier, len(devices))
    row_copies, row_waits = rows_out(place, rows.at[1], rows.at[ROWS], halo, row_send.at[0], row_recv.at[0])
    col_copies = cols_out(place, edges, sides, col_send.at[0], col_recv.at[0])

    corner_east = jnp.zeros((STATE, COLS), F32)
    corner_west = jnp.zeros((STATE, COLS), F32)
    for slot, position in ((0, 0), (1, PADDED - 1)):
        row_waits[slot].wait_recv()
        value = halo[slot].astype(F32)
        corner_east = collect(corner_east, value, position, position + 1, lanes)
        corner_west = collect(corner_west, value, position, position, lanes)
    corner_edges[0] = corner_east.astype(BF16)
    corner_edges[1] = corner_west.astype(BF16)
    corner_copies = cols_out(place, corner_edges, corners, col_send.at[1], col_recv.at[1])
    pending += row_copies + col_copies + corner_copies

    def open_windows(position, low, side_refs):
        value = low.astype(F32)
        before, after = spread(value, side_refs[0].astype(F32), side_refs[1].astype(F32), lanes, position)
        windows[position, 0:STATE] = before.astype(BF16)
        windows[position, STATE : 2 * STATE] = low
        windows[position, 2 * STATE : 3 * STATE] = after.astype(BF16)

    for copy in col_copies:
        copy.wait_recv()
    for position in range(1, PADDED - 1):
        open_windows(position, rows[position], sides)

    flat = jnp.concatenate([weights[t] for t in range(9)], axis=1)

    def cells_of(pair, bias_total):
        columns = jnp.concatenate([windows[r : r + 3].reshape(9 * STATE, COLS) for r in pair], axis=1)
        both = jnp.dot(flat, columns, preferred_element_type=F32)
        for k, r in enumerate(pair):
            preact = both[:, k * COLS : (k + 1) * COLS] + bias_cols
            input_gate = jax.nn.sigmoid(preact[0:hid])
            forget_gate = jax.nn.sigmoid(preact[hid : 2 * hid])
            output_gate = jax.nn.sigmoid(preact[2 * hid : 3 * hid])
            candidate = jnp.tanh(preact[3 * hid : 4 * hid])
            land_row = land[r : r + 1, :].astype(F32)
            fire_row = fire[r : r + 1, :].astype(F32)
            prev = cell_prev[pl.ds(r, hid, stride=ROWS), :]
            cell = land_row * (forget_gate * prev + input_gate * candidate)
            squashed = jnp.tanh(cell)
            new_hidden = (output_gate * squashed).astype(BF16).astype(F32)
            predicted = jnp.sum(read_cols * new_hidden, axis=0, keepdims=True)
            miss = 2.0 * (fire_row * (predicted - target[r : r + 1, :]))
            total_grad = wide_grad[pl.ds(r, hid, stride=ROWS), :] + miss * read_cols
            cell_grad = land_row * total_grad * output_gate * (1.0 - squashed * squashed)
            pre_grad = jnp.concatenate(
                [
                    cell_grad * candidate * input_gate * (1.0 - input_gate),
                    cell_grad * prev * forget_gate * (1.0 - forget_gate),
                    total_grad * squashed * output_gate * (1.0 - output_gate),
                    cell_grad * input_gate * (1.0 - candidate * candidate),
                ],
                axis=0,
            )
            cell_next[pl.ds(r, hid, stride=ROWS), :] = cell
            grad_cell[pl.ds(r, hid, stride=ROWS), :] = cell_grad * forget_gate
            wide[pl.ds(r, hid, stride=ROWS), :] = new_hidden
            bias_total = bias_total + pre_grad
            low_rows[r] = pre_grad.astype(BF16)
        return bias_total

    def kernel_terms(gates, rows_in, a):
        cells = jnp.concatenate([low_rows[r, gates, :] for r in rows_in], axis=1)
        seen = jnp.concatenate([windows[r + a] for r in rows_in], axis=1)
        return lax.dot_general(cells, seen, (((1,), (1,)), ((), ())), preferred_element_type=F32)

    bias_total = jnp.zeros((GATES, COLS), F32)
    for pair in EARLY:
        bias_total = cells_of(pair, bias_total)
    for a in range(3):
        kernel_acc[a] = kernel_terms(slice(None), range(1, ROWS - 1), a)

    for copy in corner_copies:
        copy.wait_recv()
    open_windows(0, halo[0], corners)
    open_windows(PADDED - 1, halo[1], corners)
    bias_total = cells_of(LATE, bias_total)

    pair_copies = []
    for a in range(3):
        part = kernel_acc[a, pl.ds(theirs, HALF), :] + kernel_terms(pl.ds(theirs, HALF), LATE, a)
        for b in range(3):
            pair_out[a, b] = part[:, b * STATE : (b + 1) * STATE].astype(BF16)
        copy = remote(pair_out.at[a], pair_in.at[a], sends.at[0, a, 0], recvs.at[0, a, 0], partner)
        copy.start()
        pair_copies.append(copy)
    for a in range(3):
        part = kernel_acc[a, pl.ds(mine, HALF), :] + kernel_terms(pl.ds(mine, HALF), LATE, a)
        for b in range(3):
            owned[a, b] = part[:, b * STATE : (b + 1) * STATE]

    first_copies = []
    for a in range(3):
        pair_copies[a].wait_recv()
        total = owned[a] + pair_in[a].astype(F32)
        owned[a] = total
        first_out[a] = total.astype(BF16)
        axis = ORDERS[a][0]
        rows1 = HALF // place.count[axis]
        copies = []
        for k, device, other in reversed(place.peers(axis)):
            start = pl.multiple_of(other * rows1, rows1)
            copy = remote(
                first_out.at[a, :, pl.ds(start, rows1), :],
                first_in[a].at[k],
                sends.at[1, a, k],
                recvs.at[1, a, k],
                device,
            )
            copy.start()
            copies.append(copy)
        first_copies.append(copies)
    pending += pair_copies

    def bias_start(stage, axis, value):
        slot = place.index[axis]
        buf = bias_bufs[stage]
        buf[slot] = value
        copies = []
        for k, device, _ in place.peers(axis):
            copy = remote(buf.at[slot], buf.at[slot], bias_send.at[stage, k], bias_recv.at[stage, k], device)
            copy.start()
            copies.append(copy)
        return copies

    def bias_finish(stage, axis, copies):
        buf = bias_bufs[stage]
        for copy in copies:
            copy.wait_recv()
        pending.extend(copies)
        total = buf[0]
        for k in range(1, place.count[axis]):
            total = total + buf[k]
        return total

    bias = lax.dot_general(
        jnp.ones((8, COLS), F32),
        bias_total,
        (((1,), (1,)), ((), ())),
        precision=lax.Precision.HIGHEST,
        preferred_element_type=F32,
    )
    bias_copies = bias_start(0, "core", bias)
    row_copies, row_waits = rows_out(
        place, low_rows.at[0], low_rows.at[ROWS - 1], low_halo, row_send.at[1], row_recv.at[1]
    )
    hidden_next[...] = wide[pl.ds(0, hid * ROWS), :].reshape(hid, ROWS, COLS).astype(BF16)
    gate_lanes = lane_ids((GATES, COLS))
    east = jnp.zeros((GATES, COLS), F32)
    west = jnp.zeros((GATES, COLS), F32)
    for r in range(ROWS):
        value = low_rows[r].astype(F32)
        east = collect(east, value, r + 1, r + 2, gate_lanes)
        west = collect(west, value, r + 1, r + 1, gate_lanes)
    bias = bias_finish(0, "core", bias_copies)
    bias_copies = bias_start(1, "x", bias)
    for slot, position in ((0, 0), (1, PADDED - 1)):
        row_waits[slot].wait_recv()
        value = low_halo[slot].astype(F32)
        east = collect(east, value, position, position + 1, gate_lanes)
        west = collect(west, value, position, position, gate_lanes)
    low_edges[0] = east.astype(BF16)
    low_edges[1] = west.astype(BF16)
    low_copies = cols_out(place, low_edges, low_sides, col_send.at[2], col_recv.at[2])
    pending += row_copies + low_copies
    bias = bias_finish(1, "x", bias_copies)
    bias_copies = bias_start(2, "y", bias)

    second_copies = []
    for a in (2, 0, 1):
        axis1, axis2, _ = ORDERS[a]
        n1, n2 = place.count[axis1], place.count[axis2]
        rows1 = HALF // n1
        rows2 = rows1 // n2
        for copy in reversed(first_copies[a]):
            copy.wait_recv()
        pending += first_copies[a]
        start = pl.multiple_of(place.index[axis1] * rows1, rows1)
        total = owned[a, :, pl.ds(start, rows1), :]
        for k in range(n1 - 1):
            total = total + first_in[a][k].astype(F32)
        for p in range(n2):
            second_out[a][p] = total[:, p * rows2 : (p + 1) * rows2, :]
        copies = []
        for k, device, other in reversed(place.peers(axis2)):
            copy = remote(second_out[a].at[other], second_in[a].at[k], sends.at[2, a, k], recvs.at[2, a, k], device)
            copy.start()
            copies.append(copy)
        second_copies.append((a, copies))

    bias = bias_finish(2, "y", bias_copies)
    bias_copies = bias_start(3, "z", bias)

    third_copies = []
    for a, copies2 in second_copies:
        _, axis2, axis3 = ORDERS[a]
        for copy in reversed(copies2):
            copy.wait_recv()
        pending += copies2
        total = second_out[a][place.index[axis2]]
        for k in range(place.count[axis2] - 1):
            total = total + second_in[a][k]
        slot = place.index[axis3]
        third[a][slot] = total
        copies = []
        for k, device, _ in reversed(place.peers(axis3)):
            copy = remote(third[a].at[slot], third[a].at[slot], sends.at[3, a, k], recvs.at[3, a, k], device)
            copy.start()
            copies.append(copy)
        third_copies.append((a, copies))

    bias_sum[...] = bias_finish(3, "z", bias_copies) * scaling

    fourth_copies = []
    for a, copies3 in third_copies:
        _, axis2, axis3 = ORDERS[a]
        for copy in reversed(copies3):
            copy.wait_recv()
        pending += copies3
        total = third[a][0]
        for k in range(1, place.count[axis3]):
            total = total + third[a][k]
        slot = place.index[axis2]
        gathered[a][slot] = total * scaling
        copies = []
        for k, device, _ in reversed(place.peers(axis2)):
            copy = remote(gathered[a].at[slot], gathered[a].at[slot], sends.at[4, a, k], recvs.at[4, a, k], device)
            copy.start()
            copies.append(copy)
        fourth_copies.append((a, copies))

    def block_of(a, owner):
        rows1 = HALF // place.count[ORDERS[a][0]]
        start = pl.multiple_of(mine + owner * rows1, rows1)
        return kernel_low.at[pl.ds(3 * a, 3), pl.ds(start, rows1), :]

    last_copies = []

    def forward(a, owner, slot):
        block = block_of(a, owner)
        copy = remote(block, block, sends.at[6, a, slot], recvs.at[6, a, slot], partner)
        copy.start()
        last_copies.append(copy)

    fifth_copies = []
    for a, copies4 in fourth_copies:
        axis1, axis2, _ = ORDERS[a]
        n1 = place.count[axis1]
        for copy in reversed(copies4):
            copy.wait_recv()
        pending += copies4
        block = block_of(a, place.index[axis1])
        block[...] = jnp.concatenate([gathered[a][p] for p in range(place.count[axis2])], axis=1).astype(BF16)
        copies = []
        for k, device, _ in reversed(place.peers(axis1)):
            copy = remote(block, block, sends.at[5, a, k], recvs.at[5, a, k], device)
            copy.start()
            copies.append((copy, k, lax.rem(place.index[axis1] + n1 - 1 - k, n1)))
        forward(a, place.index[axis1], n1 - 1)
        fifth_copies.append((a, copies))

    for copy in low_copies:
        copy.wait_recv()
    low_side = low_sides[0].astype(F32)
    high_side = low_sides[1].astype(F32)
    for position in range(PADDED):
        if position == 0:
            low = low_halo[0]
        elif position == PADDED - 1:
            low = low_halo[1]
        else:
            low = low_rows[position - 1]
        before, after = spread(low.astype(F32), low_side, high_side, gate_lanes, position)
        low_windows[position, 0:GATES] = before.astype(BF16)
        low_windows[position, GATES : 2 * GATES] = low
        low_windows[position, 2 * GATES : 3 * GATES] = after.astype(BF16)
    flipped = jnp.concatenate([turned[8 - q] for q in range(9)], axis=1)
    for pair in range(ROWS // 2):
        first = 2 * pair
        blocks = []
        for k in range(2):
            r = first + k
            pieces = [low_windows[r + d] for d in range(3)]
            if r == 0:
                pieces[0] = jnp.zeros_like(pieces[0])
            if r == ROWS - 1:
                pieces[2] = jnp.zeros_like(pieces[2])
            blocks.append(jnp.concatenate(pieces, axis=0))
        both = jnp.dot(flipped, jnp.concatenate(blocks, axis=1), preferred_element_type=F32)
        for k in range(2):
            r = first + k
            value = both[:, k * COLS : (k + 1) * COLS]
            if r == 0:
                edge = [turned[jnp.where(place.north, 2 - q, 8 - q)] for q in range(3)]
                value = value + jnp.dot(jnp.concatenate(edge, axis=1), low_windows[0], preferred_element_type=F32)
            if r == ROWS - 1:
                edge = [turned[jnp.where(place.south, 8 - q, 2 - q)] for q in range(3)]
                value = value + jnp.dot(
                    jnp.concatenate(edge, axis=1), low_windows[PADDED - 1], preferred_element_type=F32
                )
            wide[pl.ds(r, STATE, stride=ROWS), :] = value
    grad_inputs[...] = wide[pl.ds(0, width * ROWS), :].reshape(width, ROWS, COLS).astype(BF16)
    grad_hidden[...] = wide[pl.ds(width * ROWS, hid * ROWS), :].reshape(hid, ROWS, COLS).astype(BF16)

    for a, copies5 in fifth_copies:
        for copy, k, sender in reversed(copies5):
            copy.wait_recv()
            forward(a, sender, k)
            pending.append(copy)
    for copy in last_copies:
        copy.wait_recv()
    pending += last_copies
    for copy in pending:
        copy.wait_send()


def finish_kernel(
    hidden_next,
    cell_next,
    grad_inputs,
    grad_hidden,
    grad_cell,
    kernel_low,
    bias_sum,
    hidden_next_out,
    cell_next_out,
    grad_inputs_out,
    grad_hidden_out,
    grad_cell_out,
    kernel_out,
    bias_out,
    kernel_wide,
    sems,
):
    pairs = (
        (hidden_next, hidden_next_out),
        (cell_next, cell_next_out),
        (grad_inputs, grad_inputs_out),
        (grad_hidden, grad_hidden_out),
        (grad_cell, grad_cell_out),
        (bias_sum.at[0:1], bias_out),
    )
    copies = [pltpu.make_async_copy(source, target, sems.at[i]) for i, (source, target) in enumerate(pairs)]
    for copy in copies:
        copy.start()
    for a in range(3):
        taps = pl.ds(3 * a, 3)
        kernel_wide[taps] = kernel_low[taps].astype(F32)
        copy = pltpu.make_async_copy(kernel_wide.at[taps], kernel_out.at[taps], sems.at[len(pairs) + a])
        copy.start()
        copies.append(copy)
    for copy in copies:
        copy.wait()


def shape_of(shape, dtype):
    return jax.ShapeDtypeStruct(shape, dtype)


def body(
    sizes,
    inputs_below,
    hidden_prev,
    cell_prev,
    kernel_weights,
    gate_bias,
    readout,
    target_field,
    land_mask,
    fire_mask,
    hidden_grad,
):
    nx, ny, zh, zl = sizes
    count = {"x": nx, "y": ny, "z": zh * zl}
    hid = hidden_prev.shape[0]
    dma = pltpu.SemaphoreType.DMA
    scaling = 1.0 / math.sqrt(ROWS * nx * zh * 2 * COLS * ny * zl)
    most = max(nx, ny, zh * zl)
    chunk = []
    for axis1, axis2, axis3 in ORDERS:
        rows1 = HALF // count[axis1]
        chunk.append((count[axis1], rows1, count[axis2], rows1 // count[axis2], count[axis3]))
    cells = shape_of((hid, ROWS, COLS), BF16)
    wide_cells = shape_of((hid * ROWS, COLS), F32)
    inputs = (
        inputs_below,
        hidden_prev,
        cell_prev.reshape(hid * ROWS, COLS),
        kernel_weights,
        gate_bias.reshape(1, GATES),
        readout.reshape(1, hid),
        target_field,
        land_mask,
        fire_mask,
        hidden_grad,
    )
    results = pl.pallas_call(
        functools.partial(step_kernel, sizes, scaling),
        out_shape=[
            cells,
            wide_cells,
            cells,
            cells,
            wide_cells,
            shape_of((9, GATES, STATE), BF16),
            shape_of((8, GATES), F32),
        ],
        in_specs=[pl.BlockSpec(memory_space=pltpu.HBM)] * len(inputs),
        out_specs=[VMEM_SPEC] * 7,
        scratch_shapes=[pltpu.VMEM(value.shape, value.dtype) for value in inputs]
        + [
            pltpu.VMEM((STATE * ROWS, COLS), F32),
            pltpu.VMEM((hid * ROWS, COLS), F32),
            pltpu.VMEM((PADDED, STATE, COLS), BF16),
            pltpu.VMEM((2, STATE, COLS), BF16),
            pltpu.VMEM((2, STATE, COLS), BF16),
            pltpu.VMEM((2, STATE, COLS), BF16),
            pltpu.VMEM((2, STATE, COLS), BF16),
            pltpu.VMEM((2, STATE, COLS), BF16),
            pltpu.VMEM((PADDED, 3 * STATE, COLS), BF16),
            pltpu.VMEM((3, GATES, 3 * STATE), F32),
            pltpu.VMEM((9, STATE, GATES), BF16),
            pltpu.VMEM((ROWS, GATES, COLS), BF16),
            pltpu.VMEM((2, GATES, COLS), BF16),
            pltpu.VMEM((2, GATES, COLS), BF16),
            pltpu.VMEM((2, GATES, COLS), BF16),
            pltpu.VMEM((PADDED, 3 * GATES, COLS), BF16),
            pltpu.VMEM((3, 3, HALF, STATE), BF16),
            pltpu.VMEM((3, 3, HALF, STATE), BF16),
            pltpu.VMEM((3, 3, HALF, STATE), F32),
            pltpu.VMEM((3, 3, HALF, STATE), BF16),
            [pltpu.VMEM((n1 - 1, 3, r1, STATE), BF16) for n1, r1, _, _, _ in chunk],
            [pltpu.VMEM((n2, 3, r2, STATE), F32) for _, _, n2, r2, _ in chunk],
            [pltpu.VMEM((n2 - 1, 3, r2, STATE), F32) for _, _, n2, r2, _ in chunk],
            [pltpu.VMEM((n3, 3, r2, STATE), F32) for _, _, _, r2, n3 in chunk],
            [pltpu.VMEM((n2, 3, r2, STATE), F32) for _, _, n2, r2, _ in chunk],
            [pltpu.VMEM((n, 8, GATES), F32) for n in (2, nx, ny, zh * zl)],
            dma((len(inputs),)),
            dma((2, 2)),
            dma((2, 2)),
            dma((3, 2)),
            dma((3, 2)),
            dma((7, 3, most)),
            dma((7, 3, most)),
            dma((4, most)),
            dma((4, most)),
        ],
        compiler_params=pltpu.CompilerParams(
            collective_id=0, has_side_effects=True, vmem_limit_bytes=VMEM_LIMIT
        ),
        name="whole_step",
    )(*[pltpu.with_memory_space_constraint(value, pltpu.HBM) for value in inputs])

    hidden_next, cell_next, grad_inputs, grad_hidden, grad_cell, grad_kernel, grad_bias = pl.pallas_call(
        finish_kernel,
        out_shape=[
            cells,
            wide_cells,
            cells,
            cells,
            wide_cells,
            shape_of((9, GATES, STATE), F32),
            shape_of((1, GATES), F32),
        ],
        in_specs=[VMEM_SPEC] * 7,
        out_specs=[pl.BlockSpec(memory_space=pltpu.HBM)] * 7,
        scratch_shapes=[pltpu.VMEM((9, GATES, STATE), F32), dma((9,))],
        compiler_params=pltpu.CompilerParams(vmem_limit_bytes=VMEM_LIMIT),
        name="results",
    )(*results)
    shape = (hid, ROWS, COLS)
    return (
        hidden_next,
        cell_next.reshape(shape),
        grad_inputs,
        grad_hidden,
        grad_cell.reshape(shape),
        grad_kernel,
        grad_bias.reshape(GATES),
    )


def solution(mesh):
    lat, lon = mesh.shape["lat"], mesh.shape["lon"]
    sizes = {(16, 32): (4, 8, 2, 4), (4, 4): (2, 2, 1, 2)}[(lat, lon)]
    cells = P(None, "lat", "lon")
    flat = P("lat", "lon")
    return jax.shard_map(
        functools.partial(body, sizes),
        mesh=mesh,
        in_specs=(cells, cells, cells, P(), P(), P(), flat, flat, flat, cells),
        out_specs=(cells, cells, cells, cells, cells, P(), P()),
        check_vma=False,
    )
```

```python
import functools
import math

import jax
import jax.numpy as jnp
from jax import lax
from jax.experimental import pallas as pl
from jax.experimental.pallas import tpu as pltpu
from jax.sharding import PartitionSpec as P

MESH = pl.DeviceIdType.MESH
F32 = jnp.float32
BF16 = jnp.bfloat16
ROWS = 8
COLS = 128
PADDED = ROWS + 2
STATE = 128
GATES = 256
HALF = GATES // 2
LANES = 128
EDGE = 16
VMEM_SPEC = pl.BlockSpec(memory_space=pltpu.VMEM)
VMEM_LIMIT = 48 * 1024 * 1024


class Place:
    def __init__(self, sizes):
        self.nx, self.ny, self.zh, self.zl = sizes
        self.nz = self.zh * self.zl
        self.nlat = self.nx * self.zh * 2
        self.nlon = self.ny * self.zl
        self.lat = lax.axis_index("lat")
        self.lon = lax.axis_index("lon")
        self.core = lax.rem(self.lat, 2)
        chip = self.lat // 2
        self.z_hi = lax.rem(chip, self.zh)
        self.x = chip // self.zh
        self.z_lo = lax.rem(self.lon, self.zl)
        self.y = self.lon // self.zl
        self.z = self.z_hi * self.zl + self.z_lo
        self.count = {"core": 2, "x": self.nx, "y": self.ny, "z": self.nz}
        self.index = {"core": self.core, "x": self.x, "y": self.y, "z": self.z}
        self.north = self.lat == 0
        self.south = self.lat == self.nlat - 1

    def at(self, x, y, z, core):
        lat = (x * self.zh + z // self.zl) * 2 + core
        lon = y * self.zl + lax.rem(z, self.zl)
        return (lat, lon)

    def peer(self, axis, steps):
        other = lax.rem(self.index[axis] + steps, self.count[axis])
        where = dict(self.index)
        where[axis] = other
        return self.at(where["x"], where["y"], where["z"], where["core"]), other

    def peers(self, axis):
        count = self.count[axis]
        order = sorted(range(1, count), key=lambda steps: min(steps, count - steps))
        return [(steps - 1, *self.peer(axis, steps)) for steps in order]

    def up(self):
        opposite = lax.rem(self.lon + self.nlon // 2, self.nlon)
        lat = jnp.where(self.north, 0, self.lat - 1)
        return (lat, jnp.where(self.north, opposite, self.lon))

    def down(self):
        opposite = lax.rem(self.lon + self.nlon // 2, self.nlon)
        lat = jnp.where(self.south, self.nlat - 1, self.lat + 1)
        return (lat, jnp.where(self.south, opposite, self.lon))

    def east(self):
        return (self.lat, lax.rem(self.lon + 1, self.nlon))

    def west(self):
        return (self.lat, lax.rem(self.lon + self.nlon - 1, self.nlon))

    def around(self):
        return [self.up(), self.down(), self.east(), self.west()]


def greet(devices):
    barrier = pltpu.get_barrier_semaphore()
    for device in devices:
        pl.semaphore_signal(barrier, inc=1, device_id=device, device_id_type=MESH)
    return barrier


def remote(source, target, send_sem, recv_sem, device):
    return pltpu.make_async_remote_copy(
        src_ref=source,
        dst_ref=target,
        send_sem=send_sem,
        recv_sem=recv_sem,
        device_id=device,
        device_id_type=MESH,
    )


def lane_ids(shape):
    return lax.broadcasted_iota(jnp.int32, shape, len(shape) - 1)


def rows_out(place, first, last, halo, send_sem, recv_sem):
    upper_slot = jnp.where(place.north, 0, 1)
    lower_slot = jnp.where(place.south, 1, 0)
    copies = [
        remote(first, halo.at[upper_slot], send_sem.at[0], recv_sem.at[upper_slot], place.up()),
        remote(last, halo.at[lower_slot], send_sem.at[1], recv_sem.at[lower_slot], place.down()),
    ]
    for copy in copies:
        copy.start()
    waits = [
        remote(first, halo.at[0], send_sem.at[0], recv_sem.at[0], place.up()),
        remote(last, halo.at[1], send_sem.at[1], recv_sem.at[1], place.down()),
    ]
    return copies, waits


def to_edge(total):
    return jnp.transpose(total)[0:EDGE].astype(BF16)


def from_edge(edge):
    rest = jnp.zeros((LANES - EDGE, edge.shape[1]), F32)
    return jnp.transpose(jnp.concatenate([edge.astype(F32), rest], axis=0))


def collect(total, row, position, shift, lanes):
    return jnp.where(lanes == position, pltpu.roll(row, shift % LANES, 1), total)


def cols_out(place, edges, sides, send_sem, recv_sem):
    copies = [
        remote(edges.at[0], sides.at[0], send_sem.at[0], recv_sem.at[0], place.east()),
        remote(edges.at[1], sides.at[1], send_sem.at[1], recv_sem.at[1], place.west()),
    ]
    for copy in copies:
        copy.start()
    return copies


def spread(values, sides_low, sides_high, lanes, position):
    before = jnp.where(lanes == 0, pltpu.roll(sides_low, (-position) % LANES, 1), pltpu.roll(values, 1, 1))
    after = jnp.where(
        lanes == COLS - 1, pltpu.roll(sides_high, (COLS - 1 - position) % LANES, 1), pltpu.roll(values, COLS - 1, 1)
    )
    return before, after


ORDERS = (("y", "x", "z"), ("z", "x", "y"), ("x", "y", "z"))
EARLY = ((1, 2), (3, 4), (5, 6))
LATE = (0, 7)


def step_kernel(
    sizes,
    scaling,
    below_hbm,
    hidden_hbm,
    cell_hbm,
    weights_hbm,
    gate_bias_hbm,
    readout_hbm,
    target_hbm,
    land_hbm,
    fire_hbm,
    hidden_grad_hbm,
    hidden_next,
    cell_next,
    grad_inputs,
    grad_hidden,
    grad_cell,
    kernel_low,
    bias_sum,
    below,
    hidden,
    cell_prev,
    weights,
    gate_bias,
    readout,
    target,
    land,
    fire,
    hidden_grad,
    wide,
    wide_grad,
    rows,
    halo,
    edges,
    sides,
    corner_edges,
    corners,
    windows,
    kernel_acc,
    turned,
    low_rows,
    field,
    rims,
    low_halo,
    low_edges,
    low_sides,
    low_windows,
    pair_out,
    pair_in,
    owned,
    first_out,
    first_in,
    second_out,
    second_in,
    third,
    gathered,
    bias_bufs,
    load_sem,
    row_send,
    row_recv,
    col_send,
    col_recv,
    sends,
    recvs,
    bias_send,
    bias_recv,
):
    place = Place(sizes)
    hid = hidden_next.shape[0]
    width = grad_inputs.shape[0]
    partner, _ = place.peer("core", 1)
    devices = place.around()
    for axis in ("z", "y", "x"):
        devices += [device for _, device, _ in reversed(place.peers(axis))]
    devices.append(partner)
    barrier = greet(devices)
    mine = pl.multiple_of(place.core * HALF, HALF)
    theirs = pl.multiple_of((1 - place.core) * HALF, HALF)
    pending = []

    sources = (below_hbm, hidden_hbm, weights_hbm, cell_hbm, hidden_grad_hbm, gate_bias_hbm, readout_hbm,
               target_hbm, land_hbm, fire_hbm)
    targets = (below, hidden, weights, cell_prev, hidden_grad, gate_bias, readout, target, land, fire)
    loads = [
        pltpu.make_async_copy(source, destination, load_sem.at[i])
        for i, (source, destination) in enumerate(zip(sources, targets))
    ]
    for load in loads:
        load.start()

    loads[0].wait()
    wide[pl.ds(0, width * ROWS), :] = below[...].astype(F32).reshape(width * ROWS, COLS)
    loads[1].wait()
    wide[pl.ds(width * ROWS, hid * ROWS), :] = hidden[...].astype(F32).reshape(hid * ROWS, COLS)

    def state_row(r):
        return wide[pl.ds(r, STATE, stride=ROWS), :]

    for r in (0, ROWS - 1):
        rows[r + 1] = state_row(r).astype(BF16)
    pl.semaphore_wait(barrier, len(devices))
    row_copies, row_waits = rows_out(place, rows.at[1], rows.at[ROWS], halo, row_send.at[0], row_recv.at[0])

    lanes = lane_ids((STATE, COLS))
    east = jnp.zeros((STATE, COLS), F32)
    west = jnp.zeros((STATE, COLS), F32)
    for r in range(ROWS):
        value = state_row(r)
        if 0 < r < ROWS - 1:
            rows[r + 1] = value.astype(BF16)
        east = collect(east, value, r + 1, r + 2, lanes)
        west = collect(west, value, r + 1, r + 1, lanes)
    edges[0] = to_edge(east)
    edges[1] = to_edge(west)
    col_copies = cols_out(place, edges, sides, col_send.at[0], col_recv.at[0])

    for load in loads[2:]:
        load.wait()
    wide_grad[...] = hidden_grad[...].astype(F32).reshape(hid * ROWS, COLS)
    bias_cols = jnp.transpose(jnp.broadcast_to(gate_bias[...], (LANES, GATES)))
    read_cols = jnp.transpose(jnp.broadcast_to(readout[...], (LANES, hid)))
    for t in range(9):
        turned[t] = jnp.transpose(weights[t].astype(F32)).astype(BF16)

    corner_east = jnp.zeros((STATE, COLS), F32)
    corner_west = jnp.zeros((STATE, COLS), F32)
    for slot, position in ((0, 0), (1, PADDED - 1)):
        row_waits[slot].wait_recv()
        value = halo[slot].astype(F32)
        corner_east = collect(corner_east, value, position, position + 1, lanes)
        corner_west = collect(corner_west, value, position, position, lanes)
    corner_edges[0] = to_edge(corner_east)
    corner_edges[1] = to_edge(corner_west)
    corner_copies = cols_out(place, corner_edges, corners, col_send.at[1], col_recv.at[1])
    pending += row_copies + col_copies + corner_copies

    def open_windows(position, low, low_side, high_side):
        value = low.astype(F32)
        before, after = spread(value, low_side, high_side, lanes, position)
        windows[position, 0:STATE] = before.astype(BF16)
        windows[position, STATE : 2 * STATE] = low
        windows[position, 2 * STATE : 3 * STATE] = after.astype(BF16)

    for copy in col_copies:
        copy.wait_recv()
    low_side, high_side = from_edge(sides[0]), from_edge(sides[1])
    for position in range(1, PADDED - 1):
        open_windows(position, rows[position], low_side, high_side)

    flat = jnp.concatenate([weights[t] for t in range(9)], axis=1)

    def cells_of(pair, bias_total):
        columns = jnp.concatenate([windows[r : r + 3].reshape(9 * STATE, COLS) for r in pair], axis=1)
        both = jnp.dot(flat, columns, preferred_element_type=F32)
        for k, r in enumerate(pair):
            preact = both[:, k * COLS : (k + 1) * COLS] + bias_cols
            input_gate = jax.nn.sigmoid(preact[0:hid])
            forget_gate = jax.nn.sigmoid(preact[hid : 2 * hid])
            output_gate = jax.nn.sigmoid(preact[2 * hid : 3 * hid])
            candidate = jnp.tanh(preact[3 * hid : 4 * hid])
            land_row = land[r : r + 1, :].astype(F32)
            fire_row = fire[r : r + 1, :].astype(F32)
            prev = cell_prev[pl.ds(r, hid, stride=ROWS), :]
            cell = land_row * (forget_gate * prev + input_gate * candidate)
            squashed = jnp.tanh(cell)
            new_hidden = (output_gate * squashed).astype(BF16).astype(F32)
            predicted = jnp.sum(read_cols * new_hidden, axis=0, keepdims=True)
            miss = 2.0 * (fire_row * (predicted - target[r : r + 1, :]))
            total_grad = wide_grad[pl.ds(r, hid, stride=ROWS), :] + miss * read_cols
            cell_grad = land_row * total_grad * output_gate * (1.0 - squashed * squashed)
            pre_grad = jnp.concatenate(
                [
                    cell_grad * candidate * input_gate * (1.0 - input_gate),
                    cell_grad * prev * forget_gate * (1.0 - forget_gate),
                    total_grad * squashed * output_gate * (1.0 - output_gate),
                    cell_grad * input_gate * (1.0 - candidate * candidate),
                ],
                axis=0,
            )
            cell_next[pl.ds(r, hid, stride=ROWS), :] = cell
            grad_cell[pl.ds(r, hid, stride=ROWS), :] = cell_grad * forget_gate
            wide[pl.ds(r, hid, stride=ROWS), :] = new_hidden
            bias_total = bias_total + pre_grad
            low_rows[r] = pre_grad.astype(BF16)
        return bias_total

    def kernel_terms(gates, rows_in, a):
        cells = jnp.concatenate([low_rows[r, gates, :] for r in rows_in], axis=1)
        seen = jnp.concatenate([windows[r + a] for r in rows_in], axis=1)
        return lax.dot_general(cells, seen, (((1,), (1,)), ((), ())), preferred_element_type=F32)

    bias_total = jnp.zeros((GATES, COLS), F32)
    for pair in EARLY:
        bias_total = cells_of(pair, bias_total)
    for a in range(3):
        kernel_acc[a] = kernel_terms(slice(None), range(1, ROWS - 1), a)

    for copy in corner_copies:
        copy.wait_recv()
    low_side, high_side = from_edge(corners[0]), from_edge(corners[1])
    open_windows(0, halo[0], low_side, high_side)
    open_windows(PADDED - 1, halo[1], low_side, high_side)
    bias_total = cells_of(LATE, bias_total)

    pair_copies = []
    for a in range(3):
        part = kernel_acc[a, pl.ds(theirs, HALF), :] + kernel_terms(pl.ds(theirs, HALF), LATE, a)
        for b in range(3):
            pair_out[a, b] = part[:, b * STATE : (b + 1) * STATE].astype(BF16)
        copy = remote(pair_out.at[a], pair_in.at[a], sends.at[0, a, 0], recvs.at[0, a, 0], partner)
        copy.start()
        pair_copies.append(copy)
    for a in range(3):
        part = kernel_acc[a, pl.ds(mine, HALF), :] + kernel_terms(pl.ds(mine, HALF), LATE, a)
        for b in range(3):
            owned[a, b] = part[:, b * STATE : (b + 1) * STATE]

    first_copies = []
    for a in range(3):
        pair_copies[a].wait_recv()
        total = owned[a] + pair_in[a].astype(F32)
        owned[a] = total
        first_out[a] = total.astype(BF16)
        axis = ORDERS[a][0]
        rows1 = HALF // place.count[axis]
        copies = []
        for k, device, other in reversed(place.peers(axis)):
            start = pl.multiple_of(other * rows1, rows1)
            copy = remote(
                first_out.at[a, :, pl.ds(start, rows1), :],
                first_in[a].at[k],
                sends.at[1, a, k],
                recvs.at[1, a, k],
                device,
            )
            copy.start()
            copies.append(copy)
        first_copies.append(copies)
    pending += pair_copies

    def bias_start(stage, axis, value):
        slot = place.index[axis]
        buf = bias_bufs[stage]
        buf[slot] = value
        copies = []
        for k, device, _ in place.peers(axis):
            copy = remote(buf.at[slot], buf.at[slot], bias_send.at[stage, k], bias_recv.at[stage, k], device)
            copy.start()
            copies.append(copy)
        return copies

    def bias_finish(stage, axis, copies):
        buf = bias_bufs[stage]
        for copy in copies:
            copy.wait_recv()
        pending.extend(copies)
        total = buf[0]
        for k in range(1, place.count[axis]):
            total = total + buf[k]
        return total

    bias = lax.dot_general(
        jnp.ones((8, COLS), F32),
        bias_total,
        (((1,), (1,)), ((), ())),
        precision=lax.Precision.HIGHEST,
        preferred_element_type=F32,
    )
    bias_copies = bias_start(0, "core", bias)
    hidden_next[...] = wide[pl.ds(0, hid * ROWS), :].reshape(hid, ROWS, COLS).astype(BF16)

    gate_lanes = lane_ids((GATES, COLS))
    east = jnp.zeros((GATES, COLS), F32)
    west = jnp.zeros((GATES, COLS), F32)
    for r in range(ROWS):
        value = low_rows[r].astype(F32)
        before = jnp.where(gate_lanes == 0, 0.0, pltpu.roll(value, 1, 1))
        after = jnp.where(gate_lanes == COLS - 1, 0.0, pltpu.roll(value, COLS - 1, 1))
        low_windows[r + 1, 0:GATES] = before.astype(BF16)
        low_windows[r + 1, GATES : 2 * GATES] = low_rows[r]
        low_windows[r + 1, 2 * GATES : 3 * GATES] = after.astype(BF16)
        east = collect(east, value, r + 1, r + 2, gate_lanes)
        west = collect(west, value, r + 1, r + 1, gate_lanes)
    for slot, (value, last) in enumerate(((east, 2), (west, 0))):
        shifts = jnp.concatenate([pltpu.roll(value, a % LANES, 1).astype(BF16) for a in (-1, 0, 1)], axis=0)
        taps = jnp.concatenate([turned[3 * a + last] for a in range(3)], axis=1)
        low_edges[slot] = to_edge(jnp.dot(taps, shifts, preferred_element_type=F32))
    low_copies = cols_out(place, low_edges, low_sides, col_send.at[2], col_recv.at[2])

    low_windows[0] = jnp.zeros((3 * GATES, COLS), BF16)
    low_windows[PADDED - 1] = jnp.zeros((3 * GATES, COLS), BF16)
    flipped = jnp.concatenate([turned[8 - q] for q in range(9)], axis=1)
    for pair in range(ROWS // 2):
        blocks = [low_windows[r : r + 3].reshape(9 * GATES, COLS) for r in (2 * pair, 2 * pair + 1)]
        both = jnp.dot(flipped, jnp.concatenate(blocks, axis=1), preferred_element_type=F32)
        for k in range(2):
            field[2 * pair + k] = both[:, k * COLS : (k + 1) * COLS]
    field[ROWS] = jnp.dot(flipped[:, 6 * GATES :], low_windows[1], preferred_element_type=F32)
    field[ROWS + 1] = jnp.dot(flipped[:, : 3 * GATES], low_windows[ROWS], preferred_element_type=F32)
    bias = bias_finish(0, "core", bias_copies)
    bias_copies = bias_start(1, "x", bias)

    second_copies = []

    def second_start(a):
        axis1, axis2, _ = ORDERS[a]
        n1, n2 = place.count[axis1], place.count[axis2]
        rows1 = HALF // n1
        rows2 = rows1 // n2
        for copy in reversed(first_copies[a]):
            copy.wait_recv()
        pending.extend(first_copies[a])
        start = pl.multiple_of(place.index[axis1] * rows1, rows1)
        total = owned[a, :, pl.ds(start, rows1), :]
        for k in range(n1 - 1):
            total = total + first_in[a][k].astype(F32)
        for p in range(n2):
            second_out[a][p] = total[:, p * rows2 : (p + 1) * rows2, :]
        copies = []
        for k, device, other in reversed(place.peers(axis2)):
            copy = remote(second_out[a].at[other], second_in[a].at[k], sends.at[2, a, k], recvs.at[2, a, k], device)
            copy.start()
            copies.append(copy)
        second_copies.append((a, copies))

    second_start(2)

    for copy in low_copies:
        copy.wait_recv()
    low_side, high_side = from_edge(low_sides[0]), from_edge(low_sides[1])

    def arrived(position):
        first = jnp.where(lanes == 0, pltpu.roll(low_side, (-position) % LANES, 1), 0.0)
        last = jnp.where(lanes == COLS - 1, pltpu.roll(high_side, (COLS - 1 - position) % LANES, 1), 0.0)
        return first + last

    rims[0] = (field[ROWS] + arrived(0)).astype(BF16)
    rims[1] = (field[ROWS + 1] + arrived(PADDED - 1)).astype(BF16)
    row_copies, row_waits = rows_out(place, rims.at[0], rims.at[1], low_halo, row_send.at[1], row_recv.at[1])
    pending += low_copies + row_copies
    second_start(0)
    second_start(1)
    for r in range(ROWS):
        field[r] = field[r] + arrived(r + 1)
    bias = bias_finish(1, "x", bias_copies)
    bias_copies = bias_start(2, "y", bias)

    third_copies = []
    for a, copies2 in second_copies:
        _, axis2, axis3 = ORDERS[a]
        for copy in reversed(copies2):
            copy.wait_recv()
        pending += copies2
        total = second_out[a][place.index[axis2]]
        for k in range(place.count[axis2] - 1):
            total = total + second_in[a][k]
        slot = place.index[axis3]
        third[a][slot] = total
        copies = []
        for k, device, _ in reversed(place.peers(axis3)):
            copy = remote(third[a].at[slot], third[a].at[slot], sends.at[3, a, k], recvs.at[3, a, k], device)
            copy.start()
            copies.append(copy)
        third_copies.append((a, copies))

    bias = bias_finish(2, "y", bias_copies)
    bias_copies = bias_start(3, "z", bias)

    fourth_copies = []
    for a, copies3 in third_copies:
        _, axis2, axis3 = ORDERS[a]
        for copy in reversed(copies3):
            copy.wait_recv()
        pending += copies3
        total = third[a][0]
        for k in range(1, place.count[axis3]):
            total = total + third[a][k]
        slot = place.index[axis2]
        gathered[a][slot] = (total * scaling).astype(BF16)
        copies = []
        for k, device, _ in reversed(place.peers(axis2)):
            copy = remote(gathered[a].at[slot], gathered[a].at[slot], sends.at[4, a, k], recvs.at[4, a, k], device)
            copy.start()
            copies.append(copy)
        fourth_copies.append((a, copies))

    def block_of(a, owner):
        rows1 = HALF // place.count[ORDERS[a][0]]
        start = pl.multiple_of(mine + owner * rows1, rows1)
        return kernel_low.at[pl.ds(3 * a, 3), pl.ds(start, rows1), :]

    last_copies = []

    def forward(a, owner, slot):
        block = block_of(a, owner)
        copy = remote(block, block, sends.at[6, a, slot], recvs.at[6, a, slot], partner)
        copy.start()
        last_copies.append(copy)

    fifth_copies = []
    for a, copies4 in sorted(fourth_copies, key=lambda entry: entry[0]):
        axis1, axis2, _ = ORDERS[a]
        n1 = place.count[axis1]
        for copy in reversed(copies4):
            copy.wait_recv()
        pending += copies4
        block = block_of(a, place.index[axis1])
        block[...] = jnp.concatenate(
            [gathered[a][p].astype(F32) for p in range(place.count[axis2])], axis=1
        ).astype(BF16)
        copies = []
        for k, device, _ in reversed(place.peers(axis1)):
            copy = remote(block, block, sends.at[5, a, k], recvs.at[5, a, k], device)
            copy.start()
            copies.append((copy, k, lax.rem(place.index[axis1] + n1 - 1 - k, n1)))
        forward(a, place.index[axis1], n1 - 1)
        fifth_copies.append((a, copies))

    bias_sum[...] = bias_finish(3, "z", bias_copies) * scaling
    for slot, r in ((0, 0), (1, ROWS - 1)):
        row_waits[slot].wait_recv()
        field[r] = field[r] + low_halo[slot].astype(F32)
    for r in range(ROWS):
        wide[pl.ds(r, STATE, stride=ROWS), :] = field[r]
    grad_inputs[...] = wide[pl.ds(0, width * ROWS), :].reshape(width, ROWS, COLS).astype(BF16)
    grad_hidden[...] = wide[pl.ds(width * ROWS, hid * ROWS), :].reshape(hid, ROWS, COLS).astype(BF16)

    for a, copies5 in fifth_copies[2:] + fifth_copies[:2]:
        for copy, k, sender in reversed(copies5):
            copy.wait_recv()
            forward(a, sender, k)
            pending.append(copy)
    for copy in last_copies:
        copy.wait_recv()
    pending += last_copies
    for copy in pending:
        copy.wait_send()


def finish_kernel(
    hidden_next,
    cell_next,
    grad_inputs,
    grad_hidden,
    grad_cell,
    kernel_low,
    bias_sum,
    hidden_next_out,
    cell_next_out,
    grad_inputs_out,
    grad_hidden_out,
    grad_cell_out,
    kernel_out,
    bias_out,
    kernel_wide,
    sems,
):
    pairs = (
        (hidden_next, hidden_next_out),
        (cell_next, cell_next_out),
        (grad_inputs, grad_inputs_out),
        (grad_hidden, grad_hidden_out),
        (grad_cell, grad_cell_out),
        (bias_sum.at[0:1], bias_out),
    )
    copies = [pltpu.make_async_copy(source, target, sems.at[i]) for i, (source, target) in enumerate(pairs)]
    for copy in copies:
        copy.start()
    for a in range(3):
        taps = pl.ds(3 * a, 3)
        kernel_wide[taps] = kernel_low[taps].astype(F32)
        copy = pltpu.make_async_copy(kernel_wide.at[taps], kernel_out.at[taps], sems.at[len(pairs) + a])
        copy.start()
        copies.append(copy)
    for copy in copies:
        copy.wait()


def shape_of(shape, dtype):
    return jax.ShapeDtypeStruct(shape, dtype)


def body(
    sizes,
    inputs_below,
    hidden_prev,
    cell_prev,
    kernel_weights,
    gate_bias,
    readout,
    target_field,
    land_mask,
    fire_mask,
    hidden_grad,
):
    nx, ny, zh, zl = sizes
    count = {"x": nx, "y": ny, "z": zh * zl}
    hid = hidden_prev.shape[0]
    dma = pltpu.SemaphoreType.DMA
    scaling = 1.0 / math.sqrt(ROWS * nx * zh * 2 * COLS * ny * zl)
    most = max(nx, ny, zh * zl)
    chunk = []
    for axis1, axis2, axis3 in ORDERS:
        rows1 = HALF // count[axis1]
        chunk.append((count[axis1], rows1, count[axis2], rows1 // count[axis2], count[axis3]))
    cells = shape_of((hid, ROWS, COLS), BF16)
    wide_cells = shape_of((hid * ROWS, COLS), F32)
    inputs = (
        inputs_below,
        hidden_prev,
        cell_prev.reshape(hid * ROWS, COLS),
        kernel_weights,
        gate_bias.reshape(1, GATES),
        readout.reshape(1, hid),
        target_field,
        land_mask,
        fire_mask,
        hidden_grad,
    )
    results = pl.pallas_call(
        functools.partial(step_kernel, sizes, scaling),
        out_shape=[
            cells,
            wide_cells,
            cells,
            cells,
            wide_cells,
            shape_of((9, GATES, STATE), BF16),
            shape_of((8, GATES), F32),
        ],
        in_specs=[pl.BlockSpec(memory_space=pltpu.HBM)] * len(inputs),
        out_specs=[VMEM_SPEC] * 7,
        scratch_shapes=[pltpu.VMEM(value.shape, value.dtype) for value in inputs]
        + [
            pltpu.VMEM((STATE * ROWS, COLS), F32),
            pltpu.VMEM((hid * ROWS, COLS), F32),
            pltpu.VMEM((PADDED, STATE, COLS), BF16),
            pltpu.VMEM((2, STATE, COLS), BF16),
            pltpu.VMEM((2, EDGE, STATE), BF16),
            pltpu.VMEM((2, EDGE, STATE), BF16),
            pltpu.VMEM((2, EDGE, STATE), BF16),
            pltpu.VMEM((2, EDGE, STATE), BF16),
            pltpu.VMEM((PADDED, 3 * STATE, COLS), BF16),
            pltpu.VMEM((3, GATES, 3 * STATE), F32),
            pltpu.VMEM((9, STATE, GATES), BF16),
            pltpu.VMEM((ROWS, GATES, COLS), BF16),
            pltpu.VMEM((PADDED, STATE, COLS), F32),
            pltpu.VMEM((2, STATE, COLS), BF16),
            pltpu.VMEM((2, STATE, COLS), BF16),
            pltpu.VMEM((2, EDGE, STATE), BF16),
            pltpu.VMEM((2, EDGE, STATE), BF16),
            pltpu.VMEM((PADDED, 3 * GATES, COLS), BF16),
            pltpu.VMEM((3, 3, HALF, STATE), BF16),
            pltpu.VMEM((3, 3, HALF, STATE), BF16),
            pltpu.VMEM((3, 3, HALF, STATE), F32),
            pltpu.VMEM((3, 3, HALF, STATE), BF16),
            [pltpu.VMEM((n1 - 1, 3, r1, STATE), BF16) for n1, r1, _, _, _ in chunk],
            [pltpu.VMEM((n2, 3, r2, STATE), F32) for _, _, n2, r2, _ in chunk],
            [pltpu.VMEM((n2 - 1, 3, r2, STATE), F32) for _, _, n2, r2, _ in chunk],
            [pltpu.VMEM((n3, 3, r2, STATE), F32) for _, _, _, r2, n3 in chunk],
            [pltpu.VMEM((n2, 3, r2, STATE), BF16) for _, _, n2, r2, _ in chunk],
            [pltpu.VMEM((n, 8, GATES), F32) for n in (2, nx, ny, zh * zl)],
            dma((len(inputs),)),
            dma((2, 2)),
            dma((2, 2)),
            dma((3, 2)),
            dma((3, 2)),
            dma((7, 3, most)),
            dma((7, 3, most)),
            dma((4, most)),
            dma((4, most)),
        ],
        compiler_params=pltpu.CompilerParams(
            collective_id=0, has_side_effects=True, vmem_limit_bytes=VMEM_LIMIT
        ),
        name="whole_step",
    )(*[pltpu.with_memory_space_constraint(value, pltpu.HBM) for value in inputs])

    hidden_next, cell_next, grad_inputs, grad_hidden, grad_cell, grad_kernel, grad_bias = pl.pallas_call(
        finish_kernel,
        out_shape=[
            cells,
            wide_cells,
            cells,
            cells,
            wide_cells,
            shape_of((9, GATES, STATE), F32),
            shape_of((1, GATES), F32),
        ],
        in_specs=[VMEM_SPEC] * 7,
        out_specs=[pl.BlockSpec(memory_space=pltpu.HBM)] * 7,
        scratch_shapes=[pltpu.VMEM((9, GATES, STATE), F32), dma((9,))],
        compiler_params=pltpu.CompilerParams(vmem_limit_bytes=VMEM_LIMIT),
        name="results",
    )(*results)
    shape = (hid, ROWS, COLS)
    return (
        hidden_next,
        cell_next.reshape(shape),
        grad_inputs,
        grad_hidden,
        grad_cell.reshape(shape),
        grad_kernel,
        grad_bias.reshape(GATES),
    )


def solution(mesh):
    lat, lon = mesh.shape["lat"], mesh.shape["lon"]
    sizes = {(16, 32): (4, 8, 2, 4), (4, 4): (2, 2, 1, 2)}[(lat, lon)]
    cells = P(None, "lat", "lon")
    flat = P("lat", "lon")
    return jax.shard_map(
        functools.partial(body, sizes),
        mesh=mesh,
        in_specs=(cells, cells, cells, P(), P(), P(), flat, flat, flat, cells),
        out_specs=(cells, cells, cells, cells, cells, P(), P()),
        check_vma=False,
    )
```

```python
import functools
import math

import jax
import jax.numpy as jnp
from jax import lax
from jax.experimental import pallas as pl
from jax.experimental.pallas import tpu as pltpu
from jax.sharding import PartitionSpec as P

MESH = pl.DeviceIdType.MESH
F32 = jnp.float32
BF16 = jnp.bfloat16
ROWS = 8
COLS = 128
PADDED = ROWS + 2
STATE = 128
GATES = 256
HALF = GATES // 2
LANES = 128
EDGE = 16
VMEM_SPEC = pl.BlockSpec(memory_space=pltpu.VMEM)
VMEM_LIMIT = 48 * 1024 * 1024


class Place:
    def __init__(self, sizes):
        self.nx, self.ny, self.zh, self.zl = sizes
        self.nz = self.zh * self.zl
        self.nlat = self.nx * self.zh * 2
        self.nlon = self.ny * self.zl
        self.lat = lax.axis_index("lat")
        self.lon = lax.axis_index("lon")
        self.core = lax.rem(self.lat, 2)
        chip = self.lat // 2
        self.z_hi = lax.rem(chip, self.zh)
        self.x = chip // self.zh
        self.z_lo = lax.rem(self.lon, self.zl)
        self.y = self.lon // self.zl
        self.z = self.z_hi * self.zl + self.z_lo
        self.count = {"core": 2, "x": self.nx, "y": self.ny, "z": self.nz}
        self.index = {"core": self.core, "x": self.x, "y": self.y, "z": self.z}
        self.north = self.lat == 0
        self.south = self.lat == self.nlat - 1

    def at(self, x, y, z, core):
        lat = (x * self.zh + z // self.zl) * 2 + core
        lon = y * self.zl + lax.rem(z, self.zl)
        return (lat, lon)

    def peer(self, axis, steps):
        other = lax.rem(self.index[axis] + steps, self.count[axis])
        where = dict(self.index)
        where[axis] = other
        return self.at(where["x"], where["y"], where["z"], where["core"]), other

    def peers(self, axis):
        count = self.count[axis]
        order = sorted(range(1, count), key=lambda steps: min(steps, count - steps))
        return [(steps - 1, *self.peer(axis, steps)) for steps in order]

    def up(self):
        opposite = lax.rem(self.lon + self.nlon // 2, self.nlon)
        lat = jnp.where(self.north, 0, self.lat - 1)
        return (lat, jnp.where(self.north, opposite, self.lon))

    def down(self):
        opposite = lax.rem(self.lon + self.nlon // 2, self.nlon)
        lat = jnp.where(self.south, self.nlat - 1, self.lat + 1)
        return (lat, jnp.where(self.south, opposite, self.lon))

    def east(self):
        return (self.lat, lax.rem(self.lon + 1, self.nlon))

    def west(self):
        return (self.lat, lax.rem(self.lon + self.nlon - 1, self.nlon))

    def around(self):
        return [self.up(), self.down(), self.east(), self.west()]


def greet(devices):
    barrier = pltpu.get_barrier_semaphore()
    for device in devices:
        pl.semaphore_signal(barrier, inc=1, device_id=device, device_id_type=MESH)
    return barrier


def remote(source, target, send_sem, recv_sem, device):
    return pltpu.make_async_remote_copy(
        src_ref=source,
        dst_ref=target,
        send_sem=send_sem,
        recv_sem=recv_sem,
        device_id=device,
        device_id_type=MESH,
    )


def lane_ids(shape):
    return lax.broadcasted_iota(jnp.int32, shape, len(shape) - 1)


def rows_out(place, first, last, halo, send_sem, recv_sem):
    upper_slot = jnp.where(place.north, 0, 1)
    lower_slot = jnp.where(place.south, 1, 0)
    copies = [
        remote(first, halo.at[upper_slot], send_sem.at[0], recv_sem.at[upper_slot], place.up()),
        remote(last, halo.at[lower_slot], send_sem.at[1], recv_sem.at[lower_slot], place.down()),
    ]
    for copy in copies:
        copy.start()
    waits = [
        remote(first, halo.at[0], send_sem.at[0], recv_sem.at[0], place.up()),
        remote(last, halo.at[1], send_sem.at[1], recv_sem.at[1], place.down()),
    ]
    return copies, waits


def to_edge(total):
    return jnp.transpose(total)[0:EDGE].astype(BF16)


def from_edge(edge):
    rest = jnp.zeros((LANES - EDGE, edge.shape[1]), F32)
    return jnp.transpose(jnp.concatenate([edge.astype(F32), rest], axis=0))


def collect(total, row, position, shift, lanes):
    return jnp.where(lanes == position, pltpu.roll(row, shift % LANES, 1), total)


def cols_out(place, edges, sides, send_sem, recv_sem):
    copies = [
        remote(edges.at[0], sides.at[0], send_sem.at[0], recv_sem.at[0], place.east()),
        remote(edges.at[1], sides.at[1], send_sem.at[1], recv_sem.at[1], place.west()),
    ]
    for copy in copies:
        copy.start()
    return copies


def spread(values, sides_low, sides_high, lanes, position):
    before = jnp.where(lanes == 0, pltpu.roll(sides_low, (-position) % LANES, 1), pltpu.roll(values, 1, 1))
    after = jnp.where(
        lanes == COLS - 1, pltpu.roll(sides_high, (COLS - 1 - position) % LANES, 1), pltpu.roll(values, COLS - 1, 1)
    )
    return before, after


ORDERS = (("y", "x", "z"), ("z", "x", "y"), ("x", "y", "z"))
EARLY = ((1, 2), (3, 4), (5, 6))
LATE = (0, 7)


def step_kernel(
    sizes,
    scaling,
    below_hbm,
    hidden_hbm,
    cell_hbm,
    weights_hbm,
    gate_bias_hbm,
    readout_hbm,
    target_hbm,
    land_hbm,
    fire_hbm,
    hidden_grad_hbm,
    hidden_next,
    cell_next,
    grad_inputs,
    grad_hidden,
    grad_cell,
    kernel_low,
    bias_sum,
    below,
    hidden,
    cell_prev,
    weights,
    gate_bias,
    readout,
    target,
    land,
    fire,
    hidden_grad,
    wide,
    wide_grad,
    rows,
    halo,
    edges,
    sides,
    corner_edges,
    corners,
    windows,
    kernel_acc,
    turned,
    low_rows,
    field,
    rims,
    low_halo,
    low_edges,
    low_sides,
    low_windows,
    pair_out,
    pair_in,
    owned,
    first_out,
    first_in,
    second_out,
    second_in,
    third,
    gathered,
    bias_bufs,
    load_sem,
    row_send,
    row_recv,
    col_send,
    col_recv,
    sends,
    recvs,
    bias_send,
    bias_recv,
):
    place = Place(sizes)
    hid = hidden_next.shape[0]
    width = grad_inputs.shape[0]
    partner, _ = place.peer("core", 1)
    devices = place.around()
    for axis in ("z", "y", "x"):
        devices += [device for _, device, _ in reversed(place.peers(axis))]
    devices.append(partner)
    barrier = greet(devices)
    mine = pl.multiple_of(place.core * HALF, HALF)
    theirs = pl.multiple_of((1 - place.core) * HALF, HALF)
    pending = []

    sources = (below_hbm, hidden_hbm, weights_hbm, cell_hbm, hidden_grad_hbm, gate_bias_hbm, readout_hbm,
               target_hbm, land_hbm, fire_hbm)
    targets = (below, hidden, weights, cell_prev, hidden_grad, gate_bias, readout, target, land, fire)
    loads = [
        pltpu.make_async_copy(source, destination, load_sem.at[i])
        for i, (source, destination) in enumerate(zip(sources, targets))
    ]
    for load in loads:
        load.start()

    loads[0].wait()
    wide[pl.ds(0, width * ROWS), :] = below[...].astype(F32).reshape(width * ROWS, COLS)
    loads[1].wait()
    wide[pl.ds(width * ROWS, hid * ROWS), :] = hidden[...].astype(F32).reshape(hid * ROWS, COLS)

    def state_row(r):
        return wide[pl.ds(r, STATE, stride=ROWS), :]

    for r in (0, ROWS - 1):
        rows[r + 1] = state_row(r).astype(BF16)
    pl.semaphore_wait(barrier, len(devices))
    row_copies, row_waits = rows_out(place, rows.at[1], rows.at[ROWS], halo, row_send.at[0], row_recv.at[0])

    lanes = lane_ids((STATE, COLS))
    east = jnp.zeros((STATE, COLS), F32)
    west = jnp.zeros((STATE, COLS), F32)
    for r in range(ROWS):
        value = state_row(r)
        if 0 < r < ROWS - 1:
            rows[r + 1] = value.astype(BF16)
        east = collect(east, value, r + 1, r + 2, lanes)
        west = collect(west, value, r + 1, r + 1, lanes)
    edges[0] = to_edge(east)
    edges[1] = to_edge(west)
    col_copies = cols_out(place, edges, sides, col_send.at[0], col_recv.at[0])

    for load in loads[2:]:
        load.wait()
    wide_grad[...] = hidden_grad[...].astype(F32).reshape(hid * ROWS, COLS)
    bias_cols = jnp.transpose(jnp.broadcast_to(gate_bias[...], (LANES, GATES)))
    read_cols = jnp.transpose(jnp.broadcast_to(readout[...], (LANES, hid)))
    for t in range(9):
        turned[t] = jnp.transpose(weights[t].astype(F32)).astype(BF16)

    corner_east = jnp.zeros((STATE, COLS), F32)
    corner_west = jnp.zeros((STATE, COLS), F32)
    for slot, position in ((0, 0), (1, PADDED - 1)):
        row_waits[slot].wait_recv()
        value = halo[slot].astype(F32)
        corner_east = collect(corner_east, value, position, position + 1, lanes)
        corner_west = collect(corner_west, value, position, position, lanes)
    corner_edges[0] = to_edge(corner_east)
    corner_edges[1] = to_edge(corner_west)
    corner_copies = cols_out(place, corner_edges, corners, col_send.at[1], col_recv.at[1])
    pending += row_copies + col_copies + corner_copies

    def open_windows(position, low, low_side, high_side):
        value = low.astype(F32)
        before, after = spread(value, low_side, high_side, lanes, position)
        windows[position, 0:STATE] = before.astype(BF16)
        windows[position, STATE : 2 * STATE] = low
        windows[position, 2 * STATE : 3 * STATE] = after.astype(BF16)

    for copy in col_copies:
        copy.wait_recv()
    low_side, high_side = from_edge(sides[0]), from_edge(sides[1])
    for position in range(1, PADDED - 1):
        open_windows(position, rows[position], low_side, high_side)

    flat = jnp.concatenate([weights[t] for t in range(9)], axis=1)

    def cells_of(pair, bias_total):
        columns = jnp.concatenate([windows[r : r + 3].reshape(9 * STATE, COLS) for r in pair], axis=1)
        both = jnp.dot(flat, columns, preferred_element_type=F32)
        for k, r in enumerate(pair):
            preact = both[:, k * COLS : (k + 1) * COLS] + bias_cols
            input_gate = jax.nn.sigmoid(preact[0:hid])
            forget_gate = jax.nn.sigmoid(preact[hid : 2 * hid])
            output_gate = jax.nn.sigmoid(preact[2 * hid : 3 * hid])
            candidate = jnp.tanh(preact[3 * hid : 4 * hid])
            land_row = land[r : r + 1, :].astype(F32)
            fire_row = fire[r : r + 1, :].astype(F32)
            prev = cell_prev[pl.ds(r, hid, stride=ROWS), :]
            cell = land_row * (forget_gate * prev + input_gate * candidate)
            squashed = jnp.tanh(cell)
            new_hidden = (output_gate * squashed).astype(BF16).astype(F32)
            predicted = jnp.sum(read_cols * new_hidden, axis=0, keepdims=True)
            miss = 2.0 * (fire_row * (predicted - target[r : r + 1, :]))
            total_grad = wide_grad[pl.ds(r, hid, stride=ROWS), :] + miss * read_cols
            cell_grad = land_row * total_grad * output_gate * (1.0 - squashed * squashed)
            pre_grad = jnp.concatenate(
                [
                    cell_grad * candidate * input_gate * (1.0 - input_gate),
                    cell_grad * prev * forget_gate * (1.0 - forget_gate),
                    total_grad * squashed * output_gate * (1.0 - output_gate),
                    cell_grad * input_gate * (1.0 - candidate * candidate),
                ],
                axis=0,
            )
            cell_next[pl.ds(r, hid, stride=ROWS), :] = cell
            grad_cell[pl.ds(r, hid, stride=ROWS), :] = cell_grad * forget_gate
            wide[pl.ds(r, hid, stride=ROWS), :] = new_hidden
            bias_total = bias_total + pre_grad
            low_rows[r] = pre_grad.astype(BF16)
        return bias_total

    def kernel_terms(gates, rows_in, a):
        cells = jnp.concatenate([low_rows[r, gates, :] for r in rows_in], axis=1)
        seen = jnp.concatenate([windows[r + a] for r in rows_in], axis=1)
        return lax.dot_general(cells, seen, (((1,), (1,)), ((), ())), preferred_element_type=F32)

    bias_total = jnp.zeros((GATES, COLS), F32)
    for pair in EARLY:
        bias_total = cells_of(pair, bias_total)
    for a in range(3):
        kernel_acc[a] = kernel_terms(slice(None), range(1, ROWS - 1), a)

    for copy in corner_copies:
        copy.wait_recv()
    low_side, high_side = from_edge(corners[0]), from_edge(corners[1])
    open_windows(0, halo[0], low_side, high_side)
    open_windows(PADDED - 1, halo[1], low_side, high_side)
    bias_total = cells_of(LATE, bias_total)

    pair_copies = []
    for a in range(3):
        part = kernel_acc[a, pl.ds(theirs, HALF), :] + kernel_terms(pl.ds(theirs, HALF), LATE, a)
        for b in range(3):
            pair_out[a, b] = part[:, b * STATE : (b + 1) * STATE].astype(BF16)
        copy = remote(pair_out.at[a], pair_in.at[a], sends.at[0, a, 0], recvs.at[0, a, 0], partner)
        copy.start()
        pair_copies.append(copy)
    for a in range(3):
        part = kernel_acc[a, pl.ds(mine, HALF), :] + kernel_terms(pl.ds(mine, HALF), LATE, a)
        for b in range(3):
            owned[a, b] = part[:, b * STATE : (b + 1) * STATE]

    first_copies = []
    for a in range(3):
        pair_copies[a].wait_recv()
        total = owned[a] + pair_in[a].astype(F32)
        owned[a] = total
        first_out[a] = total.astype(BF16)
        axis = ORDERS[a][0]
        rows1 = HALF // place.count[axis]
        copies = []
        for k, device, other in reversed(place.peers(axis)):
            start = pl.multiple_of(other * rows1, rows1)
            copy = remote(
                first_out.at[a, :, pl.ds(start, rows1), :],
                first_in[a].at[k],
                sends.at[1, a, k],
                recvs.at[1, a, k],
                device,
            )
            copy.start()
            copies.append(copy)
        first_copies.append(copies)
    pending += pair_copies

    def bias_start(stage, axis, value):
        slot = place.index[axis]
        buf = bias_bufs[stage]
        buf[slot] = value
        copies = []
        for k, device, _ in place.peers(axis):
            copy = remote(buf.at[slot], buf.at[slot], bias_send.at[stage, k], bias_recv.at[stage, k], device)
            copy.start()
            copies.append(copy)
        return copies

    def bias_finish(stage, axis, copies):
        buf = bias_bufs[stage]
        for copy in copies:
            copy.wait_recv()
        pending.extend(copies)
        total = buf[0]
        for k in range(1, place.count[axis]):
            total = total + buf[k]
        return total

    bias = lax.dot_general(
        jnp.ones((8, COLS), F32),
        bias_total,
        (((1,), (1,)), ((), ())),
        precision=lax.Precision.HIGHEST,
        preferred_element_type=F32,
    )
    bias_copies = bias_start(0, "core", bias)
    hidden_next[...] = wide[pl.ds(0, hid * ROWS), :].reshape(hid, ROWS, COLS).astype(BF16)

    gate_lanes = lane_ids((GATES, COLS))
    east = jnp.zeros((GATES, COLS), F32)
    west = jnp.zeros((GATES, COLS), F32)
    for r in range(ROWS):
        value = low_rows[r].astype(F32)
        before = jnp.where(gate_lanes == 0, 0.0, pltpu.roll(value, 1, 1))
        after = jnp.where(gate_lanes == COLS - 1, 0.0, pltpu.roll(value, COLS - 1, 1))
        low_windows[r + 1, 0:GATES] = before.astype(BF16)
        low_windows[r + 1, GATES : 2 * GATES] = low_rows[r]
        low_windows[r + 1, 2 * GATES : 3 * GATES] = after.astype(BF16)
        east = collect(east, value, r + 1, r + 2, gate_lanes)
        west = collect(west, value, r + 1, r + 1, gate_lanes)
    for slot, (value, last) in enumerate(((east, 2), (west, 0))):
        shifts = jnp.concatenate([pltpu.roll(value, a % LANES, 1).astype(BF16) for a in (-1, 0, 1)], axis=0)
        taps = jnp.concatenate([turned[3 * a + last] for a in range(3)], axis=1)
        low_edges[slot] = to_edge(jnp.dot(taps, shifts, preferred_element_type=F32))
    low_copies = cols_out(place, low_edges, low_sides, col_send.at[2], col_recv.at[2])

    low_windows[0] = jnp.zeros((3 * GATES, COLS), BF16)
    low_windows[PADDED - 1] = jnp.zeros((3 * GATES, COLS), BF16)
    flipped = jnp.concatenate([turned[8 - q] for q in range(9)], axis=1)
    for pair in range(ROWS // 2):
        blocks = [low_windows[r : r + 3].reshape(9 * GATES, COLS) for r in (2 * pair, 2 * pair + 1)]
        both = jnp.dot(flipped, jnp.concatenate(blocks, axis=1), preferred_element_type=F32)
        for k in range(2):
            field[2 * pair + k] = both[:, k * COLS : (k + 1) * COLS]
    field[ROWS] = jnp.dot(flipped[:, 6 * GATES :], low_windows[1], preferred_element_type=F32)
    field[ROWS + 1] = jnp.dot(flipped[:, : 3 * GATES], low_windows[ROWS], preferred_element_type=F32)
    bias = bias_finish(0, "core", bias_copies)
    bias_copies = bias_start(1, "x", bias)

    second_copies = []

    def second_start(a):
        axis1, axis2, _ = ORDERS[a]
        n1, n2 = place.count[axis1], place.count[axis2]
        rows1 = HALF // n1
        rows2 = rows1 // n2
        for copy in reversed(first_copies[a]):
            copy.wait_recv()
        pending.extend(first_copies[a])
        start = pl.multiple_of(place.index[axis1] * rows1, rows1)
        total = owned[a, :, pl.ds(start, rows1), :]
        for k in range(n1 - 1):
            total = total + first_in[a][k].astype(F32)
        for p in range(n2):
            second_out[a][p] = total[:, p * rows2 : (p + 1) * rows2, :]
        copies = []
        for k, device, other in reversed(place.peers(axis2)):
            copy = remote(second_out[a].at[other], second_in[a].at[k], sends.at[2, a, k], recvs.at[2, a, k], device)
            copy.start()
            copies.append(copy)
        second_copies.append((a, copies))

    second_start(2)
    second_start(0)
    second_start(1)

    for copy in low_copies:
        copy.wait_recv()
    low_side, high_side = from_edge(low_sides[0]), from_edge(low_sides[1])

    def arrived(position):
        first = jnp.where(lanes == 0, pltpu.roll(low_side, (-position) % LANES, 1), 0.0)
        last = jnp.where(lanes == COLS - 1, pltpu.roll(high_side, (COLS - 1 - position) % LANES, 1), 0.0)
        return first + last

    rims[0] = (field[ROWS] + arrived(0)).astype(BF16)
    rims[1] = (field[ROWS + 1] + arrived(PADDED - 1)).astype(BF16)
    row_copies, row_waits = rows_out(place, rims.at[0], rims.at[1], low_halo, row_send.at[1], row_recv.at[1])
    pending += low_copies + row_copies
    for r in range(ROWS):
        field[r] = field[r] + arrived(r + 1)
    bias = bias_finish(1, "x", bias_copies)
    bias_copies = bias_start(2, "y", bias)

    third_copies = []
    for a, copies2 in second_copies:
        _, axis2, axis3 = ORDERS[a]
        for copy in reversed(copies2):
            copy.wait_recv()
        pending += copies2
        total = second_out[a][place.index[axis2]]
        for k in range(place.count[axis2] - 1):
            total = total + second_in[a][k]
        slot = place.index[axis3]
        third[a][slot] = total
        copies = []
        for k, device, _ in reversed(place.peers(axis3)):
            copy = remote(third[a].at[slot], third[a].at[slot], sends.at[3, a, k], recvs.at[3, a, k], device)
            copy.start()
            copies.append(copy)
        third_copies.append((a, copies))

    bias = bias_finish(2, "y", bias_copies)
    bias_copies = bias_start(3, "z", bias)

    fourth_copies = []
    for a, copies3 in third_copies:
        _, axis2, axis3 = ORDERS[a]
        for copy in reversed(copies3):
            copy.wait_recv()
        pending += copies3
        total = third[a][0]
        for k in range(1, place.count[axis3]):
            total = total + third[a][k]
        slot = place.index[axis2]
        gathered[a][slot] = (total * scaling).astype(BF16)
        copies = []
        for k, device, _ in reversed(place.peers(axis2)):
            copy = remote(gathered[a].at[slot], gathered[a].at[slot], sends.at[4, a, k], recvs.at[4, a, k], device)
            copy.start()
            copies.append(copy)
        fourth_copies.append((a, copies))

    def block_of(a, owner):
        rows1 = HALF // place.count[ORDERS[a][0]]
        start = pl.multiple_of(mine + owner * rows1, rows1)
        return kernel_low.at[pl.ds(3 * a, 3), pl.ds(start, rows1), :]

    last_copies = []

    def forward(a, owner, slot):
        block = block_of(a, owner)
        copy = remote(block, block, sends.at[6, a, slot], recvs.at[6, a, slot], partner)
        copy.start()
        last_copies.append(copy)

    fifth_copies = []
    for a, copies4 in sorted(fourth_copies, key=lambda entry: entry[0]):
        axis1, axis2, _ = ORDERS[a]
        n1 = place.count[axis1]
        for copy in reversed(copies4):
            copy.wait_recv()
        pending += copies4
        block = block_of(a, place.index[axis1])
        block[...] = jnp.concatenate(
            [gathered[a][p].astype(F32) for p in range(place.count[axis2])], axis=1
        ).astype(BF16)
        copies = []
        for k, device, _ in reversed(place.peers(axis1)):
            copy = remote(block, block, sends.at[5, a, k], recvs.at[5, a, k], device)
            copy.start()
            copies.append((copy, k, lax.rem(place.index[axis1] + n1 - 1 - k, n1)))
        forward(a, place.index[axis1], n1 - 1)
        fifth_copies.append((a, copies))

    bias_sum[...] = bias_finish(3, "z", bias_copies) * scaling
    for slot, r in ((0, 0), (1, ROWS - 1)):
        row_waits[slot].wait_recv()
        field[r] = field[r] + low_halo[slot].astype(F32)
    for r in range(ROWS):
        wide[pl.ds(r, STATE, stride=ROWS), :] = field[r]
    grad_inputs[...] = wide[pl.ds(0, width * ROWS), :].reshape(width, ROWS, COLS).astype(BF16)
    grad_hidden[...] = wide[pl.ds(width * ROWS, hid * ROWS), :].reshape(hid, ROWS, COLS).astype(BF16)

    for a, copies5 in fifth_copies[2:] + fifth_copies[:2]:
        for copy, k, sender in reversed(copies5):
            copy.wait_recv()
            forward(a, sender, k)
            pending.append(copy)
    for copy in last_copies:
        copy.wait_recv()
    pending += last_copies
    for copy in pending:
        copy.wait_send()


def finish_kernel(
    hidden_next,
    cell_next,
    grad_inputs,
    grad_hidden,
    grad_cell,
    kernel_low,
    bias_sum,
    hidden_next_out,
    cell_next_out,
    grad_inputs_out,
    grad_hidden_out,
    grad_cell_out,
    kernel_out,
    bias_out,
    kernel_wide,
    sems,
):
    pairs = (
        (hidden_next, hidden_next_out),
        (cell_next, cell_next_out),
        (grad_inputs, grad_inputs_out),
        (grad_hidden, grad_hidden_out),
        (grad_cell, grad_cell_out),
        (bias_sum.at[0:1], bias_out),
    )
    copies = [pltpu.make_async_copy(source, target, sems.at[i]) for i, (source, target) in enumerate(pairs)]
    for copy in copies:
        copy.start()
    for a in range(3):
        taps = pl.ds(3 * a, 3)
        kernel_wide[taps] = kernel_low[taps].astype(F32)
        copy = pltpu.make_async_copy(kernel_wide.at[taps], kernel_out.at[taps], sems.at[len(pairs) + a])
        copy.start()
        copies.append(copy)
    for copy in copies:
        copy.wait()


def shape_of(shape, dtype):
    return jax.ShapeDtypeStruct(shape, dtype)


def body(
    sizes,
    inputs_below,
    hidden_prev,
    cell_prev,
    kernel_weights,
    gate_bias,
    readout,
    target_field,
    land_mask,
    fire_mask,
    hidden_grad,
):
    nx, ny, zh, zl = sizes
    count = {"x": nx, "y": ny, "z": zh * zl}
    hid = hidden_prev.shape[0]
    dma = pltpu.SemaphoreType.DMA
    scaling = 1.0 / math.sqrt(ROWS * nx * zh * 2 * COLS * ny * zl)
    most = max(nx, ny, zh * zl)
    chunk = []
    for axis1, axis2, axis3 in ORDERS:
        rows1 = HALF // count[axis1]
        chunk.append((count[axis1], rows1, count[axis2], rows1 // count[axis2], count[axis3]))
    cells = shape_of((hid, ROWS, COLS), BF16)
    wide_cells = shape_of((hid * ROWS, COLS), F32)
    inputs = (
        inputs_below,
        hidden_prev,
        cell_prev.reshape(hid * ROWS, COLS),
        kernel_weights,
        gate_bias.reshape(1, GATES),
        readout.reshape(1, hid),
        target_field,
        land_mask,
        fire_mask,
        hidden_grad,
    )
    results = pl.pallas_call(
        functools.partial(step_kernel, sizes, scaling),
        out_shape=[
            cells,
            wide_cells,
            cells,
            cells,
            wide_cells,
            shape_of((9, GATES, STATE), BF16),
            shape_of((8, GATES), F32),
        ],
        in_specs=[pl.BlockSpec(memory_space=pltpu.HBM)] * len(inputs),
        out_specs=[VMEM_SPEC] * 7,
        scratch_shapes=[pltpu.VMEM(value.shape, value.dtype) for value in inputs]
        + [
            pltpu.VMEM((STATE * ROWS, COLS), F32),
            pltpu.VMEM((hid * ROWS, COLS), F32),
            pltpu.VMEM((PADDED, STATE, COLS), BF16),
            pltpu.VMEM((2, STATE, COLS), BF16),
            pltpu.VMEM((2, EDGE, STATE), BF16),
            pltpu.VMEM((2, EDGE, STATE), BF16),
            pltpu.VMEM((2, EDGE, STATE), BF16),
            pltpu.VMEM((2, EDGE, STATE), BF16),
            pltpu.VMEM((PADDED, 3 * STATE, COLS), BF16),
            pltpu.VMEM((3, GATES, 3 * STATE), F32),
            pltpu.VMEM((9, STATE, GATES), BF16),
            pltpu.VMEM((ROWS, GATES, COLS), BF16),
            pltpu.VMEM((PADDED, STATE, COLS), F32),
            pltpu.VMEM((2, STATE, COLS), BF16),
            pltpu.VMEM((2, STATE, COLS), BF16),
            pltpu.VMEM((2, EDGE, STATE), BF16),
            pltpu.VMEM((2, EDGE, STATE), BF16),
            pltpu.VMEM((PADDED, 3 * GATES, COLS), BF16),
            pltpu.VMEM((3, 3, HALF, STATE), BF16),
            pltpu.VMEM((3, 3, HALF, STATE), BF16),
            pltpu.VMEM((3, 3, HALF, STATE), F32),
            pltpu.VMEM((3, 3, HALF, STATE), BF16),
            [pltpu.VMEM((n1 - 1, 3, r1, STATE), BF16) for n1, r1, _, _, _ in chunk],
            [pltpu.VMEM((n2, 3, r2, STATE), F32) for _, _, n2, r2, _ in chunk],
            [pltpu.VMEM((n2 - 1, 3, r2, STATE), F32) for _, _, n2, r2, _ in chunk],
            [pltpu.VMEM((n3, 3, r2, STATE), F32) for _, _, _, r2, n3 in chunk],
            [pltpu.VMEM((n2, 3, r2, STATE), BF16) for _, _, n2, r2, _ in chunk],
            [pltpu.VMEM((n, 8, GATES), F32) for n in (2, nx, ny, zh * zl)],
            dma((len(inputs),)),
            dma((2, 2)),
            dma((2, 2)),
            dma((3, 2)),
            dma((3, 2)),
            dma((7, 3, most)),
            dma((7, 3, most)),
            dma((4, most)),
            dma((4, most)),
        ],
        compiler_params=pltpu.CompilerParams(
            collective_id=0, has_side_effects=True, vmem_limit_bytes=VMEM_LIMIT
        ),
        name="whole_step",
    )(*[pltpu.with_memory_space_constraint(value, pltpu.HBM) for value in inputs])

    hidden_next, cell_next, grad_inputs, grad_hidden, grad_cell, grad_kernel, grad_bias = pl.pallas_call(
        finish_kernel,
        out_shape=[
            cells,
            wide_cells,
            cells,
            cells,
            wide_cells,
            shape_of((9, GATES, STATE), F32),
            shape_of((1, GATES), F32),
        ],
        in_specs=[VMEM_SPEC] * 7,
        out_specs=[pl.BlockSpec(memory_space=pltpu.HBM)] * 7,
        scratch_shapes=[pltpu.VMEM((9, GATES, STATE), F32), dma((9,))],
        compiler_params=pltpu.CompilerParams(vmem_limit_bytes=VMEM_LIMIT),
        name="results",
    )(*results)
    shape = (hid, ROWS, COLS)
    return (
        hidden_next,
        cell_next.reshape(shape),
        grad_inputs,
        grad_hidden,
        grad_cell.reshape(shape),
        grad_kernel,
        grad_bias.reshape(GATES),
    )


def solution(mesh):
    lat, lon = mesh.shape["lat"], mesh.shape["lon"]
    sizes = {(16, 32): (4, 8, 2, 4), (4, 4): (2, 2, 1, 2)}[(lat, lon)]
    cells = P(None, "lat", "lon")
    flat = P("lat", "lon")
    return jax.shard_map(
        functools.partial(body, sizes),
        mesh=mesh,
        in_specs=(cells, cells, cells, P(), P(), P(), flat, flat, flat, cells),
        out_specs=(cells, cells, cells, cells, cells, P(), P()),
        check_vma=False,
    )
```

```python
import functools
import math

import jax
import jax.numpy as jnp
from jax import lax
from jax.experimental import pallas as pl
from jax.experimental.pallas import tpu as pltpu
from jax.sharding import PartitionSpec as P

MESH = pl.DeviceIdType.MESH
F32 = jnp.float32
BF16 = jnp.bfloat16
ROWS = 8
COLS = 128
PADDED = ROWS + 2
STATE = 128
GATES = 256
HALF = GATES // 2
LANES = 128
EDGE = 16
VMEM_SPEC = pl.BlockSpec(memory_space=pltpu.VMEM)
VMEM_LIMIT = 48 * 1024 * 1024


class Place:
    def __init__(self, sizes):
        self.nx, self.ny, self.zh, self.zl = sizes
        self.nz = self.zh * self.zl
        self.nlat = self.nx * self.zh * 2
        self.nlon = self.ny * self.zl
        self.lat = lax.axis_index("lat")
        self.lon = lax.axis_index("lon")
        self.core = lax.rem(self.lat, 2)
        chip = self.lat // 2
        self.z_hi = lax.rem(chip, self.zh)
        self.x = chip // self.zh
        self.z_lo = lax.rem(self.lon, self.zl)
        self.y = self.lon // self.zl
        self.z = self.z_hi * self.zl + self.z_lo
        self.count = {"core": 2, "x": self.nx, "y": self.ny, "z": self.nz}
        self.index = {"core": self.core, "x": self.x, "y": self.y, "z": self.z}
        self.north = self.lat == 0
        self.south = self.lat == self.nlat - 1

    def at(self, x, y, z, core):
        lat = (x * self.zh + z // self.zl) * 2 + core
        lon = y * self.zl + lax.rem(z, self.zl)
        return (lat, lon)

    def peer(self, axis, steps):
        other = lax.rem(self.index[axis] + steps, self.count[axis])
        where = dict(self.index)
        where[axis] = other
        return self.at(where["x"], where["y"], where["z"], where["core"]), other

    def peers(self, axis):
        count = self.count[axis]
        order = sorted(range(1, count), key=lambda steps: min(steps, count - steps))
        return [(steps - 1, *self.peer(axis, steps)) for steps in order]

    def up(self):
        opposite = lax.rem(self.lon + self.nlon // 2, self.nlon)
        lat = jnp.where(self.north, 0, self.lat - 1)
        return (lat, jnp.where(self.north, opposite, self.lon))

    def down(self):
        opposite = lax.rem(self.lon + self.nlon // 2, self.nlon)
        lat = jnp.where(self.south, self.nlat - 1, self.lat + 1)
        return (lat, jnp.where(self.south, opposite, self.lon))

    def east(self):
        return (self.lat, lax.rem(self.lon + 1, self.nlon))

    def west(self):
        return (self.lat, lax.rem(self.lon + self.nlon - 1, self.nlon))

    def around(self):
        return [self.up(), self.down(), self.east(), self.west(), *self.diagonal()]

    def diagonal(self):
        found = []
        for lat, lon in (self.up(), self.down()):
            for steps in (1, self.nlon - 1):
                found.append((lat, lax.rem(lon + steps, self.nlon)))
        return found


def greet(devices):
    barrier = pltpu.get_barrier_semaphore()
    for device in devices:
        pl.semaphore_signal(barrier, inc=1, device_id=device, device_id_type=MESH)
    return barrier


def remote(source, target, send_sem, recv_sem, device):
    return pltpu.make_async_remote_copy(
        src_ref=source,
        dst_ref=target,
        send_sem=send_sem,
        recv_sem=recv_sem,
        device_id=device,
        device_id_type=MESH,
    )


def lane_ids(shape):
    return lax.broadcasted_iota(jnp.int32, shape, len(shape) - 1)


def rows_out(place, first, last, halo, send_sem, recv_sem):
    upper_slot = jnp.where(place.north, 0, 1)
    lower_slot = jnp.where(place.south, 1, 0)
    copies = [
        remote(first, halo.at[upper_slot], send_sem.at[0], recv_sem.at[upper_slot], place.up()),
        remote(last, halo.at[lower_slot], send_sem.at[1], recv_sem.at[lower_slot], place.down()),
    ]
    for copy in copies:
        copy.start()
    waits = [
        remote(first, halo.at[0], send_sem.at[0], recv_sem.at[0], place.up()),
        remote(last, halo.at[1], send_sem.at[1], recv_sem.at[1], place.down()),
    ]
    return copies, waits


def to_edge(total):
    return jnp.transpose(total)[0:EDGE]


def corners_out(place, outgoing, corners, send_sem, recv_sem):
    copies, waits = [], []
    for i, device in enumerate(place.diagonal()):
        slot = jnp.where(place.north, 0, 1) if i < 2 else jnp.where(place.south, 1, 0)
        side = i % 2
        copy = remote(outgoing.at[i], corners.at[slot, side], send_sem.at[i], recv_sem.at[slot, side], device)
        copy.start()
        copies.append(copy)
        waits.append(remote(outgoing.at[i], corners.at[i // 2, side], send_sem.at[i], recv_sem.at[i // 2, side], device))
    return copies, waits


def from_edge(edge):
    rest = jnp.zeros((LANES - EDGE, edge.shape[1]), F32)
    return jnp.transpose(jnp.concatenate([edge.astype(F32), rest], axis=0))


def collect(total, row, position, shift, lanes):
    return jnp.where(lanes == position, pltpu.roll(row, shift % LANES, 1), total)


def cols_out(place, edges, sides, send_sem, recv_sem):
    copies = [
        remote(edges.at[0], sides.at[0], send_sem.at[0], recv_sem.at[0], place.east()),
        remote(edges.at[1], sides.at[1], send_sem.at[1], recv_sem.at[1], place.west()),
    ]
    for copy in copies:
        copy.start()
    return copies


def spread(values, sides_low, sides_high, lanes, position):
    before = jnp.where(lanes == 0, pltpu.roll(sides_low, (-position) % LANES, 1), pltpu.roll(values, 1, 1))
    after = jnp.where(
        lanes == COLS - 1, pltpu.roll(sides_high, (COLS - 1 - position) % LANES, 1), pltpu.roll(values, COLS - 1, 1)
    )
    return before, after


ORDERS = (("y", "x", "z"), ("z", "x", "y"), ("x", "y", "z"))
EARLY = ((1, 2), (3, 4), (5, 6))
LATE = (0, 7)


def step_kernel(
    sizes,
    scaling,
    below_hbm,
    hidden_hbm,
    cell_hbm,
    weights_hbm,
    gate_bias_hbm,
    readout_hbm,
    target_hbm,
    land_hbm,
    fire_hbm,
    hidden_grad_hbm,
    hidden_next,
    cell_next,
    grad_inputs,
    grad_hidden,
    grad_cell,
    kernel_low,
    bias_sum,
    below,
    hidden,
    cell_prev,
    weights,
    gate_bias,
    readout,
    target,
    land,
    fire,
    hidden_grad,
    wide,
    wide_grad,
    rows,
    halo,
    edges,
    sides,
    corner_edges,
    corners,
    windows,
    kernel_acc,
    turned,
    low_rows,
    field,
    rims,
    low_halo,
    low_edges,
    low_sides,
    low_windows,
    pair_out,
    pair_in,
    owned,
    first_out,
    first_in,
    second_out,
    second_in,
    third,
    gathered,
    bias_bufs,
    load_sem,
    row_send,
    row_recv,
    col_send,
    col_recv,
    corner_send,
    corner_recv,
    sends,
    recvs,
    bias_send,
    bias_recv,
):
    place = Place(sizes)
    hid = hidden_next.shape[0]
    width = grad_inputs.shape[0]
    partner, _ = place.peer("core", 1)
    devices = place.around()
    for axis in ("z", "y", "x"):
        devices += [device for _, device, _ in reversed(place.peers(axis))]
    devices.append(partner)
    barrier = greet(devices)
    mine = pl.multiple_of(place.core * HALF, HALF)
    theirs = pl.multiple_of((1 - place.core) * HALF, HALF)
    pending = []

    sources = (below_hbm, hidden_hbm, weights_hbm, cell_hbm, hidden_grad_hbm, gate_bias_hbm, readout_hbm,
               target_hbm, land_hbm, fire_hbm)
    targets = (below, hidden, weights, cell_prev, hidden_grad, gate_bias, readout, target, land, fire)
    loads = [
        pltpu.make_async_copy(source, destination, load_sem.at[i])
        for i, (source, destination) in enumerate(zip(sources, targets))
    ]
    for load in loads:
        load.start()

    loads[0].wait()
    wide[pl.ds(0, width * ROWS), :] = below[...].astype(F32).reshape(width * ROWS, COLS)
    loads[1].wait()
    wide[pl.ds(width * ROWS, hid * ROWS), :] = hidden[...].astype(F32).reshape(hid * ROWS, COLS)

    def state_row(r):
        return wide[pl.ds(r, STATE, stride=ROWS), :]

    for r in (0, ROWS - 1):
        rows[r + 1] = state_row(r).astype(BF16)
    pl.semaphore_wait(barrier, len(devices))
    row_copies, row_waits = rows_out(place, rows.at[1], rows.at[ROWS], halo, row_send.at[0], row_recv.at[0])

    lanes = lane_ids((STATE, COLS))
    east = jnp.zeros((STATE, COLS), F32)
    west = jnp.zeros((STATE, COLS), F32)
    for r in range(ROWS):
        value = state_row(r)
        if 0 < r < ROWS - 1:
            rows[r + 1] = value.astype(BF16)
        east = collect(east, value, r + 1, r + 2, lanes)
        west = collect(west, value, r + 1, r + 1, lanes)
    ends = (to_edge(east), to_edge(west))
    for i in range(4):
        position = 1 if i < 2 else ROWS
        corner_edges[i] = jnp.broadcast_to(ends[i % 2][position : position + 1], (8, STATE))
    corner_copies, corner_waits = corners_out(place, corner_edges, corners, corner_send, corner_recv)
    edges[0] = ends[0].astype(BF16)
    edges[1] = ends[1].astype(BF16)
    col_copies = cols_out(place, edges, sides, col_send.at[0], col_recv.at[0])
    pending += row_copies + col_copies + corner_copies

    for load in loads[2:]:
        load.wait()
    wide_grad[...] = hidden_grad[...].astype(F32).reshape(hid * ROWS, COLS)
    bias_cols = jnp.transpose(jnp.broadcast_to(gate_bias[...], (LANES, GATES)))
    read_cols = jnp.transpose(jnp.broadcast_to(readout[...], (LANES, hid)))
    for t in range(9):
        turned[t] = jnp.transpose(weights[t].astype(F32)).astype(BF16)

    def open_windows(position, low, low_side, high_side):
        before, after = spread(low.astype(F32), low_side, high_side, lanes, position)
        windows[position, 0:STATE] = before.astype(BF16)
        windows[position, STATE : 2 * STATE] = low
        windows[position, 2 * STATE : 3 * STATE] = after.astype(BF16)

    for copy in col_copies:
        copy.wait_recv()
    low_side, high_side = from_edge(sides[0]), from_edge(sides[1])
    for position in range(1, PADDED - 1):
        open_windows(position, rows[position], low_side, high_side)

    flat = jnp.concatenate([weights[t] for t in range(9)], axis=1)

    def cells_of(pair, bias_total):
        columns = jnp.concatenate([windows[r : r + 3].reshape(9 * STATE, COLS) for r in pair], axis=1)
        both = jnp.dot(flat, columns, preferred_element_type=F32)
        for k, r in enumerate(pair):
            preact = both[:, k * COLS : (k + 1) * COLS] + bias_cols
            input_gate = jax.nn.sigmoid(preact[0:hid])
            forget_gate = jax.nn.sigmoid(preact[hid : 2 * hid])
            output_gate = jax.nn.sigmoid(preact[2 * hid : 3 * hid])
            candidate = jnp.tanh(preact[3 * hid : 4 * hid])
            land_row = land[r : r + 1, :].astype(F32)
            fire_row = fire[r : r + 1, :].astype(F32)
            prev = cell_prev[pl.ds(r, hid, stride=ROWS), :]
            cell = land_row * (forget_gate * prev + input_gate * candidate)
            squashed = jnp.tanh(cell)
            new_hidden = (output_gate * squashed).astype(BF16).astype(F32)
            predicted = jnp.sum(read_cols * new_hidden, axis=0, keepdims=True)
            miss = 2.0 * (fire_row * (predicted - target[r : r + 1, :]))
            total_grad = wide_grad[pl.ds(r, hid, stride=ROWS), :] + miss * read_cols
            cell_grad = land_row * total_grad * output_gate * (1.0 - squashed * squashed)
            pre_grad = jnp.concatenate(
                [
                    cell_grad * candidate * input_gate * (1.0 - input_gate),
                    cell_grad * prev * forget_gate * (1.0 - forget_gate),
                    total_grad * squashed * output_gate * (1.0 - output_gate),
                    cell_grad * input_gate * (1.0 - candidate * candidate),
                ],
                axis=0,
            )
            cell_next[pl.ds(r, hid, stride=ROWS), :] = cell
            grad_cell[pl.ds(r, hid, stride=ROWS), :] = cell_grad * forget_gate
            wide[pl.ds(r, hid, stride=ROWS), :] = new_hidden
            bias_total = bias_total + pre_grad
            low_rows[r] = pre_grad.astype(BF16)
        return bias_total

    def kernel_terms(cells, rows_in, a):
        seen = jnp.concatenate([windows[r + a] for r in rows_in], axis=1)
        return lax.dot_general(cells, seen, (((1,), (1,)), ((), ())), preferred_element_type=F32)

    bias_total = jnp.zeros((GATES, COLS), F32)
    for pair in EARLY:
        bias_total = cells_of(pair, bias_total)
    cells = jnp.concatenate([low_rows[r] for r in range(1, ROWS - 1)], axis=1)
    for a in range(3):
        kernel_acc[a] = kernel_terms(cells, range(1, ROWS - 1), a)

    for wait in row_waits + corner_waits:
        wait.wait_recv()
    for slot, position in ((0, 0), (1, PADDED - 1)):
        ends = [jnp.transpose(jnp.broadcast_to(corners[slot, side, 0:1], (LANES, STATE))) for side in range(2)]
        open_windows(position, halo[slot], *ends)
    bias_total = cells_of(LATE, bias_total)

    halves = [pl.ds(theirs, HALF), pl.ds(mine, HALF)]
    cells = jnp.concatenate(
        [jnp.concatenate([low_rows[r, half, :] for r in LATE], axis=1) for half in halves], axis=0
    )
    pair_copies = []
    for a in range(3):
        part = kernel_terms(cells, LATE, a)
        given = part[0:HALF] + kernel_acc[a, halves[0], :]
        kept = part[HALF:] + kernel_acc[a, halves[1], :]
        for b in range(3):
            pair_out[a, b] = given[:, b * STATE : (b + 1) * STATE].astype(BF16)
        copy = remote(pair_out.at[a], pair_in.at[a], sends.at[0, a, 0], recvs.at[0, a, 0], partner)
        copy.start()
        pair_copies.append(copy)
        for b in range(3):
            owned[a, b] = kept[:, b * STATE : (b + 1) * STATE]

    first_copies = []
    for a in range(3):
        pair_copies[a].wait_recv()
        total = owned[a] + pair_in[a].astype(F32)
        owned[a] = total
        first_out[a] = total.astype(BF16)
        axis = ORDERS[a][0]
        rows1 = HALF // place.count[axis]
        copies = []
        for k, device, other in reversed(place.peers(axis)):
            start = pl.multiple_of(other * rows1, rows1)
            copy = remote(
                first_out.at[a, :, pl.ds(start, rows1), :],
                first_in[a].at[k],
                sends.at[1, a, k],
                recvs.at[1, a, k],
                device,
            )
            copy.start()
            copies.append(copy)
        first_copies.append(copies)
    pending += pair_copies

    def bias_start(stage, axis, value):
        slot = place.index[axis]
        buf = bias_bufs[stage]
        buf[slot] = value
        copies = []
        for k, device, _ in place.peers(axis):
            copy = remote(buf.at[slot], buf.at[slot], bias_send.at[stage, k], bias_recv.at[stage, k], device)
            copy.start()
            copies.append(copy)
        return copies

    def bias_finish(stage, axis, copies):
        buf = bias_bufs[stage]
        for copy in copies:
            copy.wait_recv()
        pending.extend(copies)
        total = buf[0]
        for k in range(1, place.count[axis]):
            total = total + buf[k]
        return total

    bias = lax.dot_general(
        jnp.ones((8, COLS), F32),
        bias_total,
        (((1,), (1,)), ((), ())),
        precision=lax.Precision.HIGHEST,
        preferred_element_type=F32,
    )
    bias_copies = bias_start(0, "core", bias)
    hidden_next[...] = wide[pl.ds(0, hid * ROWS), :].reshape(hid, ROWS, COLS).astype(BF16)

    gate_lanes = lane_ids((GATES, COLS))
    east = jnp.zeros((GATES, COLS), F32)
    west = jnp.zeros((GATES, COLS), F32)
    for r in range(ROWS):
        value = low_rows[r].astype(F32)
        before = jnp.where(gate_lanes == 0, 0.0, pltpu.roll(value, 1, 1))
        after = jnp.where(gate_lanes == COLS - 1, 0.0, pltpu.roll(value, COLS - 1, 1))
        low_windows[r + 1, 0:GATES] = before.astype(BF16)
        low_windows[r + 1, GATES : 2 * GATES] = low_rows[r]
        low_windows[r + 1, 2 * GATES : 3 * GATES] = after.astype(BF16)
        east = collect(east, value, r + 1, r + 2, gate_lanes)
        west = collect(west, value, r + 1, r + 1, gate_lanes)
    for slot, (value, last) in enumerate(((east, 2), (west, 0))):
        shifts = jnp.concatenate([pltpu.roll(value, a % LANES, 1).astype(BF16) for a in (-1, 0, 1)], axis=0)
        taps = jnp.concatenate([turned[3 * a + last] for a in range(3)], axis=1)
        low_edges[slot] = to_edge(jnp.dot(taps, shifts, preferred_element_type=F32)).astype(BF16)
    low_copies = cols_out(place, low_edges, low_sides, col_send.at[2], col_recv.at[2])

    low_windows[0] = jnp.zeros((3 * GATES, COLS), BF16)
    low_windows[PADDED - 1] = jnp.zeros((3 * GATES, COLS), BF16)
    flipped = jnp.concatenate([turned[8 - q] for q in range(9)], axis=1)
    for pair in range(ROWS // 2):
        blocks = [low_windows[r : r + 3].reshape(9 * GATES, COLS) for r in (2 * pair, 2 * pair + 1)]
        both = jnp.dot(flipped, jnp.concatenate(blocks, axis=1), preferred_element_type=F32)
        for k in range(2):
            field[2 * pair + k] = both[:, k * COLS : (k + 1) * COLS]
    field[ROWS] = jnp.dot(flipped[:, 6 * GATES :], low_windows[1], preferred_element_type=F32)
    field[ROWS + 1] = jnp.dot(flipped[:, : 3 * GATES], low_windows[ROWS], preferred_element_type=F32)
    bias = bias_finish(0, "core", bias_copies)
    bias_copies = bias_start(1, "x", bias)

    second_copies = []

    def second_start(a):
        axis1, axis2, _ = ORDERS[a]
        n1, n2 = place.count[axis1], place.count[axis2]
        rows1 = HALF // n1
        rows2 = rows1 // n2
        for copy in reversed(first_copies[a]):
            copy.wait_recv()
        pending.extend(first_copies[a])
        start = pl.multiple_of(place.index[axis1] * rows1, rows1)
        total = owned[a, :, pl.ds(start, rows1), :]
        for k in range(n1 - 1):
            total = total + first_in[a][k].astype(F32)
        for p in range(n2):
            second_out[a][p] = total[:, p * rows2 : (p + 1) * rows2, :]
        copies = []
        for k, device, other in reversed(place.peers(axis2)):
            copy = remote(second_out[a].at[other], second_in[a].at[k], sends.at[2, a, k], recvs.at[2, a, k], device)
            copy.start()
            copies.append(copy)
        second_copies.append((a, copies))

    second_start(2)
    second_start(0)
    second_start(1)

    for copy in low_copies:
        copy.wait_recv()
    low_side, high_side = from_edge(low_sides[0]), from_edge(low_sides[1])

    def arrived(position):
        first = jnp.where(lanes == 0, pltpu.roll(low_side, (-position) % LANES, 1), 0.0)
        last = jnp.where(lanes == COLS - 1, pltpu.roll(high_side, (COLS - 1 - position) % LANES, 1), 0.0)
        return first + last

    rims[0] = (field[ROWS] + arrived(0)).astype(BF16)
    rims[1] = (field[ROWS + 1] + arrived(PADDED - 1)).astype(BF16)
    row_copies, row_waits = rows_out(place, rims.at[0], rims.at[1], low_halo, row_send.at[1], row_recv.at[1])
    pending += low_copies + row_copies
    for r in range(ROWS):
        field[r] = field[r] + arrived(r + 1)
    bias = bias_finish(1, "x", bias_copies)
    bias_copies = bias_start(2, "y", bias)

    third_copies = []
    for a, copies2 in second_copies:
        _, axis2, axis3 = ORDERS[a]
        for copy in reversed(copies2):
            copy.wait_recv()
        pending += copies2
        total = second_out[a][place.index[axis2]]
        for k in range(place.count[axis2] - 1):
            total = total + second_in[a][k]
        slot = place.index[axis3]
        third[a][slot] = total
        copies = []
        for k, device, _ in reversed(place.peers(axis3)):
            copy = remote(third[a].at[slot], third[a].at[slot], sends.at[3, a, k], recvs.at[3, a, k], device)
            copy.start()
            copies.append(copy)
        third_copies.append((a, copies))

    bias = bias_finish(2, "y", bias_copies)
    bias_copies = bias_start(3, "z", bias)

    fourth_copies = []
    for a, copies3 in third_copies:
        _, axis2, axis3 = ORDERS[a]
        for copy in reversed(copies3):
            copy.wait_recv()
        pending += copies3
        total = third[a][0]
        for k in range(1, place.count[axis3]):
            total = total + third[a][k]
        slot = place.index[axis2]
        gathered[a][slot] = (total * scaling).astype(BF16)
        copies = []
        for k, device, _ in reversed(place.peers(axis2)):
            copy = remote(gathered[a].at[slot], gathered[a].at[slot], sends.at[4, a, k], recvs.at[4, a, k], device)
            copy.start()
            copies.append(copy)
        fourth_copies.append((a, copies))

    def block_of(a, owner):
        rows1 = HALF // place.count[ORDERS[a][0]]
        start = pl.multiple_of(mine + owner * rows1, rows1)
        return kernel_low.at[pl.ds(3 * a, 3), pl.ds(start, rows1), :]

    last_copies = []

    def forward(a, owner, slot):
        block = block_of(a, owner)
        copy = remote(block, block, sends.at[6, a, slot], recvs.at[6, a, slot], partner)
        copy.start()
        last_copies.append(copy)

    fifth_copies = []
    for a, copies4 in sorted(fourth_copies, key=lambda entry: entry[0]):
        axis1, axis2, _ = ORDERS[a]
        n1 = place.count[axis1]
        for copy in reversed(copies4):
            copy.wait_recv()
        pending += copies4
        block = block_of(a, place.index[axis1])
        block[...] = jnp.concatenate(
            [gathered[a][p].astype(F32) for p in range(place.count[axis2])], axis=1
        ).astype(BF16)
        copies = []
        for k, device, _ in reversed(place.peers(axis1)):
            copy = remote(block, block, sends.at[5, a, k], recvs.at[5, a, k], device)
            copy.start()
            copies.append((copy, k, lax.rem(place.index[axis1] + n1 - 1 - k, n1)))
        forward(a, place.index[axis1], n1 - 1)
        fifth_copies.append((a, copies))

    bias_sum[...] = bias_finish(3, "z", bias_copies) * scaling
    for slot, r in ((0, 0), (1, ROWS - 1)):
        row_waits[slot].wait_recv()
        field[r] = field[r] + low_halo[slot].astype(F32)
    for r in range(ROWS):
        wide[pl.ds(r, STATE, stride=ROWS), :] = field[r]
    grad_inputs[...] = wide[pl.ds(0, width * ROWS), :].reshape(width, ROWS, COLS).astype(BF16)
    grad_hidden[...] = wide[pl.ds(width * ROWS, hid * ROWS), :].reshape(hid, ROWS, COLS).astype(BF16)

    for a, copies5 in fifth_copies[2:] + fifth_copies[:2]:
        for copy, k, sender in reversed(copies5):
            copy.wait_recv()
            forward(a, sender, k)
            pending.append(copy)
    for copy in last_copies:
        copy.wait_recv()
    pending += last_copies
    for copy in pending:
        copy.wait_send()


def finish_kernel(
    hidden_next,
    cell_next,
    grad_inputs,
    grad_hidden,
    grad_cell,
    kernel_low,
    bias_sum,
    hidden_next_out,
    cell_next_out,
    grad_inputs_out,
    grad_hidden_out,
    grad_cell_out,
    kernel_out,
    bias_out,
    kernel_wide,
    sems,
):
    pairs = (
        (hidden_next, hidden_next_out),
        (cell_next, cell_next_out),
        (grad_inputs, grad_inputs_out),
        (grad_hidden, grad_hidden_out),
        (grad_cell, grad_cell_out),
        (bias_sum.at[0:1], bias_out),
    )
    copies = [pltpu.make_async_copy(source, target, sems.at[i]) for i, (source, target) in enumerate(pairs)]
    for copy in copies:
        copy.start()
    for a in range(3):
        taps = pl.ds(3 * a, 3)
        kernel_wide[taps] = kernel_low[taps].astype(F32)
        copy = pltpu.make_async_copy(kernel_wide.at[taps], kernel_out.at[taps], sems.at[len(pairs) + a])
        copy.start()
        copies.append(copy)
    for copy in copies:
        copy.wait()


def shape_of(shape, dtype):
    return jax.ShapeDtypeStruct(shape, dtype)


def body(
    sizes,
    inputs_below,
    hidden_prev,
    cell_prev,
    kernel_weights,
    gate_bias,
    readout,
    target_field,
    land_mask,
    fire_mask,
    hidden_grad,
):
    nx, ny, zh, zl = sizes
    count = {"x": nx, "y": ny, "z": zh * zl}
    hid = hidden_prev.shape[0]
    dma = pltpu.SemaphoreType.DMA
    scaling = 1.0 / math.sqrt(ROWS * nx * zh * 2 * COLS * ny * zl)
    most = max(nx, ny, zh * zl)
    chunk = []
    for axis1, axis2, axis3 in ORDERS:
        rows1 = HALF // count[axis1]
        chunk.append((count[axis1], rows1, count[axis2], rows1 // count[axis2], count[axis3]))
    cells = shape_of((hid, ROWS, COLS), BF16)
    wide_cells = shape_of((hid * ROWS, COLS), F32)
    inputs = (
        inputs_below,
        hidden_prev,
        cell_prev.reshape(hid * ROWS, COLS),
        kernel_weights,
        gate_bias.reshape(1, GATES),
        readout.reshape(1, hid),
        target_field,
        land_mask,
        fire_mask,
        hidden_grad,
    )
    results = pl.pallas_call(
        functools.partial(step_kernel, sizes, scaling),
        out_shape=[
            cells,
            wide_cells,
            cells,
            cells,
            wide_cells,
            shape_of((9, GATES, STATE), BF16),
            shape_of((8, GATES), F32),
        ],
        in_specs=[pl.BlockSpec(memory_space=pltpu.HBM)] * len(inputs),
        out_specs=[VMEM_SPEC] * 7,
        scratch_shapes=[pltpu.VMEM(value.shape, value.dtype) for value in inputs]
        + [
            pltpu.VMEM((STATE * ROWS, COLS), F32),
            pltpu.VMEM((hid * ROWS, COLS), F32),
            pltpu.VMEM((PADDED, STATE, COLS), BF16),
            pltpu.VMEM((2, STATE, COLS), BF16),
            pltpu.VMEM((2, EDGE, STATE), BF16),
            pltpu.VMEM((2, EDGE, STATE), BF16),
            pltpu.VMEM((4, 8, STATE), F32),
            pltpu.VMEM((2, 2, 8, STATE), F32),
            pltpu.VMEM((PADDED, 3 * STATE, COLS), BF16),
            pltpu.VMEM((3, GATES, 3 * STATE), F32),
            pltpu.VMEM((9, STATE, GATES), BF16),
            pltpu.VMEM((ROWS, GATES, COLS), BF16),
            pltpu.VMEM((PADDED, STATE, COLS), F32),
            pltpu.VMEM((2, STATE, COLS), BF16),
            pltpu.VMEM((2, STATE, COLS), BF16),
            pltpu.VMEM((2, EDGE, STATE), BF16),
            pltpu.VMEM((2, EDGE, STATE), BF16),
            pltpu.VMEM((PADDED, 3 * GATES, COLS), BF16),
            pltpu.VMEM((3, 3, HALF, STATE), BF16),
            pltpu.VMEM((3, 3, HALF, STATE), BF16),
            pltpu.VMEM((3, 3, HALF, STATE), F32),
            pltpu.VMEM((3, 3, HALF, STATE), BF16),
            [pltpu.VMEM((n1 - 1, 3, r1, STATE), BF16) for n1, r1, _, _, _ in chunk],
            [pltpu.VMEM((n2, 3, r2, STATE), F32) for _, _, n2, r2, _ in chunk],
            [pltpu.VMEM((n2 - 1, 3, r2, STATE), F32) for _, _, n2, r2, _ in chunk],
            [pltpu.VMEM((n3, 3, r2, STATE), F32) for _, _, _, r2, n3 in chunk],
            [pltpu.VMEM((n2, 3, r2, STATE), BF16) for _, _, n2, r2, _ in chunk],
            [pltpu.VMEM((n, 8, GATES), F32) for n in (2, nx, ny, zh * zl)],
            dma((len(inputs),)),
            dma((2, 2)),
            dma((2, 2)),
            dma((3, 2)),
            dma((3, 2)),
            dma((4,)),
            dma((2, 2)),
            dma((7, 3, most)),
            dma((7, 3, most)),
            dma((4, most)),
            dma((4, most)),
        ],
        compiler_params=pltpu.CompilerParams(
            collective_id=0, has_side_effects=True, vmem_limit_bytes=VMEM_LIMIT
        ),
        name="whole_step",
    )(*[pltpu.with_memory_space_constraint(value, pltpu.HBM) for value in inputs])

    hidden_next, cell_next, grad_inputs, grad_hidden, grad_cell, grad_kernel, grad_bias = pl.pallas_call(
        finish_kernel,
        out_shape=[
            cells,
            wide_cells,
            cells,
            cells,
            wide_cells,
            shape_of((9, GATES, STATE), F32),
            shape_of((1, GATES), F32),
        ],
        in_specs=[VMEM_SPEC] * 7,
        out_specs=[pl.BlockSpec(memory_space=pltpu.HBM)] * 7,
        scratch_shapes=[pltpu.VMEM((9, GATES, STATE), F32), dma((9,))],
        compiler_params=pltpu.CompilerParams(vmem_limit_bytes=VMEM_LIMIT),
        name="results",
    )(*results)
    shape = (hid, ROWS, COLS)
    return (
        hidden_next,
        cell_next.reshape(shape),
        grad_inputs,
        grad_hidden,
        grad_cell.reshape(shape),
        grad_kernel,
        grad_bias.reshape(GATES),
    )


def solution(mesh):
    lat, lon = mesh.shape["lat"], mesh.shape["lon"]
    sizes = {(16, 32): (4, 8, 2, 4), (4, 4): (2, 2, 1, 2)}[(lat, lon)]
    cells = P(None, "lat", "lon")
    flat = P("lat", "lon")
    return jax.shard_map(
        functools.partial(body, sizes),
        mesh=mesh,
        in_specs=(cells, cells, cells, P(), P(), P(), flat, flat, flat, cells),
        out_specs=(cells, cells, cells, cells, cells, P(), P()),
        check_vma=False,
    )
```

```python
import functools
import math

import jax
import jax.numpy as jnp
from jax import lax
from jax.experimental import pallas as pl
from jax.experimental.pallas import tpu as pltpu
from jax.sharding import PartitionSpec as P

MESH = pl.DeviceIdType.MESH
F32 = jnp.float32
BF16 = jnp.bfloat16
ROWS = 8
COLS = 128
PADDED = ROWS + 2
STATE = 128
GATES = 256
HALF = GATES // 2
LANES = 128
EDGE = 16
VMEM_SPEC = pl.BlockSpec(memory_space=pltpu.VMEM)
VMEM_LIMIT = 48 * 1024 * 1024


class Place:
    def __init__(self, sizes):
        self.nx, self.ny, self.zh, self.zl = sizes
        self.nz = self.zh * self.zl
        self.nlat = self.nx * self.zh * 2
        self.nlon = self.ny * self.zl
        self.lat = lax.axis_index("lat")
        self.lon = lax.axis_index("lon")
        self.core = lax.rem(self.lat, 2)
        chip = self.lat // 2
        self.z_hi = lax.rem(chip, self.zh)
        self.x = chip // self.zh
        self.z_lo = lax.rem(self.lon, self.zl)
        self.y = self.lon // self.zl
        self.z = self.z_hi * self.zl + self.z_lo
        self.count = {"core": 2, "x": self.nx, "y": self.ny, "z": self.nz}
        self.index = {"core": self.core, "x": self.x, "y": self.y, "z": self.z}
        self.north = self.lat == 0
        self.south = self.lat == self.nlat - 1

    def at(self, x, y, z, core):
        lat = (x * self.zh + z // self.zl) * 2 + core
        lon = y * self.zl + lax.rem(z, self.zl)
        return (lat, lon)

    def peer(self, axis, steps):
        other = lax.rem(self.index[axis] + steps, self.count[axis])
        where = dict(self.index)
        where[axis] = other
        return self.at(where["x"], where["y"], where["z"], where["core"]), other

    def peers(self, axis):
        count = self.count[axis]
        order = sorted(range(1, count), key=lambda steps: min(steps, count - steps))
        return [(steps - 1, *self.peer(axis, steps)) for steps in order]

    def up(self):
        opposite = lax.rem(self.lon + self.nlon // 2, self.nlon)
        lat = jnp.where(self.north, 0, self.lat - 1)
        return (lat, jnp.where(self.north, opposite, self.lon))

    def down(self):
        opposite = lax.rem(self.lon + self.nlon // 2, self.nlon)
        lat = jnp.where(self.south, self.nlat - 1, self.lat + 1)
        return (lat, jnp.where(self.south, opposite, self.lon))

    def east(self):
        return (self.lat, lax.rem(self.lon + 1, self.nlon))

    def west(self):
        return (self.lat, lax.rem(self.lon + self.nlon - 1, self.nlon))

    def around(self):
        return [self.up(), self.down(), self.east(), self.west(), *self.diagonal()]

    def diagonal(self):
        found = []
        for lat, lon in (self.up(), self.down()):
            for steps in (1, self.nlon - 1):
                found.append((lat, lax.rem(lon + steps, self.nlon)))
        return found


def greet(devices):
    barrier = pltpu.get_barrier_semaphore()
    for device in devices:
        pl.semaphore_signal(barrier, inc=1, device_id=device, device_id_type=MESH)
    return barrier


def remote(source, target, send_sem, recv_sem, device):
    return pltpu.make_async_remote_copy(
        src_ref=source,
        dst_ref=target,
        send_sem=send_sem,
        recv_sem=recv_sem,
        device_id=device,
        device_id_type=MESH,
    )


def lane_ids(shape):
    return lax.broadcasted_iota(jnp.int32, shape, len(shape) - 1)


def rows_out(place, first, last, halo, send_sem, recv_sem):
    upper_slot = jnp.where(place.north, 0, 1)
    lower_slot = jnp.where(place.south, 1, 0)
    copies = [
        remote(first, halo.at[upper_slot], send_sem.at[0], recv_sem.at[upper_slot], place.up()),
        remote(last, halo.at[lower_slot], send_sem.at[1], recv_sem.at[lower_slot], place.down()),
    ]
    for copy in copies:
        copy.start()
    waits = [
        remote(first, halo.at[0], send_sem.at[0], recv_sem.at[0], place.up()),
        remote(last, halo.at[1], send_sem.at[1], recv_sem.at[1], place.down()),
    ]
    return copies, waits


def to_edge(total):
    return jnp.transpose(total)[0:EDGE]


def corners_out(place, outgoing, corners, send_sem, recv_sem):
    copies, waits = [], []
    for i, device in enumerate(place.diagonal()):
        slot = jnp.where(place.north, 0, 1) if i < 2 else jnp.where(place.south, 1, 0)
        side = i % 2
        copy = remote(outgoing.at[i], corners.at[slot, side], send_sem.at[i], recv_sem.at[slot, side], device)
        copy.start()
        copies.append(copy)
        waits.append(remote(outgoing.at[i], corners.at[i // 2, side], send_sem.at[i], recv_sem.at[i // 2, side], device))
    return copies, waits


def from_edge(edge):
    rest = jnp.zeros((LANES - EDGE, edge.shape[1]), F32)
    return jnp.transpose(jnp.concatenate([edge.astype(F32), rest], axis=0))


def collect(total, row, position, shift, lanes):
    return jnp.where(lanes == position, pltpu.roll(row, shift % LANES, 1), total)


def cols_out(place, edges, sides, send_sem, recv_sem):
    copies = [
        remote(edges.at[0], sides.at[0], send_sem.at[0], recv_sem.at[0], place.east()),
        remote(edges.at[1], sides.at[1], send_sem.at[1], recv_sem.at[1], place.west()),
    ]
    for copy in copies:
        copy.start()
    return copies


def spread(values, sides_low, sides_high, lanes, position):
    before = jnp.where(lanes == 0, pltpu.roll(sides_low, (-position) % LANES, 1), pltpu.roll(values, 1, 1))
    after = jnp.where(
        lanes == COLS - 1, pltpu.roll(sides_high, (COLS - 1 - position) % LANES, 1), pltpu.roll(values, COLS - 1, 1)
    )
    return before, after


ORDERS = (("y", "x", "z"), ("z", "x", "y"), ("x", "y", "z"))
EARLY = ((1, 2), (3, 4), (5, 6))
LATE = (0, 7)


def step_kernel(
    sizes,
    scaling,
    below_hbm,
    hidden_hbm,
    cell_hbm,
    weights_hbm,
    gate_bias_hbm,
    readout_hbm,
    target_hbm,
    land_hbm,
    fire_hbm,
    hidden_grad_hbm,
    hidden_next,
    cell_next,
    grad_inputs,
    grad_hidden,
    grad_cell,
    kernel_low,
    bias_sum,
    below,
    hidden,
    cell_prev,
    weights,
    gate_bias,
    readout,
    target,
    land,
    fire,
    hidden_grad,
    wide,
    wide_grad,
    rows,
    halo,
    edges,
    sides,
    corner_edges,
    corners,
    windows,
    kernel_acc,
    turned,
    low_rows,
    field,
    low_corner_edges,
    low_corners,
    rims,
    low_halo,
    low_edges,
    low_sides,
    low_windows,
    pair_out,
    pair_in,
    owned,
    first_out,
    first_in,
    second_out,
    second_in,
    third,
    gathered,
    bias_bufs,
    load_sem,
    row_send,
    row_recv,
    col_send,
    col_recv,
    corner_send,
    corner_recv,
    low_corner_send,
    low_corner_recv,
    sends,
    recvs,
    bias_send,
    bias_recv,
):
    place = Place(sizes)
    hid = hidden_next.shape[0]
    width = grad_inputs.shape[0]
    partner, _ = place.peer("core", 1)
    devices = place.around()
    for axis in ("z", "y", "x"):
        devices += [device for _, device, _ in reversed(place.peers(axis))]
    devices.append(partner)
    barrier = greet(devices)
    mine = pl.multiple_of(place.core * HALF, HALF)
    theirs = pl.multiple_of((1 - place.core) * HALF, HALF)
    pending = []

    sources = (below_hbm, hidden_hbm, weights_hbm, cell_hbm, hidden_grad_hbm, gate_bias_hbm, readout_hbm,
               target_hbm, land_hbm, fire_hbm)
    targets = (below, hidden, weights, cell_prev, hidden_grad, gate_bias, readout, target, land, fire)
    loads = [
        pltpu.make_async_copy(source, destination, load_sem.at[i])
        for i, (source, destination) in enumerate(zip(sources, targets))
    ]
    for load in loads:
        load.start()

    loads[0].wait()
    wide[pl.ds(0, width * ROWS), :] = below[...].astype(F32).reshape(width * ROWS, COLS)
    loads[1].wait()
    wide[pl.ds(width * ROWS, hid * ROWS), :] = hidden[...].astype(F32).reshape(hid * ROWS, COLS)

    def state_row(r):
        return wide[pl.ds(r, STATE, stride=ROWS), :]

    for r in (0, ROWS - 1):
        rows[r + 1] = state_row(r).astype(BF16)
    pl.semaphore_wait(barrier, len(devices))
    row_copies, row_waits = rows_out(place, rows.at[1], rows.at[ROWS], halo, row_send.at[0], row_recv.at[0])

    lanes = lane_ids((STATE, COLS))
    east = jnp.zeros((STATE, COLS), F32)
    west = jnp.zeros((STATE, COLS), F32)
    for r in range(ROWS):
        value = state_row(r)
        if 0 < r < ROWS - 1:
            rows[r + 1] = value.astype(BF16)
        east = collect(east, value, r + 1, r + 2, lanes)
        west = collect(west, value, r + 1, r + 1, lanes)
    ends = (to_edge(east), to_edge(west))
    for i in range(4):
        position = 1 if i < 2 else ROWS
        corner_edges[i] = jnp.broadcast_to(ends[i % 2][position : position + 1], (8, STATE))
    corner_copies, corner_waits = corners_out(place, corner_edges, corners, corner_send, corner_recv)
    edges[0] = ends[0].astype(BF16)
    edges[1] = ends[1].astype(BF16)
    col_copies = cols_out(place, edges, sides, col_send.at[0], col_recv.at[0])
    pending += row_copies + col_copies + corner_copies

    for load in loads[2:]:
        load.wait()
    wide_grad[...] = hidden_grad[...].astype(F32).reshape(hid * ROWS, COLS)
    bias_cols = jnp.transpose(jnp.broadcast_to(gate_bias[...], (LANES, GATES)))
    read_cols = jnp.transpose(jnp.broadcast_to(readout[...], (LANES, hid)))
    for t in range(9):
        turned[t] = jnp.transpose(weights[t].astype(F32)).astype(BF16)

    def open_windows(position, low, low_side, high_side):
        before, after = spread(low.astype(F32), low_side, high_side, lanes, position)
        windows[position, 0:STATE] = before.astype(BF16)
        windows[position, STATE : 2 * STATE] = low
        windows[position, 2 * STATE : 3 * STATE] = after.astype(BF16)

    for copy in col_copies:
        copy.wait_recv()
    low_side, high_side = from_edge(sides[0]), from_edge(sides[1])
    for position in range(1, PADDED - 1):
        open_windows(position, rows[position], low_side, high_side)

    flat = jnp.concatenate([weights[t] for t in range(9)], axis=1)

    def cells_of(pair, bias_total):
        columns = jnp.concatenate([windows[r : r + 3].reshape(9 * STATE, COLS) for r in pair], axis=1)
        both = jnp.dot(flat, columns, preferred_element_type=F32)
        for k, r in enumerate(pair):
            preact = both[:, k * COLS : (k + 1) * COLS] + bias_cols
            input_gate = jax.nn.sigmoid(preact[0:hid])
            forget_gate = jax.nn.sigmoid(preact[hid : 2 * hid])
            output_gate = jax.nn.sigmoid(preact[2 * hid : 3 * hid])
            candidate = jnp.tanh(preact[3 * hid : 4 * hid])
            land_row = land[r : r + 1, :].astype(F32)
            fire_row = fire[r : r + 1, :].astype(F32)
            prev = cell_prev[pl.ds(r, hid, stride=ROWS), :]
            cell = land_row * (forget_gate * prev + input_gate * candidate)
            squashed = jnp.tanh(cell)
            new_hidden = (output_gate * squashed).astype(BF16).astype(F32)
            predicted = jnp.sum(read_cols * new_hidden, axis=0, keepdims=True)
            miss = 2.0 * (fire_row * (predicted - target[r : r + 1, :]))
            total_grad = wide_grad[pl.ds(r, hid, stride=ROWS), :] + miss * read_cols
            cell_grad = land_row * total_grad * output_gate * (1.0 - squashed * squashed)
            pre_grad = jnp.concatenate(
                [
                    cell_grad * candidate * input_gate * (1.0 - input_gate),
                    cell_grad * prev * forget_gate * (1.0 - forget_gate),
                    total_grad * squashed * output_gate * (1.0 - output_gate),
                    cell_grad * input_gate * (1.0 - candidate * candidate),
                ],
                axis=0,
            )
            cell_next[pl.ds(r, hid, stride=ROWS), :] = cell
            grad_cell[pl.ds(r, hid, stride=ROWS), :] = cell_grad * forget_gate
            wide[pl.ds(r, hid, stride=ROWS), :] = new_hidden
            bias_total = bias_total + pre_grad
            low_rows[r] = pre_grad.astype(BF16)
        return bias_total

    def kernel_terms(cells, rows_in, a):
        seen = jnp.concatenate([windows[r + a] for r in rows_in], axis=1)
        return lax.dot_general(cells, seen, (((1,), (1,)), ((), ())), preferred_element_type=F32)

    bias_total = jnp.zeros((GATES, COLS), F32)
    for pair in EARLY:
        bias_total = cells_of(pair, bias_total)
    cells = jnp.concatenate([low_rows[r] for r in range(1, ROWS - 1)], axis=1)
    for a in range(3):
        kernel_acc[a] = kernel_terms(cells, range(1, ROWS - 1), a)

    for wait in row_waits + corner_waits:
        wait.wait_recv()
    for slot, position in ((0, 0), (1, PADDED - 1)):
        ends = [jnp.transpose(jnp.broadcast_to(corners[slot, side, 0:1], (LANES, STATE))) for side in range(2)]
        open_windows(position, halo[slot], *ends)
    bias_total = cells_of(LATE, bias_total)

    halves = [pl.ds(theirs, HALF), pl.ds(mine, HALF)]
    cells = jnp.concatenate(
        [jnp.concatenate([low_rows[r, half, :] for r in LATE], axis=1) for half in halves], axis=0
    )
    pair_copies = []
    for a in range(3):
        part = kernel_terms(cells, LATE, a)
        given = part[0:HALF] + kernel_acc[a, halves[0], :]
        kept = part[HALF:] + kernel_acc[a, halves[1], :]
        for b in range(3):
            pair_out[a, b] = given[:, b * STATE : (b + 1) * STATE].astype(BF16)
        copy = remote(pair_out.at[a], pair_in.at[a], sends.at[0, a, 0], recvs.at[0, a, 0], partner)
        copy.start()
        pair_copies.append(copy)
        for b in range(3):
            owned[a, b] = kept[:, b * STATE : (b + 1) * STATE]

    first_copies = []
    for a in range(3):
        pair_copies[a].wait_recv()
        total = owned[a] + pair_in[a].astype(F32)
        owned[a] = total
        first_out[a] = total.astype(BF16)
        axis = ORDERS[a][0]
        rows1 = HALF // place.count[axis]
        copies = []
        for k, device, other in reversed(place.peers(axis)):
            start = pl.multiple_of(other * rows1, rows1)
            copy = remote(
                first_out.at[a, :, pl.ds(start, rows1), :],
                first_in[a].at[k],
                sends.at[1, a, k],
                recvs.at[1, a, k],
                device,
            )
            copy.start()
            copies.append(copy)
        first_copies.append(copies)
    pending += pair_copies

    def bias_start(stage, axis, value):
        slot = place.index[axis]
        buf = bias_bufs[stage]
        buf[slot] = value
        copies = []
        for k, device, _ in place.peers(axis):
            copy = remote(buf.at[slot], buf.at[slot], bias_send.at[stage, k], bias_recv.at[stage, k], device)
            copy.start()
            copies.append(copy)
        return copies

    def bias_finish(stage, axis, copies):
        buf = bias_bufs[stage]
        for copy in copies:
            copy.wait_recv()
        pending.extend(copies)
        total = buf[0]
        for k in range(1, place.count[axis]):
            total = total + buf[k]
        return total

    bias = lax.dot_general(
        jnp.ones((8, COLS), F32),
        bias_total,
        (((1,), (1,)), ((), ())),
        precision=lax.Precision.HIGHEST,
        preferred_element_type=F32,
    )
    bias_copies = bias_start(0, "core", bias)
    hidden_next[...] = wide[pl.ds(0, hid * ROWS), :].reshape(hid, ROWS, COLS).astype(BF16)

    gate_lanes = lane_ids((GATES, COLS))
    east = jnp.zeros((GATES, COLS), F32)
    west = jnp.zeros((GATES, COLS), F32)
    for r in range(ROWS):
        value = low_rows[r].astype(F32)
        before = jnp.where(gate_lanes == 0, 0.0, pltpu.roll(value, 1, 1))
        after = jnp.where(gate_lanes == COLS - 1, 0.0, pltpu.roll(value, COLS - 1, 1))
        low_windows[r + 1, 0:GATES] = before.astype(BF16)
        low_windows[r + 1, GATES : 2 * GATES] = low_rows[r]
        low_windows[r + 1, 2 * GATES : 3 * GATES] = after.astype(BF16)
        east = collect(east, value, r + 1, r + 2, gate_lanes)
        west = collect(west, value, r + 1, r + 1, gate_lanes)
    for slot, (value, last) in enumerate(((east, 2), (west, 0))):
        shifts = jnp.concatenate([pltpu.roll(value, a % LANES, 1).astype(BF16) for a in (-1, 0, 1)], axis=0)
        taps = jnp.concatenate([turned[3 * a + last] for a in range(3)], axis=1)
        given_cells = to_edge(jnp.dot(taps, shifts, preferred_element_type=F32))
        low_edges[slot] = given_cells.astype(BF16)
        for i, position in ((slot, 0), (slot + 2, PADDED - 1)):
            low_corner_edges[i] = jnp.broadcast_to(given_cells[position : position + 1], (8, STATE))
    low_copies = cols_out(place, low_edges, low_sides, col_send.at[2], col_recv.at[2])
    low_corner_copies, low_corner_waits = corners_out(
        place, low_corner_edges, low_corners, low_corner_send, low_corner_recv
    )

    flipped = jnp.concatenate([turned[8 - q] for q in range(9)], axis=1)
    rims[0] = jnp.dot(flipped[:, 6 * GATES :], low_windows[1], preferred_element_type=F32).astype(BF16)
    rims[1] = jnp.dot(flipped[:, : 3 * GATES], low_windows[ROWS], preferred_element_type=F32).astype(BF16)
    row_copies, row_waits = rows_out(place, rims.at[0], rims.at[1], low_halo, row_send.at[1], row_recv.at[1])
    low_windows[0] = jnp.zeros((3 * GATES, COLS), BF16)
    low_windows[PADDED - 1] = jnp.zeros((3 * GATES, COLS), BF16)
    for pair in range(ROWS // 2):
        blocks = [low_windows[r : r + 3].reshape(9 * GATES, COLS) for r in (2 * pair, 2 * pair + 1)]
        both = jnp.dot(flipped, jnp.concatenate(blocks, axis=1), preferred_element_type=F32)
        for k in range(2):
            field[2 * pair + k] = both[:, k * COLS : (k + 1) * COLS]
    bias = bias_finish(0, "core", bias_copies)
    bias_copies = bias_start(1, "x", bias)

    second_copies = []

    def second_start(a):
        axis1, axis2, _ = ORDERS[a]
        n1, n2 = place.count[axis1], place.count[axis2]
        rows1 = HALF // n1
        rows2 = rows1 // n2
        for copy in reversed(first_copies[a]):
            copy.wait_recv()
        pending.extend(first_copies[a])
        start = pl.multiple_of(place.index[axis1] * rows1, rows1)
        total = owned[a, :, pl.ds(start, rows1), :]
        for k in range(n1 - 1):
            total = total + first_in[a][k].astype(F32)
        for p in range(n2):
            second_out[a][p] = total[:, p * rows2 : (p + 1) * rows2, :]
        copies = []
        for k, device, other in reversed(place.peers(axis2)):
            copy = remote(second_out[a].at[other], second_in[a].at[k], sends.at[2, a, k], recvs.at[2, a, k], device)
            copy.start()
            copies.append(copy)
        second_copies.append((a, copies))

    second_start(2)
    second_start(0)
    second_start(1)

    for copy in low_copies:
        copy.wait_recv()
    low_side, high_side = from_edge(low_sides[0]), from_edge(low_sides[1])

    def arrived(low_side, high_side, position):
        first = jnp.where(lanes == 0, pltpu.roll(low_side, (-position) % LANES, 1), 0.0)
        last = jnp.where(lanes == COLS - 1, pltpu.roll(high_side, (COLS - 1 - position) % LANES, 1), 0.0)
        return first + last

    pending += low_copies + row_copies + low_corner_copies
    for r in range(ROWS):
        field[r] = field[r] + arrived(low_side, high_side, r + 1)
    bias = bias_finish(1, "x", bias_copies)
    bias_copies = bias_start(2, "y", bias)

    third_copies = []
    for a, copies2 in sorted(second_copies, key=lambda entry: entry[0]):
        _, axis2, axis3 = ORDERS[a]
        for copy in reversed(copies2):
            copy.wait_recv()
        pending += copies2
        total = second_out[a][place.index[axis2]]
        for k in range(place.count[axis2] - 1):
            total = total + second_in[a][k]
        slot = place.index[axis3]
        third[a][slot] = total
        copies = []
        for k, device, _ in reversed(place.peers(axis3)):
            copy = remote(third[a].at[slot], third[a].at[slot], sends.at[3, a, k], recvs.at[3, a, k], device)
            copy.start()
            copies.append(copy)
        third_copies.append((a, copies))

    bias = bias_finish(2, "y", bias_copies)
    bias_copies = bias_start(3, "z", bias)

    fourth_copies = []
    for a, copies3 in third_copies:
        _, axis2, axis3 = ORDERS[a]
        for copy in reversed(copies3):
            copy.wait_recv()
        pending += copies3
        total = third[a][0]
        for k in range(1, place.count[axis3]):
            total = total + third[a][k]
        slot = place.index[axis2]
        gathered[a][slot] = (total * scaling).astype(BF16)
        copies = []
        for k, device, _ in reversed(place.peers(axis2)):
            copy = remote(gathered[a].at[slot], gathered[a].at[slot], sends.at[4, a, k], recvs.at[4, a, k], device)
            copy.start()
            copies.append(copy)
        fourth_copies.append((a, copies))

    def block_of(a, owner):
        rows1 = HALF // place.count[ORDERS[a][0]]
        start = pl.multiple_of(mine + owner * rows1, rows1)
        return kernel_low.at[pl.ds(3 * a, 3), pl.ds(start, rows1), :]

    last_copies = []

    def forward(a, owner, slot):
        block = block_of(a, owner)
        copy = remote(block, block, sends.at[6, a, slot], recvs.at[6, a, slot], partner)
        copy.start()
        last_copies.append(copy)

    fifth_copies = []
    for a, copies4 in fourth_copies:
        axis1, axis2, _ = ORDERS[a]
        n1 = place.count[axis1]
        for copy in reversed(copies4):
            copy.wait_recv()
        pending += copies4
        block = block_of(a, place.index[axis1])
        block[...] = jnp.concatenate(
            [gathered[a][p].astype(F32) for p in range(place.count[axis2])], axis=1
        ).astype(BF16)
        copies = []
        for k, device, _ in reversed(place.peers(axis1)):
            copy = remote(block, block, sends.at[5, a, k], recvs.at[5, a, k], device)
            copy.start()
            copies.append((copy, k, lax.rem(place.index[axis1] + n1 - 1 - k, n1)))
        forward(a, place.index[axis1], n1 - 1)
        fifth_copies.append((a, copies))

    bias_sum[...] = bias_finish(3, "z", bias_copies) * scaling
    for slot, r in ((0, 0), (1, ROWS - 1)):
        row_waits[slot].wait_recv()
        for wait in low_corner_waits[2 * slot : 2 * slot + 2]:
            wait.wait_recv()
        ends = [jnp.transpose(jnp.broadcast_to(low_corners[slot, side, 0:1], (LANES, STATE))) for side in range(2)]
        given_cells = jnp.where(lanes == 0, ends[0], jnp.where(lanes == COLS - 1, ends[1], 0.0))
        field[r] = field[r] + low_halo[slot].astype(F32) + given_cells
    for r in range(ROWS):
        wide[pl.ds(r, STATE, stride=ROWS), :] = field[r]
    grad_inputs[...] = wide[pl.ds(0, width * ROWS), :].reshape(width, ROWS, COLS).astype(BF16)
    grad_hidden[...] = wide[pl.ds(width * ROWS, hid * ROWS), :].reshape(hid, ROWS, COLS).astype(BF16)

    for a, copies5 in fifth_copies:
        for copy, k, sender in reversed(copies5):
            copy.wait_recv()
            forward(a, sender, k)
            pending.append(copy)
    for copy in last_copies:
        copy.wait_recv()
    pending += last_copies
    for copy in pending:
        copy.wait_send()


def finish_kernel(
    hidden_next,
    cell_next,
    grad_inputs,
    grad_hidden,
    grad_cell,
    kernel_low,
    bias_sum,
    hidden_next_out,
    cell_next_out,
    grad_inputs_out,
    grad_hidden_out,
    grad_cell_out,
    kernel_out,
    bias_out,
    kernel_wide,
    sems,
):
    pairs = (
        (hidden_next, hidden_next_out),
        (cell_next, cell_next_out),
        (grad_inputs, grad_inputs_out),
        (grad_hidden, grad_hidden_out),
        (grad_cell, grad_cell_out),
        (bias_sum.at[0:1], bias_out),
    )
    copies = [pltpu.make_async_copy(source, target, sems.at[i]) for i, (source, target) in enumerate(pairs)]
    for copy in copies:
        copy.start()
    for a in range(3):
        taps = pl.ds(3 * a, 3)
        kernel_wide[taps] = kernel_low[taps].astype(F32)
        copy = pltpu.make_async_copy(kernel_wide.at[taps], kernel_out.at[taps], sems.at[len(pairs) + a])
        copy.start()
        copies.append(copy)
    for copy in copies:
        copy.wait()


def shape_of(shape, dtype):
    return jax.ShapeDtypeStruct(shape, dtype)


def body(
    sizes,
    inputs_below,
    hidden_prev,
    cell_prev,
    kernel_weights,
    gate_bias,
    readout,
    target_field,
    land_mask,
    fire_mask,
    hidden_grad,
):
    nx, ny, zh, zl = sizes
    count = {"x": nx, "y": ny, "z": zh * zl}
    hid = hidden_prev.shape[0]
    dma = pltpu.SemaphoreType.DMA
    scaling = 1.0 / math.sqrt(ROWS * nx * zh * 2 * COLS * ny * zl)
    most = max(nx, ny, zh * zl)
    chunk = []
    for axis1, axis2, axis3 in ORDERS:
        rows1 = HALF // count[axis1]
        chunk.append((count[axis1], rows1, count[axis2], rows1 // count[axis2], count[axis3]))
    cells = shape_of((hid, ROWS, COLS), BF16)
    wide_cells = shape_of((hid * ROWS, COLS), F32)
    inputs = (
        inputs_below,
        hidden_prev,
        cell_prev.reshape(hid * ROWS, COLS),
        kernel_weights,
        gate_bias.reshape(1, GATES),
        readout.reshape(1, hid),
        target_field,
        land_mask,
        fire_mask,
        hidden_grad,
    )
    results = pl.pallas_call(
        functools.partial(step_kernel, sizes, scaling),
        out_shape=[
            cells,
            wide_cells,
            cells,
            cells,
            wide_cells,
            shape_of((9, GATES, STATE), BF16),
            shape_of((8, GATES), F32),
        ],
        in_specs=[pl.BlockSpec(memory_space=pltpu.HBM)] * len(inputs),
        out_specs=[VMEM_SPEC] * 7,
        scratch_shapes=[pltpu.VMEM(value.shape, value.dtype) for value in inputs]
        + [
            pltpu.VMEM((STATE * ROWS, COLS), F32),
            pltpu.VMEM((hid * ROWS, COLS), F32),
            pltpu.VMEM((PADDED, STATE, COLS), BF16),
            pltpu.VMEM((2, STATE, COLS), BF16),
            pltpu.VMEM((2, EDGE, STATE), BF16),
            pltpu.VMEM((2, EDGE, STATE), BF16),
            pltpu.VMEM((4, 8, STATE), F32),
            pltpu.VMEM((2, 2, 8, STATE), F32),
            pltpu.VMEM((PADDED, 3 * STATE, COLS), BF16),
            pltpu.VMEM((3, GATES, 3 * STATE), F32),
            pltpu.VMEM((9, STATE, GATES), BF16),
            pltpu.VMEM((ROWS, GATES, COLS), BF16),
            pltpu.VMEM((ROWS, STATE, COLS), F32),
            pltpu.VMEM((4, 8, STATE), F32),
            pltpu.VMEM((2, 2, 8, STATE), F32),
            pltpu.VMEM((2, STATE, COLS), BF16),
            pltpu.VMEM((2, STATE, COLS), BF16),
            pltpu.VMEM((2, EDGE, STATE), BF16),
            pltpu.VMEM((2, EDGE, STATE), BF16),
            pltpu.VMEM((PADDED, 3 * GATES, COLS), BF16),
            pltpu.VMEM((3, 3, HALF, STATE), BF16),
            pltpu.VMEM((3, 3, HALF, STATE), BF16),
            pltpu.VMEM((3, 3, HALF, STATE), F32),
            pltpu.VMEM((3, 3, HALF, STATE), BF16),
            [pltpu.VMEM((n1 - 1, 3, r1, STATE), BF16) for n1, r1, _, _, _ in chunk],
            [pltpu.VMEM((n2, 3, r2, STATE), F32) for _, _, n2, r2, _ in chunk],
            [pltpu.VMEM((n2 - 1, 3, r2, STATE), F32) for _, _, n2, r2, _ in chunk],
            [pltpu.VMEM((n3, 3, r2, STATE), F32) for _, _, _, r2, n3 in chunk],
            [pltpu.VMEM((n2, 3, r2, STATE), BF16) for _, _, n2, r2, _ in chunk],
            [pltpu.VMEM((n, 8, GATES), F32) for n in (2, nx, ny, zh * zl)],
            dma((len(inputs),)),
            dma((2, 2)),
            dma((2, 2)),
            dma((3, 2)),
            dma((3, 2)),
            dma((4,)),
            dma((2, 2)),
            dma((4,)),
            dma((2, 2)),
            dma((7, 3, most)),
            dma((7, 3, most)),
            dma((4, most)),
            dma((4, most)),
        ],
        compiler_params=pltpu.CompilerParams(
            collective_id=0, has_side_effects=True, vmem_limit_bytes=VMEM_LIMIT
        ),
        name="whole_step",
    )(*[pltpu.with_memory_space_constraint(value, pltpu.HBM) for value in inputs])

    hidden_next, cell_next, grad_inputs, grad_hidden, grad_cell, grad_kernel, grad_bias = pl.pallas_call(
        finish_kernel,
        out_shape=[
            cells,
            wide_cells,
            cells,
            cells,
            wide_cells,
            shape_of((9, GATES, STATE), F32),
            shape_of((1, GATES), F32),
        ],
        in_specs=[VMEM_SPEC] * 7,
        out_specs=[pl.BlockSpec(memory_space=pltpu.HBM)] * 7,
        scratch_shapes=[pltpu.VMEM((9, GATES, STATE), F32), dma((9,))],
        compiler_params=pltpu.CompilerParams(vmem_limit_bytes=VMEM_LIMIT),
        name="results",
    )(*results)
    shape = (hid, ROWS, COLS)
    return (
        hidden_next,
        cell_next.reshape(shape),
        grad_inputs,
        grad_hidden,
        grad_cell.reshape(shape),
        grad_kernel,
        grad_bias.reshape(GATES),
    )


def solution(mesh):
    lat, lon = mesh.shape["lat"], mesh.shape["lon"]
    sizes = {(16, 32): (4, 8, 2, 4), (4, 4): (2, 2, 1, 2)}[(lat, lon)]
    cells = P(None, "lat", "lon")
    flat = P("lat", "lon")
    return jax.shard_map(
        functools.partial(body, sizes),
        mesh=mesh,
        in_specs=(cells, cells, cells, P(), P(), P(), flat, flat, flat, cells),
        out_specs=(cells, cells, cells, cells, cells, P(), P()),
        check_vma=False,
    )
```

```python
import functools
import math

import jax
import jax.numpy as jnp
from jax import lax
from jax.experimental import pallas as pl
from jax.experimental.pallas import tpu as pltpu
from jax.sharding import PartitionSpec as P

MESH = pl.DeviceIdType.MESH
F32 = jnp.float32
BF16 = jnp.bfloat16
ROWS = 8
COLS = 128
PADDED = ROWS + 2
STATE = 128
GATES = 256
HALF = GATES // 2
LANES = 128
EDGE = 16
VMEM_SPEC = pl.BlockSpec(memory_space=pltpu.VMEM)
VMEM_LIMIT = 48 * 1024 * 1024


class Place:
    def __init__(self, sizes):
        self.nx, self.ny, self.zh, self.zl = sizes
        self.nz = self.zh * self.zl
        self.nlat = self.nx * self.zh * 2
        self.nlon = self.ny * self.zl
        self.lat = lax.axis_index("lat")
        self.lon = lax.axis_index("lon")
        self.core = lax.rem(self.lat, 2)
        chip = self.lat // 2
        self.z_hi = lax.rem(chip, self.zh)
        self.x = chip // self.zh
        self.z_lo = lax.rem(self.lon, self.zl)
        self.y = self.lon // self.zl
        self.z = self.z_hi * self.zl + self.z_lo
        self.count = {"core": 2, "x": self.nx, "y": self.ny, "z": self.nz}
        self.index = {"core": self.core, "x": self.x, "y": self.y, "z": self.z}
        self.north = self.lat == 0
        self.south = self.lat == self.nlat - 1

    def at(self, x, y, z, core):
        lat = (x * self.zh + z // self.zl) * 2 + core
        lon = y * self.zl + lax.rem(z, self.zl)
        return (lat, lon)

    def peer(self, axis, steps):
        other = lax.rem(self.index[axis] + steps, self.count[axis])
        where = dict(self.index)
        where[axis] = other
        return self.at(where["x"], where["y"], where["z"], where["core"]), other

    def peers(self, axis):
        count = self.count[axis]
        order = sorted(range(1, count), key=lambda steps: min(steps, count - steps))
        return [(steps - 1, *self.peer(axis, steps)) for steps in order]

    def up(self):
        opposite = lax.rem(self.lon + self.nlon // 2, self.nlon)
        lat = jnp.where(self.north, 0, self.lat - 1)
        return (lat, jnp.where(self.north, opposite, self.lon))

    def down(self):
        opposite = lax.rem(self.lon + self.nlon // 2, self.nlon)
        lat = jnp.where(self.south, self.nlat - 1, self.lat + 1)
        return (lat, jnp.where(self.south, opposite, self.lon))

    def east(self):
        return (self.lat, lax.rem(self.lon + 1, self.nlon))

    def west(self):
        return (self.lat, lax.rem(self.lon + self.nlon - 1, self.nlon))

    def around(self):
        return [self.up(), self.down(), self.east(), self.west(), *self.diagonal()]

    def diagonal(self):
        found = []
        for lat, lon in (self.up(), self.down()):
            for steps in (1, self.nlon - 1):
                found.append((lat, lax.rem(lon + steps, self.nlon)))
        return found


def greet(devices):
    barrier = pltpu.get_barrier_semaphore()
    for device in devices:
        pl.semaphore_signal(barrier, inc=1, device_id=device, device_id_type=MESH)
    return barrier


def remote(source, target, send_sem, recv_sem, device):
    return pltpu.make_async_remote_copy(
        src_ref=source,
        dst_ref=target,
        send_sem=send_sem,
        recv_sem=recv_sem,
        device_id=device,
        device_id_type=MESH,
    )


def lane_ids(shape):
    return lax.broadcasted_iota(jnp.int32, shape, len(shape) - 1)


def rows_out(place, first, last, halo, send_sem, recv_sem):
    upper_slot = jnp.where(place.north, 0, 1)
    lower_slot = jnp.where(place.south, 1, 0)
    copies = [
        remote(first, halo.at[upper_slot], send_sem.at[0], recv_sem.at[upper_slot], place.up()),
        remote(last, halo.at[lower_slot], send_sem.at[1], recv_sem.at[lower_slot], place.down()),
    ]
    for copy in copies:
        copy.start()
    waits = [
        remote(first, halo.at[0], send_sem.at[0], recv_sem.at[0], place.up()),
        remote(last, halo.at[1], send_sem.at[1], recv_sem.at[1], place.down()),
    ]
    return copies, waits


def to_edge(total):
    return jnp.transpose(total)[0:EDGE]


def corners_out(place, outgoing, corners, send_sem, recv_sem):
    copies, waits = [], []
    for i, device in enumerate(place.diagonal()):
        slot = jnp.where(place.north, 0, 1) if i < 2 else jnp.where(place.south, 1, 0)
        side = i % 2
        copy = remote(outgoing.at[i], corners.at[slot, side], send_sem.at[i], recv_sem.at[slot, side], device)
        copy.start()
        copies.append(copy)
        waits.append(remote(outgoing.at[i], corners.at[i // 2, side], send_sem.at[i], recv_sem.at[i // 2, side], device))
    return copies, waits


def from_edge(edge):
    rest = jnp.zeros((LANES - EDGE, edge.shape[1]), F32)
    return jnp.transpose(jnp.concatenate([edge.astype(F32), rest], axis=0))


def collect(total, row, position, shift, lanes):
    return jnp.where(lanes == position, pltpu.roll(row, shift % LANES, 1), total)


def cols_out(place, edges, sides, send_sem, recv_sem):
    copies = [
        remote(edges.at[0], sides.at[0], send_sem.at[0], recv_sem.at[0], place.east()),
        remote(edges.at[1], sides.at[1], send_sem.at[1], recv_sem.at[1], place.west()),
    ]
    for copy in copies:
        copy.start()
    return copies


def spread(values, sides_low, sides_high, lanes, position):
    before = jnp.where(lanes == 0, pltpu.roll(sides_low, (-position) % LANES, 1), pltpu.roll(values, 1, 1))
    after = jnp.where(
        lanes == COLS - 1, pltpu.roll(sides_high, (COLS - 1 - position) % LANES, 1), pltpu.roll(values, COLS - 1, 1)
    )
    return before, after


ORDERS = (("y", "x", "z"), ("z", "x", "y"), ("x", "y", "z"))
EARLY = ((1, 2), (3, 4), (5, 6))
LATE = (0, 7)


def step_kernel(
    sizes,
    scaling,
    below_hbm,
    hidden_hbm,
    cell_hbm,
    weights_hbm,
    gate_bias_hbm,
    readout_hbm,
    target_hbm,
    land_hbm,
    fire_hbm,
    hidden_grad_hbm,
    hidden_next,
    cell_next,
    grad_inputs,
    grad_hidden,
    grad_cell,
    kernel_low,
    bias_sum,
    below,
    hidden,
    cell_prev,
    weights,
    gate_bias,
    readout,
    target,
    land,
    fire,
    hidden_grad,
    wide,
    wide_grad,
    rows,
    halo,
    edges,
    sides,
    corner_edges,
    corners,
    windows,
    kernel_acc,
    turned,
    low_rows,
    field,
    low_corner_edges,
    low_corners,
    rims,
    low_halo,
    low_edges,
    low_sides,
    low_windows,
    pair_out,
    pair_in,
    owned,
    first_out,
    first_in,
    second_out,
    second_in,
    third,
    gathered,
    bias_bufs,
    load_sem,
    row_send,
    row_recv,
    col_send,
    col_recv,
    corner_send,
    corner_recv,
    low_corner_send,
    low_corner_recv,
    sends,
    recvs,
    bias_send,
    bias_recv,
):
    place = Place(sizes)
    hid = hidden_next.shape[0]
    width = grad_inputs.shape[0]
    partner, _ = place.peer("core", 1)
    devices = place.around()
    for axis in ("z", "y", "x"):
        devices += [device for _, device, _ in reversed(place.peers(axis))]
    devices.append(partner)
    barrier = greet(devices)
    mine = pl.multiple_of(place.core * HALF, HALF)
    theirs = pl.multiple_of((1 - place.core) * HALF, HALF)
    pending = []

    sources = (below_hbm, hidden_hbm, weights_hbm, cell_hbm, hidden_grad_hbm, gate_bias_hbm, readout_hbm,
               target_hbm, land_hbm, fire_hbm)
    targets = (below, hidden, weights, cell_prev, hidden_grad, gate_bias, readout, target, land, fire)
    loads = [
        pltpu.make_async_copy(source, destination, load_sem.at[i])
        for i, (source, destination) in enumerate(zip(sources, targets))
    ]
    for load in loads:
        load.start()

    loads[0].wait()
    wide[pl.ds(0, width * ROWS), :] = below[...].astype(F32).reshape(width * ROWS, COLS)
    loads[1].wait()
    wide[pl.ds(width * ROWS, hid * ROWS), :] = hidden[...].astype(F32).reshape(hid * ROWS, COLS)

    def state_row(r):
        return wide[pl.ds(r, STATE, stride=ROWS), :]

    for r in (0, ROWS - 1):
        rows[r + 1] = state_row(r).astype(BF16)
    pl.semaphore_wait(barrier, len(devices))
    row_copies, row_waits = rows_out(place, rows.at[1], rows.at[ROWS], halo, row_send.at[0], row_recv.at[0])

    lanes = lane_ids((STATE, COLS))
    east = jnp.zeros((STATE, COLS), F32)
    west = jnp.zeros((STATE, COLS), F32)
    for r in range(ROWS):
        value = state_row(r)
        if 0 < r < ROWS - 1:
            rows[r + 1] = value.astype(BF16)
        east = collect(east, value, r + 1, r + 2, lanes)
        west = collect(west, value, r + 1, r + 1, lanes)
    ends = (to_edge(east), to_edge(west))
    for i in range(4):
        position = 1 if i < 2 else ROWS
        corner_edges[i] = jnp.broadcast_to(ends[i % 2][position : position + 1], (8, STATE))
    corner_copies, corner_waits = corners_out(place, corner_edges, corners, corner_send, corner_recv)
    edges[0] = ends[0].astype(BF16)
    edges[1] = ends[1].astype(BF16)
    col_copies = cols_out(place, edges, sides, col_send.at[0], col_recv.at[0])
    pending += row_copies + col_copies + corner_copies

    for load in loads[2:]:
        load.wait()
    wide_grad[...] = hidden_grad[...].astype(F32).reshape(hid * ROWS, COLS)
    bias_cols = jnp.transpose(jnp.broadcast_to(gate_bias[...], (LANES, GATES)))
    read_cols = jnp.transpose(jnp.broadcast_to(readout[...], (LANES, hid)))
    for t in range(9):
        turned[t] = jnp.transpose(weights[t].astype(F32)).astype(BF16)

    def open_windows(position, low, low_side, high_side):
        before, after = spread(low.astype(F32), low_side, high_side, lanes, position)
        windows[position, 0:STATE] = before.astype(BF16)
        windows[position, STATE : 2 * STATE] = low
        windows[position, 2 * STATE : 3 * STATE] = after.astype(BF16)

    for copy in col_copies:
        copy.wait_recv()
    low_side, high_side = from_edge(sides[0]), from_edge(sides[1])
    for position in range(1, PADDED - 1):
        open_windows(position, rows[position], low_side, high_side)

    flat = jnp.concatenate([weights[t] for t in range(9)], axis=1)

    def cells_of(pair, bias_total):
        columns = jnp.concatenate([windows[r : r + 3].reshape(9 * STATE, COLS) for r in pair], axis=1)
        both = jnp.dot(flat, columns, preferred_element_type=F32)
        for k, r in enumerate(pair):
            preact = both[:, k * COLS : (k + 1) * COLS] + bias_cols
            input_gate = jax.nn.sigmoid(preact[0:hid])
            forget_gate = jax.nn.sigmoid(preact[hid : 2 * hid])
            output_gate = jax.nn.sigmoid(preact[2 * hid : 3 * hid])
            candidate = jnp.tanh(preact[3 * hid : 4 * hid])
            land_row = land[r : r + 1, :].astype(F32)
            fire_row = fire[r : r + 1, :].astype(F32)
            prev = cell_prev[pl.ds(r, hid, stride=ROWS), :]
            cell = land_row * (forget_gate * prev + input_gate * candidate)
            squashed = jnp.tanh(cell)
            new_hidden = (output_gate * squashed).astype(BF16).astype(F32)
            predicted = jnp.sum(read_cols * new_hidden, axis=0, keepdims=True)
            miss = 2.0 * (fire_row * (predicted - target[r : r + 1, :]))
            total_grad = wide_grad[pl.ds(r, hid, stride=ROWS), :] + miss * read_cols
            cell_grad = land_row * total_grad * output_gate * (1.0 - squashed * squashed)
            pre_grad = jnp.concatenate(
                [
                    cell_grad * candidate * input_gate * (1.0 - input_gate),
                    cell_grad * prev * forget_gate * (1.0 - forget_gate),
                    total_grad * squashed * output_gate * (1.0 - output_gate),
                    cell_grad * input_gate * (1.0 - candidate * candidate),
                ],
                axis=0,
            )
            cell_next[pl.ds(r, hid, stride=ROWS), :] = cell
            grad_cell[pl.ds(r, hid, stride=ROWS), :] = cell_grad * forget_gate
            wide[pl.ds(r, hid, stride=ROWS), :] = new_hidden
            bias_total = bias_total + pre_grad
            low_rows[r] = pre_grad.astype(BF16)
        return bias_total

    def kernel_terms(cells, rows_in, a):
        seen = jnp.concatenate([windows[r + a] for r in rows_in], axis=1)
        return lax.dot_general(cells, seen, (((1,), (1,)), ((), ())), preferred_element_type=F32)

    bias_total = jnp.zeros((GATES, COLS), F32)
    for pair in EARLY:
        bias_total = cells_of(pair, bias_total)
    cells = jnp.concatenate([low_rows[r] for r in range(1, ROWS - 1)], axis=1)
    for a in range(3):
        kernel_acc[a] = kernel_terms(cells, range(1, ROWS - 1), a)

    for wait in row_waits + corner_waits:
        wait.wait_recv()
    for slot, position in ((0, 0), (1, PADDED - 1)):
        ends = [jnp.transpose(jnp.broadcast_to(corners[slot, side, 0:1], (LANES, STATE))) for side in range(2)]
        open_windows(position, halo[slot], *ends)
    bias_total = cells_of(LATE, bias_total)

    halves = [pl.ds(theirs, HALF), pl.ds(mine, HALF)]
    cells = jnp.concatenate(
        [jnp.concatenate([low_rows[r, half, :] for r in LATE], axis=1) for half in halves], axis=0
    )
    pair_copies = []
    for a in range(3):
        part = kernel_terms(cells, LATE, a)
        given = part[0:HALF] + kernel_acc[a, halves[0], :]
        kept = part[HALF:] + kernel_acc[a, halves[1], :]
        for b in range(3):
            pair_out[a, b] = given[:, b * STATE : (b + 1) * STATE].astype(BF16)
        copy = remote(pair_out.at[a], pair_in.at[a], sends.at[0, a, 0], recvs.at[0, a, 0], partner)
        copy.start()
        pair_copies.append(copy)
        for b in range(3):
            owned[a, b] = kept[:, b * STATE : (b + 1) * STATE]

    first_copies = []
    for a in range(3):
        pair_copies[a].wait_recv()
        total = owned[a] + pair_in[a].astype(F32)
        owned[a] = total
        first_out[a] = total.astype(BF16)
        axis = ORDERS[a][0]
        rows1 = HALF // place.count[axis]
        copies = []
        for k, device, other in reversed(place.peers(axis)):
            start = pl.multiple_of(other * rows1, rows1)
            copy = remote(
                first_out.at[a, :, pl.ds(start, rows1), :],
                first_in[a].at[k],
                sends.at[1, a, k],
                recvs.at[1, a, k],
                device,
            )
            copy.start()
            copies.append(copy)
        first_copies.append(copies)
    pending += pair_copies

    def bias_start(stage, axis, value):
        slot = place.index[axis]
        buf = bias_bufs[stage]
        buf[slot] = value
        copies = []
        for k, device, _ in place.peers(axis):
            copy = remote(buf.at[slot], buf.at[slot], bias_send.at[stage, k], bias_recv.at[stage, k], device)
            copy.start()
            copies.append(copy)
        return copies

    def bias_finish(stage, axis, copies):
        buf = bias_bufs[stage]
        for copy in copies:
            copy.wait_recv()
        pending.extend(copies)
        total = buf[0]
        for k in range(1, place.count[axis]):
            total = total + buf[k]
        return total

    bias = lax.dot_general(
        jnp.ones((8, COLS), F32),
        bias_total,
        (((1,), (1,)), ((), ())),
        precision=lax.Precision.HIGHEST,
        preferred_element_type=F32,
    )
    bias_copies = bias_start(0, "core", bias)

    gate_lanes = lane_ids((GATES, COLS))
    east = jnp.zeros((GATES, COLS), F32)
    west = jnp.zeros((GATES, COLS), F32)
    for r in range(ROWS):
        value = low_rows[r].astype(F32)
        before = jnp.where(gate_lanes == 0, 0.0, pltpu.roll(value, 1, 1))
        after = jnp.where(gate_lanes == COLS - 1, 0.0, pltpu.roll(value, COLS - 1, 1))
        low_windows[r + 1, 0:GATES] = before.astype(BF16)
        low_windows[r + 1, GATES : 2 * GATES] = low_rows[r]
        low_windows[r + 1, 2 * GATES : 3 * GATES] = after.astype(BF16)
        east = collect(east, value, r + 1, r + 2, gate_lanes)
        west = collect(west, value, r + 1, r + 1, gate_lanes)
    for slot, (value, last) in enumerate(((east, 2), (west, 0))):
        shifts = jnp.concatenate([pltpu.roll(value, a % LANES, 1).astype(BF16) for a in (-1, 0, 1)], axis=0)
        taps = jnp.concatenate([turned[3 * a + last] for a in range(3)], axis=1)
        given_cells = to_edge(jnp.dot(taps, shifts, preferred_element_type=F32))
        low_edges[slot] = given_cells.astype(BF16)
        for i, position in ((slot, 0), (slot + 2, PADDED - 1)):
            low_corner_edges[i] = jnp.broadcast_to(given_cells[position : position + 1], (8, STATE))
    low_copies = cols_out(place, low_edges, low_sides, col_send.at[2], col_recv.at[2])
    low_corner_copies, low_corner_waits = corners_out(
        place, low_corner_edges, low_corners, low_corner_send, low_corner_recv
    )

    flipped = jnp.concatenate([turned[8 - q] for q in range(9)], axis=1)
    rims[0] = jnp.dot(flipped[:, 6 * GATES :], low_windows[1], preferred_element_type=F32).astype(BF16)
    rims[1] = jnp.dot(flipped[:, : 3 * GATES], low_windows[ROWS], preferred_element_type=F32).astype(BF16)
    row_copies, row_waits = rows_out(place, rims.at[0], rims.at[1], low_halo, row_send.at[1], row_recv.at[1])
    bias = bias_finish(0, "core", bias_copies)
    bias_copies = bias_start(1, "x", bias)

    second_copies = []

    def second_start(a):
        axis1, axis2, _ = ORDERS[a]
        n1, n2 = place.count[axis1], place.count[axis2]
        rows1 = HALF // n1
        rows2 = rows1 // n2
        for copy in reversed(first_copies[a]):
            copy.wait_recv()
        pending.extend(first_copies[a])
        start = pl.multiple_of(place.index[axis1] * rows1, rows1)
        total = owned[a, :, pl.ds(start, rows1), :]
        for k in range(n1 - 1):
            total = total + first_in[a][k].astype(F32)
        for p in range(n2):
            second_out[a][p] = total[:, p * rows2 : (p + 1) * rows2, :]
        copies = []
        for k, device, other in reversed(place.peers(axis2)):
            copy = remote(second_out[a].at[other], second_in[a].at[k], sends.at[2, a, k], recvs.at[2, a, k], device)
            copy.start()
            copies.append(copy)
        second_copies.append((a, copies))

    second_start(2)
    second_start(0)
    second_start(1)

    bias = bias_finish(1, "x", bias_copies)
    bias_copies = bias_start(2, "y", bias)

    third_copies = []
    for a, copies2 in sorted(second_copies, key=lambda entry: entry[0]):
        _, axis2, axis3 = ORDERS[a]
        for copy in reversed(copies2):
            copy.wait_recv()
        pending += copies2
        total = second_out[a][place.index[axis2]]
        for k in range(place.count[axis2] - 1):
            total = total + second_in[a][k]
        slot = place.index[axis3]
        third[a][slot] = total
        copies = []
        for k, device, _ in reversed(place.peers(axis3)):
            copy = remote(third[a].at[slot], third[a].at[slot], sends.at[3, a, k], recvs.at[3, a, k], device)
            copy.start()
            copies.append(copy)
        third_copies.append((a, copies))

    hidden_next[...] = wide[pl.ds(0, hid * ROWS), :].reshape(hid, ROWS, COLS).astype(BF16)
    low_windows[0] = jnp.zeros((3 * GATES, COLS), BF16)
    low_windows[PADDED - 1] = jnp.zeros((3 * GATES, COLS), BF16)
    for pair in range(ROWS // 2):
        blocks = [low_windows[r : r + 3].reshape(9 * GATES, COLS) for r in (2 * pair, 2 * pair + 1)]
        both = jnp.dot(flipped, jnp.concatenate(blocks, axis=1), preferred_element_type=F32)
        for k in range(2):
            field[2 * pair + k] = both[:, k * COLS : (k + 1) * COLS]
    for copy in low_copies:
        copy.wait_recv()
    low_side, high_side = from_edge(low_sides[0]), from_edge(low_sides[1])

    def arrived(low_side, high_side, position):
        first = jnp.where(lanes == 0, pltpu.roll(low_side, (-position) % LANES, 1), 0.0)
        last = jnp.where(lanes == COLS - 1, pltpu.roll(high_side, (COLS - 1 - position) % LANES, 1), 0.0)
        return first + last

    pending += low_copies + row_copies + low_corner_copies
    for r in range(ROWS):
        field[r] = field[r] + arrived(low_side, high_side, r + 1)
    bias = bias_finish(2, "y", bias_copies)
    bias_copies = bias_start(3, "z", bias)

    fourth_copies = []
    for a, copies3 in third_copies:
        _, axis2, axis3 = ORDERS[a]
        for copy in reversed(copies3):
            copy.wait_recv()
        pending += copies3
        total = third[a][0]
        for k in range(1, place.count[axis3]):
            total = total + third[a][k]
        slot = place.index[axis2]
        gathered[a][slot] = (total * scaling).astype(BF16)
        copies = []
        for k, device, _ in reversed(place.peers(axis2)):
            copy = remote(gathered[a].at[slot], gathered[a].at[slot], sends.at[4, a, k], recvs.at[4, a, k], device)
            copy.start()
            copies.append(copy)
        fourth_copies.append((a, copies))

    def block_of(a, owner):
        rows1 = HALF // place.count[ORDERS[a][0]]
        start = pl.multiple_of(mine + owner * rows1, rows1)
        return kernel_low.at[pl.ds(3 * a, 3), pl.ds(start, rows1), :]

    last_copies = []

    def forward(a, owner, slot):
        block = block_of(a, owner)
        copy = remote(block, block, sends.at[6, a, slot], recvs.at[6, a, slot], partner)
        copy.start()
        last_copies.append(copy)

    fifth_copies = []
    for a, copies4 in fourth_copies:
        axis1, axis2, _ = ORDERS[a]
        n1 = place.count[axis1]
        for copy in reversed(copies4):
            copy.wait_recv()
        pending += copies4
        block = block_of(a, place.index[axis1])
        block[...] = jnp.concatenate(
            [gathered[a][p].astype(F32) for p in range(place.count[axis2])], axis=1
        ).astype(BF16)
        copies = []
        for k, device, _ in reversed(place.peers(axis1)):
            copy = remote(block, block, sends.at[5, a, k], recvs.at[5, a, k], device)
            copy.start()
            copies.append((copy, k, lax.rem(place.index[axis1] + n1 - 1 - k, n1)))
        forward(a, place.index[axis1], n1 - 1)
        fifth_copies.append((a, copies))

    for slot, r in ((0, 0), (1, ROWS - 1)):
        row_waits[slot].wait_recv()
        for wait in low_corner_waits[2 * slot : 2 * slot + 2]:
            wait.wait_recv()
        ends = [jnp.transpose(jnp.broadcast_to(low_corners[slot, side, 0:1], (LANES, STATE))) for side in range(2)]
        given_cells = jnp.where(lanes == 0, ends[0], jnp.where(lanes == COLS - 1, ends[1], 0.0))
        field[r] = field[r] + low_halo[slot].astype(F32) + given_cells
    for r in range(ROWS):
        wide[pl.ds(r, STATE, stride=ROWS), :] = field[r]
    grad_inputs[...] = wide[pl.ds(0, width * ROWS), :].reshape(width, ROWS, COLS).astype(BF16)
    grad_hidden[...] = wide[pl.ds(width * ROWS, hid * ROWS), :].reshape(hid, ROWS, COLS).astype(BF16)

    for a, copies5 in fifth_copies:
        for copy, k, sender in reversed(copies5):
            copy.wait_recv()
            forward(a, sender, k)
            pending.append(copy)
    bias_sum[...] = bias_finish(3, "z", bias_copies) * scaling
    for copy in last_copies:
        copy.wait_recv()
    pending += last_copies
    for copy in pending:
        copy.wait_send()


def finish_kernel(
    hidden_next,
    cell_next,
    grad_inputs,
    grad_hidden,
    grad_cell,
    kernel_low,
    bias_sum,
    hidden_next_out,
    cell_next_out,
    grad_inputs_out,
    grad_hidden_out,
    grad_cell_out,
    kernel_out,
    bias_out,
    kernel_wide,
    sems,
):
    pairs = (
        (hidden_next, hidden_next_out),
        (cell_next, cell_next_out),
        (grad_inputs, grad_inputs_out),
        (grad_hidden, grad_hidden_out),
        (grad_cell, grad_cell_out),
        (bias_sum.at[0:1], bias_out),
    )
    copies = [pltpu.make_async_copy(source, target, sems.at[i]) for i, (source, target) in enumerate(pairs)]
    for copy in copies:
        copy.start()
    for a in range(3):
        taps = pl.ds(3 * a, 3)
        kernel_wide[taps] = kernel_low[taps].astype(F32)
        copy = pltpu.make_async_copy(kernel_wide.at[taps], kernel_out.at[taps], sems.at[len(pairs) + a])
        copy.start()
        copies.append(copy)
    for copy in copies:
        copy.wait()


def shape_of(shape, dtype):
    return jax.ShapeDtypeStruct(shape, dtype)


def body(
    sizes,
    inputs_below,
    hidden_prev,
    cell_prev,
    kernel_weights,
    gate_bias,
    readout,
    target_field,
    land_mask,
    fire_mask,
    hidden_grad,
):
    nx, ny, zh, zl = sizes
    count = {"x": nx, "y": ny, "z": zh * zl}
    hid = hidden_prev.shape[0]
    dma = pltpu.SemaphoreType.DMA
    scaling = 1.0 / math.sqrt(ROWS * nx * zh * 2 * COLS * ny * zl)
    most = max(nx, ny, zh * zl)
    chunk = []
    for axis1, axis2, axis3 in ORDERS:
        rows1 = HALF // count[axis1]
        chunk.append((count[axis1], rows1, count[axis2], rows1 // count[axis2], count[axis3]))
    cells = shape_of((hid, ROWS, COLS), BF16)
    wide_cells = shape_of((hid * ROWS, COLS), F32)
    inputs = (
        inputs_below,
        hidden_prev,
        cell_prev.reshape(hid * ROWS, COLS),
        kernel_weights,
        gate_bias.reshape(1, GATES),
        readout.reshape(1, hid),
        target_field,
        land_mask,
        fire_mask,
        hidden_grad,
    )
    results = pl.pallas_call(
        functools.partial(step_kernel, sizes, scaling),
        out_shape=[
            cells,
            wide_cells,
            cells,
            cells,
            wide_cells,
            shape_of((9, GATES, STATE), BF16),
            shape_of((8, GATES), F32),
        ],
        in_specs=[pl.BlockSpec(memory_space=pltpu.HBM)] * len(inputs),
        out_specs=[VMEM_SPEC] * 7,
        scratch_shapes=[pltpu.VMEM(value.shape, value.dtype) for value in inputs]
        + [
            pltpu.VMEM((STATE * ROWS, COLS), F32),
            pltpu.VMEM((hid * ROWS, COLS), F32),
            pltpu.VMEM((PADDED, STATE, COLS), BF16),
            pltpu.VMEM((2, STATE, COLS), BF16),
            pltpu.VMEM((2, EDGE, STATE), BF16),
            pltpu.VMEM((2, EDGE, STATE), BF16),
            pltpu.VMEM((4, 8, STATE), F32),
            pltpu.VMEM((2, 2, 8, STATE), F32),
            pltpu.VMEM((PADDED, 3 * STATE, COLS), BF16),
            pltpu.VMEM((3, GATES, 3 * STATE), F32),
            pltpu.VMEM((9, STATE, GATES), BF16),
            pltpu.VMEM((ROWS, GATES, COLS), BF16),
            pltpu.VMEM((ROWS, STATE, COLS), F32),
            pltpu.VMEM((4, 8, STATE), F32),
            pltpu.VMEM((2, 2, 8, STATE), F32),
            pltpu.VMEM((2, STATE, COLS), BF16),
            pltpu.VMEM((2, STATE, COLS), BF16),
            pltpu.VMEM((2, EDGE, STATE), BF16),
            pltpu.VMEM((2, EDGE, STATE), BF16),
            pltpu.VMEM((PADDED, 3 * GATES, COLS), BF16),
            pltpu.VMEM((3, 3, HALF, STATE), BF16),
            pltpu.VMEM((3, 3, HALF, STATE), BF16),
            pltpu.VMEM((3, 3, HALF, STATE), F32),
            pltpu.VMEM((3, 3, HALF, STATE), BF16),
            [pltpu.VMEM((n1 - 1, 3, r1, STATE), BF16) for n1, r1, _, _, _ in chunk],
            [pltpu.VMEM((n2, 3, r2, STATE), F32) for _, _, n2, r2, _ in chunk],
            [pltpu.VMEM((n2 - 1, 3, r2, STATE), F32) for _, _, n2, r2, _ in chunk],
            [pltpu.VMEM((n3, 3, r2, STATE), F32) for _, _, _, r2, n3 in chunk],
            [pltpu.VMEM((n2, 3, r2, STATE), BF16) for _, _, n2, r2, _ in chunk],
            [pltpu.VMEM((n, 8, GATES), F32) for n in (2, nx, ny, zh * zl)],
            dma((len(inputs),)),
            dma((2, 2)),
            dma((2, 2)),
            dma((3, 2)),
            dma((3, 2)),
            dma((4,)),
            dma((2, 2)),
            dma((4,)),
            dma((2, 2)),
            dma((7, 3, most)),
            dma((7, 3, most)),
            dma((4, most)),
            dma((4, most)),
        ],
        compiler_params=pltpu.CompilerParams(
            collective_id=0, has_side_effects=True, vmem_limit_bytes=VMEM_LIMIT
        ),
        name="whole_step",
    )(*[pltpu.with_memory_space_constraint(value, pltpu.HBM) for value in inputs])

    hidden_next, cell_next, grad_inputs, grad_hidden, grad_cell, grad_kernel, grad_bias = pl.pallas_call(
        finish_kernel,
        out_shape=[
            cells,
            wide_cells,
            cells,
            cells,
            wide_cells,
            shape_of((9, GATES, STATE), F32),
            shape_of((1, GATES), F32),
        ],
        in_specs=[VMEM_SPEC] * 7,
        out_specs=[pl.BlockSpec(memory_space=pltpu.HBM)] * 7,
        scratch_shapes=[pltpu.VMEM((9, GATES, STATE), F32), dma((9,))],
        compiler_params=pltpu.CompilerParams(vmem_limit_bytes=VMEM_LIMIT),
        name="results",
    )(*results)
    shape = (hid, ROWS, COLS)
    return (
        hidden_next,
        cell_next.reshape(shape),
        grad_inputs,
        grad_hidden,
        grad_cell.reshape(shape),
        grad_kernel,
        grad_bias.reshape(GATES),
    )


def solution(mesh):
    lat, lon = mesh.shape["lat"], mesh.shape["lon"]
    sizes = {(16, 32): (4, 8, 2, 4), (4, 4): (2, 2, 1, 2)}[(lat, lon)]
    cells = P(None, "lat", "lon")
    flat = P("lat", "lon")
    return jax.shard_map(
        functools.partial(body, sizes),
        mesh=mesh,
        in_specs=(cells, cells, cells, P(), P(), P(), flat, flat, flat, cells),
        out_specs=(cells, cells, cells, cells, cells, P(), P()),
        check_vma=False,
    )
```

```python
import functools
import math

import jax
import jax.numpy as jnp
from jax import lax
from jax.experimental import pallas as pl
from jax.experimental.pallas import tpu as pltpu
from jax.sharding import PartitionSpec as P

MESH = pl.DeviceIdType.MESH
F32 = jnp.float32
BF16 = jnp.bfloat16
ROWS = 8
COLS = 128
PADDED = ROWS + 2
STATE = 128
GATES = 256
HALF = GATES // 2
LANES = 128
EDGE = 16
VMEM_SPEC = pl.BlockSpec(memory_space=pltpu.VMEM)
VMEM_LIMIT = 48 * 1024 * 1024


class Place:
    def __init__(self, sizes):
        self.nx, self.ny, self.zh, self.zl = sizes
        self.nz = self.zh * self.zl
        self.nlat = self.nx * self.zh * 2
        self.nlon = self.ny * self.zl
        self.lat = lax.axis_index("lat")
        self.lon = lax.axis_index("lon")
        self.core = lax.rem(self.lat, 2)
        chip = self.lat // 2
        self.z_hi = lax.rem(chip, self.zh)
        self.x = chip // self.zh
        self.z_lo = lax.rem(self.lon, self.zl)
        self.y = self.lon // self.zl
        self.z = self.z_hi * self.zl + self.z_lo
        self.count = {"core": 2, "x": self.nx, "y": self.ny, "z": self.nz}
        self.index = {"core": self.core, "x": self.x, "y": self.y, "z": self.z}
        self.north = self.lat == 0
        self.south = self.lat == self.nlat - 1

    def at(self, x, y, z, core):
        lat = (x * self.zh + z // self.zl) * 2 + core
        lon = y * self.zl + lax.rem(z, self.zl)
        return (lat, lon)

    def peer(self, axis, steps):
        other = lax.rem(self.index[axis] + steps, self.count[axis])
        where = dict(self.index)
        where[axis] = other
        return self.at(where["x"], where["y"], where["z"], where["core"]), other

    def peers(self, axis):
        count = self.count[axis]
        order = sorted(range(1, count), key=lambda steps: min(steps, count - steps))
        return [(steps - 1, *self.peer(axis, steps)) for steps in order]

    def up(self):
        opposite = lax.rem(self.lon + self.nlon // 2, self.nlon)
        lat = jnp.where(self.north, 0, self.lat - 1)
        return (lat, jnp.where(self.north, opposite, self.lon))

    def down(self):
        opposite = lax.rem(self.lon + self.nlon // 2, self.nlon)
        lat = jnp.where(self.south, self.nlat - 1, self.lat + 1)
        return (lat, jnp.where(self.south, opposite, self.lon))

    def east(self):
        return (self.lat, lax.rem(self.lon + 1, self.nlon))

    def west(self):
        return (self.lat, lax.rem(self.lon + self.nlon - 1, self.nlon))

    def around(self):
        return [self.up(), self.down(), self.east(), self.west(), *self.diagonal()]

    def diagonal(self):
        found = []
        for lat, lon in (self.up(), self.down()):
            for steps in (1, self.nlon - 1):
                found.append((lat, lax.rem(lon + steps, self.nlon)))
        return found


def greet(devices):
    barrier = pltpu.get_barrier_semaphore()
    for device in devices:
        pl.semaphore_signal(barrier, inc=1, device_id=device, device_id_type=MESH)
    return barrier


def remote(source, target, send_sem, recv_sem, device):
    return pltpu.make_async_remote_copy(
        src_ref=source,
        dst_ref=target,
        send_sem=send_sem,
        recv_sem=recv_sem,
        device_id=device,
        device_id_type=MESH,
    )


def lane_ids(shape):
    return lax.broadcasted_iota(jnp.int32, shape, len(shape) - 1)


def rows_out(place, first, last, halo, send_sem, recv_sem):
    upper_slot = jnp.where(place.north, 0, 1)
    lower_slot = jnp.where(place.south, 1, 0)
    copies = [
        remote(first, halo.at[upper_slot], send_sem.at[0], recv_sem.at[upper_slot], place.up()),
        remote(last, halo.at[lower_slot], send_sem.at[1], recv_sem.at[lower_slot], place.down()),
    ]
    for copy in copies:
        copy.start()
    waits = [
        remote(first, halo.at[0], send_sem.at[0], recv_sem.at[0], place.up()),
        remote(last, halo.at[1], send_sem.at[1], recv_sem.at[1], place.down()),
    ]
    return copies, waits


def to_edge(total):
    return jnp.transpose(total)[0:EDGE]


def corners_out(place, outgoing, corners, send_sem, recv_sem):
    copies, waits = [], []
    for i, device in enumerate(place.diagonal()):
        slot = jnp.where(place.north, 0, 1) if i < 2 else jnp.where(place.south, 1, 0)
        side = i % 2
        copy = remote(outgoing.at[i], corners.at[slot, side], send_sem.at[i], recv_sem.at[slot, side], device)
        copy.start()
        copies.append(copy)
        waits.append(remote(outgoing.at[i], corners.at[i // 2, side], send_sem.at[i], recv_sem.at[i // 2, side], device))
    return copies, waits


def from_edge(edge):
    rest = jnp.zeros((LANES - EDGE, edge.shape[1]), F32)
    return jnp.transpose(jnp.concatenate([edge.astype(F32), rest], axis=0))


def collect(total, row, position, shift, lanes):
    return jnp.where(lanes == position, pltpu.roll(row, shift % LANES, 1), total)


def cols_out(place, edges, sides, send_sem, recv_sem):
    copies = [
        remote(edges.at[0], sides.at[0], send_sem.at[0], recv_sem.at[0], place.east()),
        remote(edges.at[1], sides.at[1], send_sem.at[1], recv_sem.at[1], place.west()),
    ]
    for copy in copies:
        copy.start()
    return copies


def spread(values, sides_low, sides_high, lanes, position):
    before = jnp.where(lanes == 0, pltpu.roll(sides_low, (-position) % LANES, 1), pltpu.roll(values, 1, 1))
    after = jnp.where(
        lanes == COLS - 1, pltpu.roll(sides_high, (COLS - 1 - position) % LANES, 1), pltpu.roll(values, COLS - 1, 1)
    )
    return before, after


ORDERS = (("y", "x", "z"), ("z", "x", "y"), ("x", "y", "z"))
EARLY = ((1, 2), (3, 4), (5, 6))
LATE = (0, 7)


def step_kernel(
    sizes,
    scaling,
    below_hbm,
    hidden_hbm,
    cell_hbm,
    weights_hbm,
    gate_bias_hbm,
    readout_hbm,
    target_hbm,
    land_hbm,
    fire_hbm,
    hidden_grad_hbm,
    hidden_next,
    cell_next,
    grad_inputs,
    grad_hidden,
    grad_cell,
    kernel_low,
    bias_sum,
    below,
    hidden,
    cell_prev,
    weights,
    gate_bias,
    readout,
    target,
    land,
    fire,
    hidden_grad,
    wide,
    wide_grad,
    rows,
    halo,
    edges,
    sides,
    corner_edges,
    corners,
    windows,
    kernel_acc,
    turned,
    low_rows,
    field,
    low_corner_edges,
    low_corners,
    rims,
    low_halo,
    low_edges,
    low_sides,
    low_windows,
    pair_out,
    pair_in,
    owned,
    first_out,
    first_in,
    second_out,
    second_in,
    third,
    gathered,
    bias_bufs,
    load_sem,
    row_send,
    row_recv,
    col_send,
    col_recv,
    corner_send,
    corner_recv,
    low_corner_send,
    low_corner_recv,
    sends,
    recvs,
    bias_send,
    bias_recv,
):
    place = Place(sizes)
    hid = hidden_next.shape[0]
    width = grad_inputs.shape[0]
    partner, _ = place.peer("core", 1)
    devices = place.around()
    for axis in ("z", "y", "x"):
        devices += [device for _, device, _ in reversed(place.peers(axis))]
    devices.append(partner)
    barrier = greet(devices)
    mine = pl.multiple_of(place.core * HALF, HALF)
    theirs = pl.multiple_of((1 - place.core) * HALF, HALF)
    pending = []

    sources = (below_hbm, hidden_hbm, weights_hbm, cell_hbm, hidden_grad_hbm, gate_bias_hbm, readout_hbm,
               target_hbm, land_hbm, fire_hbm)
    targets = (below, hidden, weights, cell_prev, hidden_grad, gate_bias, readout, target, land, fire)
    loads = [
        pltpu.make_async_copy(source, destination, load_sem.at[i])
        for i, (source, destination) in enumerate(zip(sources, targets))
    ]
    for load in loads:
        load.start()

    loads[0].wait()
    wide[pl.ds(0, width * ROWS), :] = below[...].astype(F32).reshape(width * ROWS, COLS)
    loads[1].wait()
    wide[pl.ds(width * ROWS, hid * ROWS), :] = hidden[...].astype(F32).reshape(hid * ROWS, COLS)

    def state_row(r):
        return wide[pl.ds(r, STATE, stride=ROWS), :]

    for r in (0, ROWS - 1):
        rows[r + 1] = state_row(r).astype(BF16)
    pl.semaphore_wait(barrier, len(devices))
    row_copies, row_waits = rows_out(place, rows.at[1], rows.at[ROWS], halo, row_send.at[0], row_recv.at[0])

    lanes = lane_ids((STATE, COLS))
    east = jnp.zeros((STATE, COLS), F32)
    west = jnp.zeros((STATE, COLS), F32)
    for r in range(ROWS):
        value = state_row(r)
        if 0 < r < ROWS - 1:
            rows[r + 1] = value.astype(BF16)
        east = collect(east, value, r + 1, r + 2, lanes)
        west = collect(west, value, r + 1, r + 1, lanes)
    ends = (to_edge(east), to_edge(west))
    for i in range(4):
        position = 1 if i < 2 else ROWS
        corner_edges[i] = jnp.broadcast_to(ends[i % 2][position : position + 1], (8, STATE))
    corner_copies, corner_waits = corners_out(place, corner_edges, corners, corner_send, corner_recv)
    edges[0] = ends[0].astype(BF16)
    edges[1] = ends[1].astype(BF16)
    col_copies = cols_out(place, edges, sides, col_send.at[0], col_recv.at[0])
    pending += row_copies + col_copies + corner_copies

    for load in loads[2:]:
        load.wait()
    wide_grad[...] = hidden_grad[...].astype(F32).reshape(hid * ROWS, COLS)
    bias_cols = jnp.transpose(jnp.broadcast_to(gate_bias[...], (LANES, GATES)))
    read_cols = jnp.transpose(jnp.broadcast_to(readout[...], (LANES, hid)))
    for t in range(9):
        turned[t] = jnp.transpose(weights[t].astype(F32)).astype(BF16)

    def open_windows(position, low, low_side, high_side):
        before, after = spread(low.astype(F32), low_side, high_side, lanes, position)
        windows[position, 0:STATE] = before.astype(BF16)
        windows[position, STATE : 2 * STATE] = low
        windows[position, 2 * STATE : 3 * STATE] = after.astype(BF16)

    for copy in col_copies:
        copy.wait_recv()
    low_side, high_side = from_edge(sides[0]), from_edge(sides[1])
    for position in range(1, PADDED - 1):
        open_windows(position, rows[position], low_side, high_side)

    flat = jnp.concatenate([weights[t] for t in range(9)], axis=1)

    def cells_of(pair, bias_total):
        columns = jnp.concatenate([windows[r : r + 3].reshape(9 * STATE, COLS) for r in pair], axis=1)
        both = jnp.dot(flat, columns, preferred_element_type=F32)
        for k, r in enumerate(pair):
            preact = both[:, k * COLS : (k + 1) * COLS] + bias_cols
            input_gate = jax.nn.sigmoid(preact[0:hid])
            forget_gate = jax.nn.sigmoid(preact[hid : 2 * hid])
            output_gate = jax.nn.sigmoid(preact[2 * hid : 3 * hid])
            candidate = jnp.tanh(preact[3 * hid : 4 * hid])
            land_row = land[r : r + 1, :].astype(F32)
            fire_row = fire[r : r + 1, :].astype(F32)
            prev = cell_prev[pl.ds(r, hid, stride=ROWS), :]
            cell = land_row * (forget_gate * prev + input_gate * candidate)
            squashed = jnp.tanh(cell)
            new_hidden = (output_gate * squashed).astype(BF16).astype(F32)
            predicted = jnp.sum(read_cols * new_hidden, axis=0, keepdims=True)
            miss = 2.0 * (fire_row * (predicted - target[r : r + 1, :]))
            total_grad = wide_grad[pl.ds(r, hid, stride=ROWS), :] + miss * read_cols
            cell_grad = land_row * total_grad * output_gate * (1.0 - squashed * squashed)
            pre_grad = jnp.concatenate(
                [
                    cell_grad * candidate * input_gate * (1.0 - input_gate),
                    cell_grad * prev * forget_gate * (1.0 - forget_gate),
                    total_grad * squashed * output_gate * (1.0 - output_gate),
                    cell_grad * input_gate * (1.0 - candidate * candidate),
                ],
                axis=0,
            )
            cell_next[pl.ds(r, hid, stride=ROWS), :] = cell
            grad_cell[pl.ds(r, hid, stride=ROWS), :] = cell_grad * forget_gate
            wide[pl.ds(r, hid, stride=ROWS), :] = new_hidden
            bias_total = bias_total + pre_grad
            low_rows[r] = pre_grad.astype(BF16)
        return bias_total

    def kernel_terms(cells, rows_in, a):
        seen = jnp.concatenate([windows[r + a] for r in rows_in], axis=1)
        return lax.dot_general(cells, seen, (((1,), (1,)), ((), ())), preferred_element_type=F32)

    bias_total = jnp.zeros((GATES, COLS), F32)
    for pair in EARLY:
        bias_total = cells_of(pair, bias_total)
    cells = jnp.concatenate([low_rows[r] for r in range(1, ROWS - 1)], axis=1)
    for a in range(3):
        kernel_acc[a] = kernel_terms(cells, range(1, ROWS - 1), a)

    for wait in row_waits + corner_waits:
        wait.wait_recv()
    for slot, position in ((0, 0), (1, PADDED - 1)):
        ends = [jnp.transpose(jnp.broadcast_to(corners[slot, side, 0:1], (LANES, STATE))) for side in range(2)]
        open_windows(position, halo[slot], *ends)
    bias_total = cells_of(LATE, bias_total)

    halves = [pl.ds(theirs, HALF), pl.ds(mine, HALF)]
    cells = jnp.concatenate(
        [jnp.concatenate([low_rows[r, half, :] for r in LATE], axis=1) for half in halves], axis=0
    )
    pair_copies = []
    for a in range(3):
        part = kernel_terms(cells, LATE, a)
        given = part[0:HALF] + kernel_acc[a, halves[0], :]
        kept = part[HALF:] + kernel_acc[a, halves[1], :]
        for b in range(3):
            pair_out[a, b] = given[:, b * STATE : (b + 1) * STATE].astype(BF16)
        copy = remote(pair_out.at[a], pair_in.at[a], sends.at[0, a, 0], recvs.at[0, a, 0], partner)
        copy.start()
        pair_copies.append(copy)
        for b in range(3):
            owned[a, b] = kept[:, b * STATE : (b + 1) * STATE]

    first_copies = []
    for a in range(3):
        pair_copies[a].wait_recv()
        total = owned[a] + pair_in[a].astype(F32)
        owned[a] = total
        first_out[a] = total.astype(BF16)
        axis = ORDERS[a][0]
        rows1 = HALF // place.count[axis]
        copies = []
        for k, device, other in reversed(place.peers(axis)):
            start = pl.multiple_of(other * rows1, rows1)
            copy = remote(
                first_out.at[a, :, pl.ds(start, rows1), :],
                first_in[a].at[k],
                sends.at[1, a, k],
                recvs.at[1, a, k],
                device,
            )
            copy.start()
            copies.append(copy)
        first_copies.append(copies)
    pending += pair_copies

    def bias_start(stage, axis, value):
        slot = place.index[axis]
        buf = bias_bufs[stage]
        buf[slot] = value
        copies = []
        for k, device, _ in place.peers(axis):
            copy = remote(buf.at[slot], buf.at[slot], bias_send.at[stage, k], bias_recv.at[stage, k], device)
            copy.start()
            copies.append(copy)
        return copies

    def bias_finish(stage, axis, copies):
        buf = bias_bufs[stage]
        for copy in copies:
            copy.wait_recv()
        pending.extend(copies)
        total = buf[0]
        for k in range(1, place.count[axis]):
            total = total + buf[k]
        return total

    bias = lax.dot_general(
        jnp.ones((8, COLS), F32),
        bias_total,
        (((1,), (1,)), ((), ())),
        precision=lax.Precision.HIGHEST,
        preferred_element_type=F32,
    )
    bias_copies = bias_start(0, "core", bias)

    gate_lanes = lane_ids((GATES, COLS))
    east = jnp.zeros((GATES, COLS), F32)
    west = jnp.zeros((GATES, COLS), F32)
    for r in range(ROWS):
        value = low_rows[r].astype(F32)
        before = jnp.where(gate_lanes == 0, 0.0, pltpu.roll(value, 1, 1))
        after = jnp.where(gate_lanes == COLS - 1, 0.0, pltpu.roll(value, COLS - 1, 1))
        low_windows[r + 1, 0:GATES] = before.astype(BF16)
        low_windows[r + 1, GATES : 2 * GATES] = low_rows[r]
        low_windows[r + 1, 2 * GATES : 3 * GATES] = after.astype(BF16)
        east = collect(east, value, r + 1, r + 2, gate_lanes)
        west = collect(west, value, r + 1, r + 1, gate_lanes)
    for slot, (value, last) in enumerate(((east, 2), (west, 0))):
        shifts = jnp.concatenate([pltpu.roll(value, a % LANES, 1).astype(BF16) for a in (-1, 0, 1)], axis=0)
        taps = jnp.concatenate([turned[3 * a + last] for a in range(3)], axis=1)
        given_cells = to_edge(jnp.dot(taps, shifts, preferred_element_type=F32))
        low_edges[slot] = given_cells.astype(BF16)
        for i, position in ((slot, 0), (slot + 2, PADDED - 1)):
            low_corner_edges[i] = jnp.broadcast_to(given_cells[position : position + 1], (8, STATE))
    low_copies = cols_out(place, low_edges, low_sides, col_send.at[2], col_recv.at[2])
    low_corner_copies, low_corner_waits = corners_out(
        place, low_corner_edges, low_corners, low_corner_send, low_corner_recv
    )

    flipped = jnp.concatenate([turned[8 - q] for q in range(9)], axis=1)
    rims[0] = jnp.dot(flipped[:, 6 * GATES :], low_windows[1], preferred_element_type=F32).astype(BF16)
    rims[1] = jnp.dot(flipped[:, : 3 * GATES], low_windows[ROWS], preferred_element_type=F32).astype(BF16)
    row_copies, row_waits = rows_out(place, rims.at[0], rims.at[1], low_halo, row_send.at[1], row_recv.at[1])
    bias = bias_finish(0, "core", bias_copies)
    bias_copies = bias_start(1, "x", bias)

    second_copies = []

    def second_start(a):
        axis1, axis2, _ = ORDERS[a]
        n1, n2 = place.count[axis1], place.count[axis2]
        rows1 = HALF // n1
        rows2 = rows1 // n2
        for copy in reversed(first_copies[a]):
            copy.wait_recv()
        pending.extend(first_copies[a])
        start = pl.multiple_of(place.index[axis1] * rows1, rows1)
        total = owned[a, :, pl.ds(start, rows1), :]
        for k in range(n1 - 1):
            total = total + first_in[a][k].astype(F32)
        for p in range(n2):
            second_out[a][p] = total[:, p * rows2 : (p + 1) * rows2, :]
        copies = []
        for k, device, other in reversed(place.peers(axis2)):
            copy = remote(second_out[a].at[other], second_in[a].at[k], sends.at[2, a, k], recvs.at[2, a, k], device)
            copy.start()
            copies.append(copy)
        second_copies.append((a, copies))

    second_start(2)
    second_start(0)
    second_start(1)

    bias = bias_finish(1, "x", bias_copies)
    bias_copies = bias_start(2, "y", bias)

    third_copies = []
    for a, copies2 in sorted(second_copies, key=lambda entry: entry[0]):
        _, axis2, axis3 = ORDERS[a]
        for copy in reversed(copies2):
            copy.wait_recv()
        pending += copies2
        total = second_out[a][place.index[axis2]]
        for k in range(place.count[axis2] - 1):
            total = total + second_in[a][k]
        slot = place.index[axis3]
        third[a][slot] = total.astype(BF16)
        copies = []
        for k, device, _ in reversed(place.peers(axis3)):
            copy = remote(third[a].at[slot], third[a].at[slot], sends.at[3, a, k], recvs.at[3, a, k], device)
            copy.start()
            copies.append(copy)
        third_copies.append((a, copies))

    hidden_next[...] = wide[pl.ds(0, hid * ROWS), :].reshape(hid, ROWS, COLS).astype(BF16)
    low_windows[0] = jnp.zeros((3 * GATES, COLS), BF16)
    low_windows[PADDED - 1] = jnp.zeros((3 * GATES, COLS), BF16)
    for pair in range(ROWS // 2):
        blocks = [low_windows[r : r + 3].reshape(9 * GATES, COLS) for r in (2 * pair, 2 * pair + 1)]
        both = jnp.dot(flipped, jnp.concatenate(blocks, axis=1), preferred_element_type=F32)
        for k in range(2):
            field[2 * pair + k] = both[:, k * COLS : (k + 1) * COLS]
    for copy in low_copies:
        copy.wait_recv()
    low_side, high_side = from_edge(low_sides[0]), from_edge(low_sides[1])

    def arrived(low_side, high_side, position):
        first = jnp.where(lanes == 0, pltpu.roll(low_side, (-position) % LANES, 1), 0.0)
        last = jnp.where(lanes == COLS - 1, pltpu.roll(high_side, (COLS - 1 - position) % LANES, 1), 0.0)
        return first + last

    pending += low_copies + row_copies + low_corner_copies
    for r in range(ROWS):
        field[r] = field[r] + arrived(low_side, high_side, r + 1)
    bias = bias_finish(2, "y", bias_copies)
    bias_copies = bias_start(3, "z", bias)

    fourth_copies = []
    for a, copies3 in third_copies:
        _, axis2, axis3 = ORDERS[a]
        for copy in reversed(copies3):
            copy.wait_recv()
        pending += copies3
        total = third[a][0].astype(F32)
        for k in range(1, place.count[axis3]):
            total = total + third[a][k].astype(F32)
        slot = place.index[axis2]
        gathered[a][slot] = (total * scaling).astype(BF16)
        copies = []
        for k, device, _ in reversed(place.peers(axis2)):
            copy = remote(gathered[a].at[slot], gathered[a].at[slot], sends.at[4, a, k], recvs.at[4, a, k], device)
            copy.start()
            copies.append(copy)
        fourth_copies.append((a, copies))

    def block_of(a, owner):
        rows1 = HALF // place.count[ORDERS[a][0]]
        start = pl.multiple_of(mine + owner * rows1, rows1)
        return kernel_low.at[pl.ds(3 * a, 3), pl.ds(start, rows1), :]

    last_copies = []

    def forward(a, owner, slot):
        block = block_of(a, owner)
        copy = remote(block, block, sends.at[6, a, slot], recvs.at[6, a, slot], partner)
        copy.start()
        last_copies.append(copy)

    fifth_copies = []
    for a, copies4 in fourth_copies:
        axis1, axis2, _ = ORDERS[a]
        n1 = place.count[axis1]
        for copy in reversed(copies4):
            copy.wait_recv()
        pending += copies4
        block = block_of(a, place.index[axis1])
        block[...] = jnp.concatenate(
            [gathered[a][p].astype(F32) for p in range(place.count[axis2])], axis=1
        ).astype(BF16)
        copies = []
        for k, device, _ in reversed(place.peers(axis1)):
            copy = remote(block, block, sends.at[5, a, k], recvs.at[5, a, k], device)
            copy.start()
            copies.append((copy, k, lax.rem(place.index[axis1] + n1 - 1 - k, n1)))
        forward(a, place.index[axis1], n1 - 1)
        fifth_copies.append((a, copies))

    for slot, r in ((0, 0), (1, ROWS - 1)):
        row_waits[slot].wait_recv()
        for wait in low_corner_waits[2 * slot : 2 * slot + 2]:
            wait.wait_recv()
        ends = [jnp.transpose(jnp.broadcast_to(low_corners[slot, side, 0:1], (LANES, STATE))) for side in range(2)]
        given_cells = jnp.where(lanes == 0, ends[0], jnp.where(lanes == COLS - 1, ends[1], 0.0))
        field[r] = field[r] + low_halo[slot].astype(F32) + given_cells
    for r in range(ROWS):
        wide[pl.ds(r, STATE, stride=ROWS), :] = field[r]
    grad_inputs[...] = wide[pl.ds(0, width * ROWS), :].reshape(width, ROWS, COLS).astype(BF16)
    grad_hidden[...] = wide[pl.ds(width * ROWS, hid * ROWS), :].reshape(hid, ROWS, COLS).astype(BF16)

    for a, copies5 in fifth_copies:
        for copy, k, sender in reversed(copies5):
            copy.wait_recv()
            forward(a, sender, k)
            pending.append(copy)
    bias_sum[...] = bias_finish(3, "z", bias_copies) * scaling
    for copy in last_copies:
        copy.wait_recv()
    pending += last_copies
    for copy in pending:
        copy.wait_send()


def finish_kernel(
    hidden_next,
    cell_next,
    grad_inputs,
    grad_hidden,
    grad_cell,
    kernel_low,
    bias_sum,
    hidden_next_out,
    cell_next_out,
    grad_inputs_out,
    grad_hidden_out,
    grad_cell_out,
    kernel_out,
    bias_out,
    kernel_wide,
    sems,
):
    pairs = (
        (hidden_next, hidden_next_out),
        (cell_next, cell_next_out),
        (grad_inputs, grad_inputs_out),
        (grad_hidden, grad_hidden_out),
        (grad_cell, grad_cell_out),
        (bias_sum.at[0:1], bias_out),
    )
    copies = [pltpu.make_async_copy(source, target, sems.at[i]) for i, (source, target) in enumerate(pairs)]
    for copy in copies:
        copy.start()
    for a in range(3):
        taps = pl.ds(3 * a, 3)
        kernel_wide[taps] = kernel_low[taps].astype(F32)
        copy = pltpu.make_async_copy(kernel_wide.at[taps], kernel_out.at[taps], sems.at[len(pairs) + a])
        copy.start()
        copies.append(copy)
    for copy in copies:
        copy.wait()


def shape_of(shape, dtype):
    return jax.ShapeDtypeStruct(shape, dtype)


def body(
    sizes,
    inputs_below,
    hidden_prev,
    cell_prev,
    kernel_weights,
    gate_bias,
    readout,
    target_field,
    land_mask,
    fire_mask,
    hidden_grad,
):
    nx, ny, zh, zl = sizes
    count = {"x": nx, "y": ny, "z": zh * zl}
    hid = hidden_prev.shape[0]
    dma = pltpu.SemaphoreType.DMA
    scaling = 1.0 / math.sqrt(ROWS * nx * zh * 2 * COLS * ny * zl)
    most = max(nx, ny, zh * zl)
    chunk = []
    for axis1, axis2, axis3 in ORDERS:
        rows1 = HALF // count[axis1]
        chunk.append((count[axis1], rows1, count[axis2], rows1 // count[axis2], count[axis3]))
    cells = shape_of((hid, ROWS, COLS), BF16)
    wide_cells = shape_of((hid * ROWS, COLS), F32)
    inputs = (
        inputs_below,
        hidden_prev,
        cell_prev.reshape(hid * ROWS, COLS),
        kernel_weights,
        gate_bias.reshape(1, GATES),
        readout.reshape(1, hid),
        target_field,
        land_mask,
        fire_mask,
        hidden_grad,
    )
    results = pl.pallas_call(
        functools.partial(step_kernel, sizes, scaling),
        out_shape=[
            cells,
            wide_cells,
            cells,
            cells,
            wide_cells,
            shape_of((9, GATES, STATE), BF16),
            shape_of((8, GATES), F32),
        ],
        in_specs=[pl.BlockSpec(memory_space=pltpu.HBM)] * len(inputs),
        out_specs=[VMEM_SPEC] * 7,
        scratch_shapes=[pltpu.VMEM(value.shape, value.dtype) for value in inputs]
        + [
            pltpu.VMEM((STATE * ROWS, COLS), F32),
            pltpu.VMEM((hid * ROWS, COLS), F32),
            pltpu.VMEM((PADDED, STATE, COLS), BF16),
            pltpu.VMEM((2, STATE, COLS), BF16),
            pltpu.VMEM((2, EDGE, STATE), BF16),
            pltpu.VMEM((2, EDGE, STATE), BF16),
            pltpu.VMEM((4, 8, STATE), F32),
            pltpu.VMEM((2, 2, 8, STATE), F32),
            pltpu.VMEM((PADDED, 3 * STATE, COLS), BF16),
            pltpu.VMEM((3, GATES, 3 * STATE), F32),
            pltpu.VMEM((9, STATE, GATES), BF16),
            pltpu.VMEM((ROWS, GATES, COLS), BF16),
            pltpu.VMEM((ROWS, STATE, COLS), F32),
            pltpu.VMEM((4, 8, STATE), F32),
            pltpu.VMEM((2, 2, 8, STATE), F32),
            pltpu.VMEM((2, STATE, COLS), BF16),
            pltpu.VMEM((2, STATE, COLS), BF16),
            pltpu.VMEM((2, EDGE, STATE), BF16),
            pltpu.VMEM((2, EDGE, STATE), BF16),
            pltpu.VMEM((PADDED, 3 * GATES, COLS), BF16),
            pltpu.VMEM((3, 3, HALF, STATE), BF16),
            pltpu.VMEM((3, 3, HALF, STATE), BF16),
            pltpu.VMEM((3, 3, HALF, STATE), F32),
            pltpu.VMEM((3, 3, HALF, STATE), BF16),
            [pltpu.VMEM((n1 - 1, 3, r1, STATE), BF16) for n1, r1, _, _, _ in chunk],
            [pltpu.VMEM((n2, 3, r2, STATE), F32) for _, _, n2, r2, _ in chunk],
            [pltpu.VMEM((n2 - 1, 3, r2, STATE), F32) for _, _, n2, r2, _ in chunk],
            [pltpu.VMEM((n3, 3, r2, STATE), BF16) for _, _, _, r2, n3 in chunk],
            [pltpu.VMEM((n2, 3, r2, STATE), BF16) for _, _, n2, r2, _ in chunk],
            [pltpu.VMEM((n, 8, GATES), F32) for n in (2, nx, ny, zh * zl)],
            dma((len(inputs),)),
            dma((2, 2)),
            dma((2, 2)),
            dma((3, 2)),
            dma((3, 2)),
            dma((4,)),
            dma((2, 2)),
            dma((4,)),
            dma((2, 2)),
            dma((7, 3, most)),
            dma((7, 3, most)),
            dma((4, most)),
            dma((4, most)),
        ],
        compiler_params=pltpu.CompilerParams(
            collective_id=0, has_side_effects=True, vmem_limit_bytes=VMEM_LIMIT
        ),
        name="whole_step",
    )(*[pltpu.with_memory_space_constraint(value, pltpu.HBM) for value in inputs])

    hidden_next, cell_next, grad_inputs, grad_hidden, grad_cell, grad_kernel, grad_bias = pl.pallas_call(
        finish_kernel,
        out_shape=[
            cells,
            wide_cells,
            cells,
            cells,
            wide_cells,
            shape_of((9, GATES, STATE), F32),
            shape_of((1, GATES), F32),
        ],
        in_specs=[VMEM_SPEC] * 7,
        out_specs=[pl.BlockSpec(memory_space=pltpu.HBM)] * 7,
        scratch_shapes=[pltpu.VMEM((9, GATES, STATE), F32), dma((9,))],
        compiler_params=pltpu.CompilerParams(vmem_limit_bytes=VMEM_LIMIT),
        name="results",
    )(*results)
    shape = (hid, ROWS, COLS)
    return (
        hidden_next,
        cell_next.reshape(shape),
        grad_inputs,
        grad_hidden,
        grad_cell.reshape(shape),
        grad_kernel,
        grad_bias.reshape(GATES),
    )


def solution(mesh):
    lat, lon = mesh.shape["lat"], mesh.shape["lon"]
    sizes = {(16, 32): (4, 8, 2, 4), (4, 4): (2, 2, 1, 2)}[(lat, lon)]
    cells = P(None, "lat", "lon")
    flat = P("lat", "lon")
    return jax.shard_map(
        functools.partial(body, sizes),
        mesh=mesh,
        in_specs=(cells, cells, cells, P(), P(), P(), flat, flat, flat, cells),
        out_specs=(cells, cells, cells, cells, cells, P(), P()),
        check_vma=False,
    )
```

```python
import functools
import math

import jax
import jax.numpy as jnp
from jax import lax
from jax.experimental import pallas as pl
from jax.experimental.pallas import tpu as pltpu
from jax.sharding import PartitionSpec as P

MESH = pl.DeviceIdType.MESH
F32 = jnp.float32
BF16 = jnp.bfloat16
ROWS = 8
COLS = 128
PADDED = ROWS + 2
STATE = 128
GATES = 256
HALF = GATES // 2
LANES = 128
EDGE = 16
VMEM_SPEC = pl.BlockSpec(memory_space=pltpu.VMEM)
VMEM_LIMIT = 48 * 1024 * 1024


class Place:
    def __init__(self, sizes):
        self.nx, self.ny, self.zh, self.zl = sizes
        self.nz = self.zh * self.zl
        self.nlat = self.nx * self.zh * 2
        self.nlon = self.ny * self.zl
        self.lat = lax.axis_index("lat")
        self.lon = lax.axis_index("lon")
        self.core = lax.rem(self.lat, 2)
        chip = self.lat // 2
        self.z_hi = lax.rem(chip, self.zh)
        self.x = chip // self.zh
        self.z_lo = lax.rem(self.lon, self.zl)
        self.y = self.lon // self.zl
        self.z = self.z_hi * self.zl + self.z_lo
        self.count = {"core": 2, "x": self.nx, "y": self.ny, "z": self.nz}
        self.index = {"core": self.core, "x": self.x, "y": self.y, "z": self.z}
        self.north = self.lat == 0
        self.south = self.lat == self.nlat - 1

    def at(self, x, y, z, core):
        lat = (x * self.zh + z // self.zl) * 2 + core
        lon = y * self.zl + lax.rem(z, self.zl)
        return (lat, lon)

    def peer(self, axis, steps):
        other = lax.rem(self.index[axis] + steps, self.count[axis])
        where = dict(self.index)
        where[axis] = other
        return self.at(where["x"], where["y"], where["z"], where["core"]), other

    def peers(self, axis):
        count = self.count[axis]
        order = sorted(range(1, count), key=lambda steps: min(steps, count - steps))
        return [(steps - 1, *self.peer(axis, steps)) for steps in order]

    def up(self):
        opposite = lax.rem(self.lon + self.nlon // 2, self.nlon)
        lat = jnp.where(self.north, 0, self.lat - 1)
        return (lat, jnp.where(self.north, opposite, self.lon))

    def down(self):
        opposite = lax.rem(self.lon + self.nlon // 2, self.nlon)
        lat = jnp.where(self.south, self.nlat - 1, self.lat + 1)
        return (lat, jnp.where(self.south, opposite, self.lon))

    def east(self):
        return (self.lat, lax.rem(self.lon + 1, self.nlon))

    def west(self):
        return (self.lat, lax.rem(self.lon + self.nlon - 1, self.nlon))

    def around(self):
        return [self.up(), self.down(), self.east(), self.west(), *self.diagonal()]

    def diagonal(self):
        found = []
        for lat, lon in (self.up(), self.down()):
            for steps in (1, self.nlon - 1):
                found.append((lat, lax.rem(lon + steps, self.nlon)))
        return found


def greet(devices):
    barrier = pltpu.get_barrier_semaphore()
    for device in devices:
        pl.semaphore_signal(barrier, inc=1, device_id=device, device_id_type=MESH)
    return barrier


def remote(source, target, send_sem, recv_sem, device):
    return pltpu.make_async_remote_copy(
        src_ref=source,
        dst_ref=target,
        send_sem=send_sem,
        recv_sem=recv_sem,
        device_id=device,
        device_id_type=MESH,
    )


def lane_ids(shape):
    return lax.broadcasted_iota(jnp.int32, shape, len(shape) - 1)


def rows_out(place, first, last, halo, send_sem, recv_sem):
    upper_slot = jnp.where(place.north, 0, 1)
    lower_slot = jnp.where(place.south, 1, 0)
    copies = [
        remote(first, halo.at[upper_slot], send_sem.at[0], recv_sem.at[upper_slot], place.up()),
        remote(last, halo.at[lower_slot], send_sem.at[1], recv_sem.at[lower_slot], place.down()),
    ]
    for copy in copies:
        copy.start()
    waits = [
        remote(first, halo.at[0], send_sem.at[0], recv_sem.at[0], place.up()),
        remote(last, halo.at[1], send_sem.at[1], recv_sem.at[1], place.down()),
    ]
    return copies, waits


def to_edge(total):
    return jnp.transpose(total)[0:EDGE]


def corners_out(place, outgoing, corners, send_sem, recv_sem):
    copies, waits = [], []
    for i, device in enumerate(place.diagonal()):
        slot = jnp.where(place.north, 0, 1) if i < 2 else jnp.where(place.south, 1, 0)
        side = i % 2
        copy = remote(outgoing.at[i], corners.at[slot, side], send_sem.at[i], recv_sem.at[slot, side], device)
        copy.start()
        copies.append(copy)
        waits.append(remote(outgoing.at[i], corners.at[i // 2, side], send_sem.at[i], recv_sem.at[i // 2, side], device))
    return copies, waits


def from_edge(edge):
    rest = jnp.zeros((LANES - EDGE, edge.shape[1]), F32)
    return jnp.transpose(jnp.concatenate([edge.astype(F32), rest], axis=0))


def collect(total, row, position, shift, lanes):
    return jnp.where(lanes == position, pltpu.roll(row, shift % LANES, 1), total)


def cols_out(place, edges, sides, send_sem, recv_sem):
    copies = [
        remote(edges.at[0], sides.at[0], send_sem.at[0], recv_sem.at[0], place.east()),
        remote(edges.at[1], sides.at[1], send_sem.at[1], recv_sem.at[1], place.west()),
    ]
    for copy in copies:
        copy.start()
    return copies


def spread(values, sides_low, sides_high, lanes, position):
    before = jnp.where(lanes == 0, pltpu.roll(sides_low, (-position) % LANES, 1), pltpu.roll(values, 1, 1))
    after = jnp.where(
        lanes == COLS - 1, pltpu.roll(sides_high, (COLS - 1 - position) % LANES, 1), pltpu.roll(values, COLS - 1, 1)
    )
    return before, after


ORDERS = (("y", "x", "z"), ("z", "x", "y"), ("x", "y", "z"))
EARLY = ((1, 2), (3, 4), (5, 6))
LATE = (0, 7)


def step_kernel(
    sizes,
    scaling,
    below_hbm,
    hidden_hbm,
    cell_hbm,
    weights_hbm,
    gate_bias_hbm,
    readout_hbm,
    target_hbm,
    land_hbm,
    fire_hbm,
    hidden_grad_hbm,
    hidden_next,
    cell_next,
    grad_inputs,
    grad_hidden,
    grad_cell,
    kernel_low,
    bias_sum,
    below,
    hidden,
    cell_prev,
    weights,
    gate_bias,
    readout,
    target,
    land,
    fire,
    hidden_grad,
    wide,
    wide_grad,
    rows,
    halo,
    edges,
    sides,
    corner_edges,
    corners,
    windows,
    kernel_acc,
    turned,
    low_rows,
    field,
    low_corner_edges,
    low_corners,
    rims,
    low_halo,
    low_edges,
    low_sides,
    low_windows,
    pair_out,
    pair_in,
    owned,
    first_out,
    first_in,
    second_out,
    second_in,
    third,
    gathered,
    bias_bufs,
    load_sem,
    row_send,
    row_recv,
    col_send,
    col_recv,
    corner_send,
    corner_recv,
    low_corner_send,
    low_corner_recv,
    sends,
    recvs,
    bias_send,
    bias_recv,
):
    place = Place(sizes)
    hid = hidden_next.shape[0]
    width = grad_inputs.shape[0]
    partner, _ = place.peer("core", 1)
    devices = place.around()
    for axis in ("z", "y", "x"):
        devices += [device for _, device, _ in reversed(place.peers(axis))]
    devices.append(partner)
    barrier = greet(devices)
    mine = pl.multiple_of(place.core * HALF, HALF)
    theirs = pl.multiple_of((1 - place.core) * HALF, HALF)
    pending = []

    sources = (below_hbm, hidden_hbm, weights_hbm, cell_hbm, hidden_grad_hbm, gate_bias_hbm, readout_hbm,
               target_hbm, land_hbm, fire_hbm)
    targets = (below, hidden, weights, cell_prev, hidden_grad, gate_bias, readout, target, land, fire)
    loads = [
        pltpu.make_async_copy(source, destination, load_sem.at[i])
        for i, (source, destination) in enumerate(zip(sources, targets))
    ]
    for load in loads:
        load.start()

    loads[0].wait()
    wide[pl.ds(0, width * ROWS), :] = below[...].astype(F32).reshape(width * ROWS, COLS)
    loads[1].wait()
    wide[pl.ds(width * ROWS, hid * ROWS), :] = hidden[...].astype(F32).reshape(hid * ROWS, COLS)

    def state_row(r):
        return wide[pl.ds(r, STATE, stride=ROWS), :]

    for r in (0, ROWS - 1):
        rows[r + 1] = state_row(r).astype(BF16)
    pl.semaphore_wait(barrier, len(devices))
    row_copies, row_waits = rows_out(place, rows.at[1], rows.at[ROWS], halo, row_send.at[0], row_recv.at[0])

    lanes = lane_ids((STATE, COLS))
    east = jnp.zeros((STATE, COLS), F32)
    west = jnp.zeros((STATE, COLS), F32)
    for r in range(ROWS):
        value = state_row(r)
        if 0 < r < ROWS - 1:
            rows[r + 1] = value.astype(BF16)
        east = collect(east, value, r + 1, r + 2, lanes)
        west = collect(west, value, r + 1, r + 1, lanes)
    ends = (to_edge(east), to_edge(west))
    for i in range(4):
        position = 1 if i < 2 else ROWS
        corner_edges[i] = jnp.broadcast_to(ends[i % 2][position : position + 1], (8, STATE))
    corner_copies, corner_waits = corners_out(place, corner_edges, corners, corner_send, corner_recv)
    edges[0] = ends[0].astype(BF16)
    edges[1] = ends[1].astype(BF16)
    col_copies = cols_out(place, edges, sides, col_send.at[0], col_recv.at[0])
    pending += row_copies + col_copies + corner_copies

    for load in loads[2:]:
        load.wait()
    wide_grad[...] = hidden_grad[...].astype(F32).reshape(hid * ROWS, COLS)
    bias_cols = jnp.transpose(jnp.broadcast_to(gate_bias[...], (LANES, GATES)))
    read_cols = jnp.transpose(jnp.broadcast_to(readout[...], (LANES, hid)))
    for t in range(9):
        turned[t] = jnp.transpose(weights[t].astype(F32)).astype(BF16)

    def open_windows(position, low, low_side, high_side):
        before, after = spread(low.astype(F32), low_side, high_side, lanes, position)
        windows[position, 0:STATE] = before.astype(BF16)
        windows[position, STATE : 2 * STATE] = low
        windows[position, 2 * STATE : 3 * STATE] = after.astype(BF16)

    for copy in col_copies:
        copy.wait_recv()
    low_side, high_side = from_edge(sides[0]), from_edge(sides[1])
    for position in range(1, PADDED - 1):
        open_windows(position, rows[position], low_side, high_side)

    flat = jnp.concatenate([weights[t] for t in range(9)], axis=1)

    def cells_of(pair, bias_total):
        columns = jnp.concatenate([windows[r : r + 3].reshape(9 * STATE, COLS) for r in pair], axis=1)
        both = jnp.dot(flat, columns, preferred_element_type=F32)
        for k, r in enumerate(pair):
            preact = both[:, k * COLS : (k + 1) * COLS] + bias_cols
            input_gate = jax.nn.sigmoid(preact[0:hid])
            forget_gate = jax.nn.sigmoid(preact[hid : 2 * hid])
            output_gate = jax.nn.sigmoid(preact[2 * hid : 3 * hid])
            candidate = jnp.tanh(preact[3 * hid : 4 * hid])
            land_row = land[r : r + 1, :].astype(F32)
            fire_row = fire[r : r + 1, :].astype(F32)
            prev = cell_prev[pl.ds(r, hid, stride=ROWS), :]
            cell = land_row * (forget_gate * prev + input_gate * candidate)
            squashed = jnp.tanh(cell)
            new_hidden = (output_gate * squashed).astype(BF16).astype(F32)
            predicted = jnp.sum(read_cols * new_hidden, axis=0, keepdims=True)
            miss = 2.0 * (fire_row * (predicted - target[r : r + 1, :]))
            total_grad = wide_grad[pl.ds(r, hid, stride=ROWS), :] + miss * read_cols
            cell_grad = land_row * total_grad * output_gate * (1.0 - squashed * squashed)
            pre_grad = jnp.concatenate(
                [
                    cell_grad * candidate * input_gate * (1.0 - input_gate),
                    cell_grad * prev * forget_gate * (1.0 - forget_gate),
                    total_grad * squashed * output_gate * (1.0 - output_gate),
                    cell_grad * input_gate * (1.0 - candidate * candidate),
                ],
                axis=0,
            )
            cell_next[pl.ds(r, hid, stride=ROWS), :] = cell
            grad_cell[pl.ds(r, hid, stride=ROWS), :] = cell_grad * forget_gate
            wide[pl.ds(r, hid, stride=ROWS), :] = new_hidden
            bias_total = bias_total + pre_grad
            low_rows[r] = pre_grad.astype(BF16)
        return bias_total

    def kernel_terms(cells, rows_in, a):
        seen = jnp.concatenate([windows[r + a] for r in rows_in], axis=1)
        return lax.dot_general(cells, seen, (((1,), (1,)), ((), ())), preferred_element_type=F32)

    bias_total = jnp.zeros((GATES, COLS), F32)
    for pair in EARLY:
        bias_total = cells_of(pair, bias_total)
    cells = jnp.concatenate([low_rows[r] for r in range(1, ROWS - 1)], axis=1)
    for a in range(3):
        kernel_acc[a] = kernel_terms(cells, range(1, ROWS - 1), a)

    for wait in row_waits + corner_waits:
        wait.wait_recv()
    for slot, position in ((0, 0), (1, PADDED - 1)):
        ends = [jnp.transpose(jnp.broadcast_to(corners[slot, side, 0:1], (LANES, STATE))) for side in range(2)]
        open_windows(position, halo[slot], *ends)
    bias_total = cells_of(LATE, bias_total)

    halves = [pl.ds(theirs, HALF), pl.ds(mine, HALF)]
    cells = jnp.concatenate(
        [jnp.concatenate([low_rows[r, half, :] for r in LATE], axis=1) for half in halves], axis=0
    )
    pair_copies = []
    for a in range(3):
        part = kernel_terms(cells, LATE, a)
        given = part[0:HALF] + kernel_acc[a, halves[0], :]
        kept = part[HALF:] + kernel_acc[a, halves[1], :]
        for b in range(3):
            pair_out[a, b] = given[:, b * STATE : (b + 1) * STATE].astype(BF16)
        copy = remote(pair_out.at[a], pair_in.at[a], sends.at[0, a, 0], recvs.at[0, a, 0], partner)
        copy.start()
        pair_copies.append(copy)
        for b in range(3):
            owned[a, b] = kept[:, b * STATE : (b + 1) * STATE]

    first_copies = []
    for a in range(3):
        pair_copies[a].wait_recv()
        total = owned[a] + pair_in[a].astype(F32)
        owned[a] = total
        first_out[a] = total.astype(BF16)
        axis = ORDERS[a][0]
        rows1 = HALF // place.count[axis]
        copies = []
        for k, device, other in reversed(place.peers(axis)):
            start = pl.multiple_of(other * rows1, rows1)
            copy = remote(
                first_out.at[a, :, pl.ds(start, rows1), :],
                first_in[a].at[k],
                sends.at[1, a, k],
                recvs.at[1, a, k],
                device,
            )
            copy.start()
            copies.append(copy)
        first_copies.append(copies)
    pending += pair_copies

    def bias_start(stage, axis, value):
        slot = place.index[axis]
        buf = bias_bufs[stage]
        buf[slot] = value
        copies = []
        for k, device, _ in place.peers(axis):
            copy = remote(buf.at[slot], buf.at[slot], bias_send.at[stage, k], bias_recv.at[stage, k], device)
            copy.start()
            copies.append(copy)
        return copies

    def bias_finish(stage, axis, copies):
        buf = bias_bufs[stage]
        for copy in copies:
            copy.wait_recv()
        pending.extend(copies)
        total = buf[0]
        for k in range(1, place.count[axis]):
            total = total + buf[k]
        return total

    bias = lax.dot_general(
        jnp.ones((8, COLS), F32),
        bias_total,
        (((1,), (1,)), ((), ())),
        precision=lax.Precision.HIGHEST,
        preferred_element_type=F32,
    )
    bias_copies = bias_start(0, "core", bias)

    gate_lanes = lane_ids((GATES, COLS))
    east = jnp.zeros((GATES, COLS), F32)
    west = jnp.zeros((GATES, COLS), F32)
    for r in range(ROWS):
        value = low_rows[r].astype(F32)
        before = jnp.where(gate_lanes == 0, 0.0, pltpu.roll(value, 1, 1))
        after = jnp.where(gate_lanes == COLS - 1, 0.0, pltpu.roll(value, COLS - 1, 1))
        low_windows[r + 1, 0:GATES] = before.astype(BF16)
        low_windows[r + 1, GATES : 2 * GATES] = low_rows[r]
        low_windows[r + 1, 2 * GATES : 3 * GATES] = after.astype(BF16)
        east = collect(east, value, r + 1, r + 2, gate_lanes)
        west = collect(west, value, r + 1, r + 1, gate_lanes)
    for slot, (value, last) in enumerate(((east, 2), (west, 0))):
        shifts = jnp.concatenate([pltpu.roll(value, a % LANES, 1).astype(BF16) for a in (-1, 0, 1)], axis=0)
        taps = jnp.concatenate([turned[3 * a + last] for a in range(3)], axis=1)
        given_cells = to_edge(jnp.dot(taps, shifts, preferred_element_type=F32))
        low_edges[slot] = given_cells.astype(BF16)
        for i, position in ((slot, 0), (slot + 2, PADDED - 1)):
            low_corner_edges[i] = jnp.broadcast_to(given_cells[position : position + 1], (8, STATE))
    low_copies = cols_out(place, low_edges, low_sides, col_send.at[2], col_recv.at[2])
    low_corner_copies, low_corner_waits = corners_out(
        place, low_corner_edges, low_corners, low_corner_send, low_corner_recv
    )

    flipped = jnp.concatenate([turned[8 - q] for q in range(9)], axis=1)
    rims[0] = jnp.dot(flipped[:, 6 * GATES :], low_windows[1], preferred_element_type=F32).astype(BF16)
    rims[1] = jnp.dot(flipped[:, : 3 * GATES], low_windows[ROWS], preferred_element_type=F32).astype(BF16)
    row_copies, row_waits = rows_out(place, rims.at[0], rims.at[1], low_halo, row_send.at[1], row_recv.at[1])
    bias = bias_finish(0, "core", bias_copies)
    bias_copies = bias_start(1, "x", bias)

    second_copies = []

    def second_start(a):
        axis1, axis2, _ = ORDERS[a]
        n1, n2 = place.count[axis1], place.count[axis2]
        rows1 = HALF // n1
        rows2 = rows1 // n2
        for copy in reversed(first_copies[a]):
            copy.wait_recv()
        pending.extend(first_copies[a])
        start = pl.multiple_of(place.index[axis1] * rows1, rows1)
        total = owned[a, :, pl.ds(start, rows1), :]
        for k in range(n1 - 1):
            total = total + first_in[a][k].astype(F32)
        for p in range(n2):
            second_out[a][p] = total[:, p * rows2 : (p + 1) * rows2, :]
        copies = []
        for k, device, other in reversed(place.peers(axis2)):
            copy = remote(second_out[a].at[other], second_in[a].at[k], sends.at[2, a, k], recvs.at[2, a, k], device)
            copy.start()
            copies.append(copy)
        second_copies.append((a, copies))

    second_start(2)
    second_start(0)
    second_start(1)

    bias = bias_finish(1, "x", bias_copies)
    bias_copies = bias_start(2, "y", bias)

    third_copies = []
    for a, copies2 in sorted(second_copies, key=lambda entry: entry[0]):
        _, axis2, axis3 = ORDERS[a]
        for copy in reversed(copies2):
            copy.wait_recv()
        pending += copies2
        total = second_out[a][place.index[axis2]]
        for k in range(place.count[axis2] - 1):
            total = total + second_in[a][k]
        slot = place.index[axis3]
        third[a][slot] = total
        copies = []
        for k, device, _ in reversed(place.peers(axis3)):
            copy = remote(third[a].at[slot], third[a].at[slot], sends.at[3, a, k], recvs.at[3, a, k], device)
            copy.start()
            copies.append(copy)
        third_copies.append((a, copies))

    hidden_next[...] = wide[pl.ds(0, hid * ROWS), :].reshape(hid, ROWS, COLS).astype(BF16)
    low_windows[0] = jnp.zeros((3 * GATES, COLS), BF16)
    low_windows[PADDED - 1] = jnp.zeros((3 * GATES, COLS), BF16)
    for pair in range(ROWS // 2):
        blocks = [low_windows[r : r + 3].reshape(9 * GATES, COLS) for r in (2 * pair, 2 * pair + 1)]
        both = jnp.dot(flipped, jnp.concatenate(blocks, axis=1), preferred_element_type=F32)
        for k in range(2):
            field[2 * pair + k] = both[:, k * COLS : (k + 1) * COLS]
    for copy in low_copies:
        copy.wait_recv()
    low_side, high_side = from_edge(low_sides[0]), from_edge(low_sides[1])

    def arrived(low_side, high_side, position):
        first = jnp.where(lanes == 0, pltpu.roll(low_side, (-position) % LANES, 1), 0.0)
        last = jnp.where(lanes == COLS - 1, pltpu.roll(high_side, (COLS - 1 - position) % LANES, 1), 0.0)
        return first + last

    pending += low_copies + row_copies + low_corner_copies
    for r in range(ROWS):
        field[r] = field[r] + arrived(low_side, high_side, r + 1)
    bias = bias_finish(2, "y", bias_copies)
    bias_copies = bias_start(3, "z", bias)

    fourth_copies = []
    for a, copies3 in third_copies:
        _, axis2, axis3 = ORDERS[a]
        for copy in reversed(copies3):
            copy.wait_recv()
        pending += copies3
        total = third[a][0]
        for k in range(1, place.count[axis3]):
            total = total + third[a][k]
        slot = place.index[axis2]
        gathered[a][slot] = (total * scaling).astype(BF16)
        copies = []
        for k, device, _ in reversed(place.peers(axis2)):
            copy = remote(gathered[a].at[slot], gathered[a].at[slot], sends.at[4, a, k], recvs.at[4, a, k], device)
            copy.start()
            copies.append(copy)
        fourth_copies.append((a, copies))

    def block_of(a, owner):
        rows1 = HALF // place.count[ORDERS[a][0]]
        start = pl.multiple_of(mine + owner * rows1, rows1)
        return kernel_low.at[pl.ds(3 * a, 3), pl.ds(start, rows1), :]

    last_copies = []

    def forward(a, owner, slot):
        block = block_of(a, owner)
        copy = remote(block, block, sends.at[6, a, slot], recvs.at[6, a, slot], partner)
        copy.start()
        last_copies.append(copy)

    fifth_copies = []
    for a, copies4 in fourth_copies:
        axis1, axis2, _ = ORDERS[a]
        n1 = place.count[axis1]
        for copy in reversed(copies4):
            copy.wait_recv()
        pending += copies4
        block = block_of(a, place.index[axis1])
        block[...] = jnp.concatenate(
            [gathered[a][p].astype(F32) for p in range(place.count[axis2])], axis=1
        ).astype(BF16)
        copies = []
        for k, device, _ in reversed(place.peers(axis1)):
            copy = remote(block, block, sends.at[5, a, k], recvs.at[5, a, k], device)
            copy.start()
            copies.append((copy, k, lax.rem(place.index[axis1] + n1 - 1 - k, n1)))
        forward(a, place.index[axis1], n1 - 1)
        fifth_copies.append((a, copies))

    for slot, r in ((0, 0), (1, ROWS - 1)):
        row_waits[slot].wait_recv()
        for wait in low_corner_waits[2 * slot : 2 * slot + 2]:
            wait.wait_recv()
        ends = [jnp.transpose(jnp.broadcast_to(low_corners[slot, side, 0:1], (LANES, STATE))) for side in range(2)]
        given_cells = jnp.where(lanes == 0, ends[0], jnp.where(lanes == COLS - 1, ends[1], 0.0))
        field[r] = field[r] + low_halo[slot].astype(F32) + given_cells
    for r in range(ROWS):
        wide[pl.ds(r, STATE, stride=ROWS), :] = field[r]
    grad_inputs[...] = wide[pl.ds(0, width * ROWS), :].reshape(width, ROWS, COLS).astype(BF16)
    grad_hidden[...] = wide[pl.ds(width * ROWS, hid * ROWS), :].reshape(hid, ROWS, COLS).astype(BF16)

    arrivals = []
    for a, copies5 in fifth_copies:
        count = place.count[ORDERS[a][0]]
        arrivals += [(min(k + 1, count - 1 - k), a, copy, k, sender) for copy, k, sender in copies5]
    for _, a, copy, k, sender in sorted(arrivals, key=lambda entry: entry[:2]):
        copy.wait_recv()
        forward(a, sender, k)
        pending.append(copy)
    bias_sum[...] = bias_finish(3, "z", bias_copies) * scaling
    for copy in last_copies:
        copy.wait_recv()
    pending += last_copies
    for copy in pending:
        copy.wait_send()


def finish_kernel(
    hidden_next,
    cell_next,
    grad_inputs,
    grad_hidden,
    grad_cell,
    kernel_low,
    bias_sum,
    hidden_next_out,
    cell_next_out,
    grad_inputs_out,
    grad_hidden_out,
    grad_cell_out,
    kernel_out,
    bias_out,
    kernel_wide,
    sems,
):
    pairs = (
        (hidden_next, hidden_next_out),
        (cell_next, cell_next_out),
        (grad_inputs, grad_inputs_out),
        (grad_hidden, grad_hidden_out),
        (grad_cell, grad_cell_out),
        (bias_sum.at[0:1], bias_out),
    )
    copies = [pltpu.make_async_copy(source, target, sems.at[i]) for i, (source, target) in enumerate(pairs)]
    for copy in copies:
        copy.start()
    for a in range(3):
        taps = pl.ds(3 * a, 3)
        kernel_wide[taps] = kernel_low[taps].astype(F32)
        copy = pltpu.make_async_copy(kernel_wide.at[taps], kernel_out.at[taps], sems.at[len(pairs) + a])
        copy.start()
        copies.append(copy)
    for copy in copies:
        copy.wait()


def shape_of(shape, dtype):
    return jax.ShapeDtypeStruct(shape, dtype)


def body(
    sizes,
    inputs_below,
    hidden_prev,
    cell_prev,
    kernel_weights,
    gate_bias,
    readout,
    target_field,
    land_mask,
    fire_mask,
    hidden_grad,
):
    nx, ny, zh, zl = sizes
    count = {"x": nx, "y": ny, "z": zh * zl}
    hid = hidden_prev.shape[0]
    dma = pltpu.SemaphoreType.DMA
    scaling = 1.0 / math.sqrt(ROWS * nx * zh * 2 * COLS * ny * zl)
    most = max(nx, ny, zh * zl)
    chunk = []
    for axis1, axis2, axis3 in ORDERS:
        rows1 = HALF // count[axis1]
        chunk.append((count[axis1], rows1, count[axis2], rows1 // count[axis2], count[axis3]))
    cells = shape_of((hid, ROWS, COLS), BF16)
    wide_cells = shape_of((hid * ROWS, COLS), F32)
    inputs = (
        inputs_below,
        hidden_prev,
        cell_prev.reshape(hid * ROWS, COLS),
        kernel_weights,
        gate_bias.reshape(1, GATES),
        readout.reshape(1, hid),
        target_field,
        land_mask,
        fire_mask,
        hidden_grad,
    )
    results = pl.pallas_call(
        functools.partial(step_kernel, sizes, scaling),
        out_shape=[
            cells,
            wide_cells,
            cells,
            cells,
            wide_cells,
            shape_of((9, GATES, STATE), BF16),
            shape_of((8, GATES), F32),
        ],
        in_specs=[pl.BlockSpec(memory_space=pltpu.HBM)] * len(inputs),
        out_specs=[VMEM_SPEC] * 7,
        scratch_shapes=[pltpu.VMEM(value.shape, value.dtype) for value in inputs]
        + [
            pltpu.VMEM((STATE * ROWS, COLS), F32),
            pltpu.VMEM((hid * ROWS, COLS), F32),
            pltpu.VMEM((PADDED, STATE, COLS), BF16),
            pltpu.VMEM((2, STATE, COLS), BF16),
            pltpu.VMEM((2, EDGE, STATE), BF16),
            pltpu.VMEM((2, EDGE, STATE), BF16),
            pltpu.VMEM((4, 8, STATE), F32),
            pltpu.VMEM((2, 2, 8, STATE), F32),
            pltpu.VMEM((PADDED, 3 * STATE, COLS), BF16),
            pltpu.VMEM((3, GATES, 3 * STATE), F32),
            pltpu.VMEM((9, STATE, GATES), BF16),
            pltpu.VMEM((ROWS, GATES, COLS), BF16),
            pltpu.VMEM((ROWS, STATE, COLS), F32),
            pltpu.VMEM((4, 8, STATE), F32),
            pltpu.VMEM((2, 2, 8, STATE), F32),
            pltpu.VMEM((2, STATE, COLS), BF16),
            pltpu.VMEM((2, STATE, COLS), BF16),
            pltpu.VMEM((2, EDGE, STATE), BF16),
            pltpu.VMEM((2, EDGE, STATE), BF16),
            pltpu.VMEM((PADDED, 3 * GATES, COLS), BF16),
            pltpu.VMEM((3, 3, HALF, STATE), BF16),
            pltpu.VMEM((3, 3, HALF, STATE), BF16),
            pltpu.VMEM((3, 3, HALF, STATE), F32),
            pltpu.VMEM((3, 3, HALF, STATE), BF16),
            [pltpu.VMEM((n1 - 1, 3, r1, STATE), BF16) for n1, r1, _, _, _ in chunk],
            [pltpu.VMEM((n2, 3, r2, STATE), F32) for _, _, n2, r2, _ in chunk],
            [pltpu.VMEM((n2 - 1, 3, r2, STATE), F32) for _, _, n2, r2, _ in chunk],
            [pltpu.VMEM((n3, 3, r2, STATE), F32) for _, _, _, r2, n3 in chunk],
            [pltpu.VMEM((n2, 3, r2, STATE), BF16) for _, _, n2, r2, _ in chunk],
            [pltpu.VMEM((n, 8, GATES), F32) for n in (2, nx, ny, zh * zl)],
            dma((len(inputs),)),
            dma((2, 2)),
            dma((2, 2)),
            dma((3, 2)),
            dma((3, 2)),
            dma((4,)),
            dma((2, 2)),
            dma((4,)),
            dma((2, 2)),
            dma((7, 3, most)),
            dma((7, 3, most)),
            dma((4, most)),
            dma((4, most)),
        ],
        compiler_params=pltpu.CompilerParams(
            collective_id=0, has_side_effects=True, vmem_limit_bytes=VMEM_LIMIT
        ),
        name="whole_step",
    )(*[pltpu.with_memory_space_constraint(value, pltpu.HBM) for value in inputs])

    hidden_next, cell_next, grad_inputs, grad_hidden, grad_cell, grad_kernel, grad_bias = pl.pallas_call(
        finish_kernel,
        out_shape=[
            cells,
            wide_cells,
            cells,
            cells,
            wide_cells,
            shape_of((9, GATES, STATE), F32),
            shape_of((1, GATES), F32),
        ],
        in_specs=[VMEM_SPEC] * 7,
        out_specs=[pl.BlockSpec(memory_space=pltpu.HBM)] * 7,
        scratch_shapes=[pltpu.VMEM((9, GATES, STATE), F32), dma((9,))],
        compiler_params=pltpu.CompilerParams(vmem_limit_bytes=VMEM_LIMIT),
        name="results",
    )(*results)
    shape = (hid, ROWS, COLS)
    return (
        hidden_next,
        cell_next.reshape(shape),
        grad_inputs,
        grad_hidden,
        grad_cell.reshape(shape),
        grad_kernel,
        grad_bias.reshape(GATES),
    )


def solution(mesh):
    lat, lon = mesh.shape["lat"], mesh.shape["lon"]
    sizes = {(16, 32): (4, 8, 2, 4), (4, 4): (2, 2, 1, 2)}[(lat, lon)]
    cells = P(None, "lat", "lon")
    flat = P("lat", "lon")
    return jax.shard_map(
        functools.partial(body, sizes),
        mesh=mesh,
        in_specs=(cells, cells, cells, P(), P(), P(), flat, flat, flat, cells),
        out_specs=(cells, cells, cells, cells, cells, P(), P()),
        check_vma=False,
    )
```

```python
import functools
import math

import jax
import jax.numpy as jnp
from jax import lax
from jax.experimental import pallas as pl
from jax.experimental.pallas import tpu as pltpu
from jax.sharding import PartitionSpec as P

MESH = pl.DeviceIdType.MESH
F32 = jnp.float32
BF16 = jnp.bfloat16
ROWS = 8
COLS = 128
PADDED = ROWS + 2
STATE = 128
GATES = 256
HALF = GATES // 2
LANES = 128
EDGE = 16
VMEM_SPEC = pl.BlockSpec(memory_space=pltpu.VMEM)
VMEM_LIMIT = 48 * 1024 * 1024


class Place:
    def __init__(self, sizes):
        self.nx, self.ny, self.zh, self.zl = sizes
        self.nz = self.zh * self.zl
        self.nlat = self.nx * self.zh * 2
        self.nlon = self.ny * self.zl
        self.lat = lax.axis_index("lat")
        self.lon = lax.axis_index("lon")
        self.core = lax.rem(self.lat, 2)
        chip = self.lat // 2
        self.z_hi = lax.rem(chip, self.zh)
        self.x = chip // self.zh
        self.z_lo = lax.rem(self.lon, self.zl)
        self.y = self.lon // self.zl
        self.z = self.z_hi * self.zl + self.z_lo
        self.count = {"core": 2, "x": self.nx, "y": self.ny, "z": self.nz}
        self.index = {"core": self.core, "x": self.x, "y": self.y, "z": self.z}
        self.north = self.lat == 0
        self.south = self.lat == self.nlat - 1

    def at(self, x, y, z, core):
        lat = (x * self.zh + z // self.zl) * 2 + core
        lon = y * self.zl + lax.rem(z, self.zl)
        return (lat, lon)

    def peer(self, axis, steps):
        other = lax.rem(self.index[axis] + steps, self.count[axis])
        where = dict(self.index)
        where[axis] = other
        return self.at(where["x"], where["y"], where["z"], where["core"]), other

    def peers(self, axis):
        count = self.count[axis]
        order = sorted(range(1, count), key=lambda steps: min(steps, count - steps))
        return [(steps - 1, *self.peer(axis, steps)) for steps in order]

    def up(self):
        opposite = lax.rem(self.lon + self.nlon // 2, self.nlon)
        lat = jnp.where(self.north, 0, self.lat - 1)
        return (lat, jnp.where(self.north, opposite, self.lon))

    def down(self):
        opposite = lax.rem(self.lon + self.nlon // 2, self.nlon)
        lat = jnp.where(self.south, self.nlat - 1, self.lat + 1)
        return (lat, jnp.where(self.south, opposite, self.lon))

    def east(self):
        return (self.lat, lax.rem(self.lon + 1, self.nlon))

    def west(self):
        return (self.lat, lax.rem(self.lon + self.nlon - 1, self.nlon))

    def around(self):
        return [self.up(), self.down(), self.east(), self.west(), *self.diagonal()]

    def diagonal(self):
        found = []
        for lat, lon in (self.up(), self.down()):
            for steps in (1, self.nlon - 1):
                found.append((lat, lax.rem(lon + steps, self.nlon)))
        return found


def greet(devices):
    barrier = pltpu.get_barrier_semaphore()
    for device in devices:
        pl.semaphore_signal(barrier, inc=1, device_id=device, device_id_type=MESH)
    return barrier


def remote(source, target, send_sem, recv_sem, device):
    return pltpu.make_async_remote_copy(
        src_ref=source,
        dst_ref=target,
        send_sem=send_sem,
        recv_sem=recv_sem,
        device_id=device,
        device_id_type=MESH,
    )


def lane_ids(shape):
    return lax.broadcasted_iota(jnp.int32, shape, len(shape) - 1)


def rows_out(place, first, last, halo, send_sem, recv_sem):
    upper_slot = jnp.where(place.north, 0, 1)
    lower_slot = jnp.where(place.south, 1, 0)
    copies = [
        remote(first, halo.at[upper_slot], send_sem.at[0], recv_sem.at[upper_slot], place.up()),
        remote(last, halo.at[lower_slot], send_sem.at[1], recv_sem.at[lower_slot], place.down()),
    ]
    for copy in copies:
        copy.start()
    waits = [
        remote(first, halo.at[0], send_sem.at[0], recv_sem.at[0], place.up()),
        remote(last, halo.at[1], send_sem.at[1], recv_sem.at[1], place.down()),
    ]
    return copies, waits


def to_edge(total):
    return jnp.transpose(total)[0:EDGE]


def corners_out(place, outgoing, corners, send_sem, recv_sem):
    copies, waits = [], []
    for i, device in enumerate(place.diagonal()):
        slot = jnp.where(place.north, 0, 1) if i < 2 else jnp.where(place.south, 1, 0)
        side = i % 2
        copy = remote(outgoing.at[i], corners.at[slot, side], send_sem.at[i], recv_sem.at[slot, side], device)
        copy.start()
        copies.append(copy)
        waits.append(remote(outgoing.at[i], corners.at[i // 2, side], send_sem.at[i], recv_sem.at[i // 2, side], device))
    return copies, waits


def from_edge(edge):
    rest = jnp.zeros((LANES - EDGE, edge.shape[1]), F32)
    return jnp.transpose(jnp.concatenate([edge.astype(F32), rest], axis=0))


def collect(total, row, position, shift, lanes):
    return jnp.where(lanes == position, pltpu.roll(row, shift % LANES, 1), total)


def cols_out(place, edges, sides, send_sem, recv_sem):
    copies = [
        remote(edges.at[0], sides.at[0], send_sem.at[0], recv_sem.at[0], place.east()),
        remote(edges.at[1], sides.at[1], send_sem.at[1], recv_sem.at[1], place.west()),
    ]
    for copy in copies:
        copy.start()
    return copies


def spread(values, sides_low, sides_high, lanes, position):
    before = jnp.where(lanes == 0, pltpu.roll(sides_low, (-position) % LANES, 1), pltpu.roll(values, 1, 1))
    after = jnp.where(
        lanes == COLS - 1, pltpu.roll(sides_high, (COLS - 1 - position) % LANES, 1), pltpu.roll(values, COLS - 1, 1)
    )
    return before, after


ORDERS = (("y", "x", "z"), ("z", "x", "y"), ("x", "y", "z"))
EARLY = ((1, 2), (3, 4), (5, 6))
LATE = (0, 7)


def step_kernel(
    sizes,
    scaling,
    below_hbm,
    hidden_hbm,
    cell_hbm,
    weights_hbm,
    gate_bias_hbm,
    readout_hbm,
    target_hbm,
    land_hbm,
    fire_hbm,
    hidden_grad_hbm,
    hidden_next,
    cell_next,
    grad_inputs,
    grad_hidden,
    grad_cell,
    kernel_low,
    bias_sum,
    below,
    hidden,
    cell_prev,
    weights,
    gate_bias,
    readout,
    target,
    land,
    fire,
    hidden_grad,
    wide,
    wide_grad,
    rows,
    halo,
    edges,
    sides,
    corner_edges,
    corners,
    windows,
    kernel_acc,
    turned,
    low_rows,
    field,
    low_corner_edges,
    low_corners,
    rims,
    low_halo,
    low_edges,
    low_sides,
    low_windows,
    pair_out,
    pair_in,
    owned,
    first_out,
    first_in,
    second_out,
    second_in,
    third,
    gathered,
    bias_bufs,
    load_sem,
    row_send,
    row_recv,
    col_send,
    col_recv,
    corner_send,
    corner_recv,
    low_corner_send,
    low_corner_recv,
    sends,
    recvs,
    bias_send,
    bias_recv,
):
    place = Place(sizes)
    hid = hidden_next.shape[0]
    width = grad_inputs.shape[0]
    partner, _ = place.peer("core", 1)
    devices = place.around()
    for axis in ("z", "y", "x"):
        devices += [device for _, device, _ in reversed(place.peers(axis))]
    devices.append(partner)
    barrier = greet(devices)
    mine = pl.multiple_of(place.core * HALF, HALF)
    theirs = pl.multiple_of((1 - place.core) * HALF, HALF)
    pending = []

    sources = (below_hbm, hidden_hbm, weights_hbm, cell_hbm, hidden_grad_hbm, gate_bias_hbm, readout_hbm,
               target_hbm, land_hbm, fire_hbm)
    targets = (below, hidden, weights, cell_prev, hidden_grad, gate_bias, readout, target, land, fire)
    loads = [
        pltpu.make_async_copy(source, destination, load_sem.at[i])
        for i, (source, destination) in enumerate(zip(sources, targets))
    ]
    for load in loads:
        load.start()

    loads[0].wait()
    wide[pl.ds(0, width * ROWS), :] = below[...].astype(F32).reshape(width * ROWS, COLS)
    loads[1].wait()
    wide[pl.ds(width * ROWS, hid * ROWS), :] = hidden[...].astype(F32).reshape(hid * ROWS, COLS)

    def state_row(r):
        return wide[pl.ds(r, STATE, stride=ROWS), :]

    for r in (0, ROWS - 1):
        rows[r + 1] = state_row(r).astype(BF16)
    pl.semaphore_wait(barrier, len(devices))
    row_copies, row_waits = rows_out(place, rows.at[1], rows.at[ROWS], halo, row_send.at[0], row_recv.at[0])

    lanes = lane_ids((STATE, COLS))
    east = jnp.zeros((STATE, COLS), F32)
    west = jnp.zeros((STATE, COLS), F32)
    for r in range(ROWS):
        value = state_row(r)
        if 0 < r < ROWS - 1:
            rows[r + 1] = value.astype(BF16)
        east = collect(east, value, r + 1, r + 2, lanes)
        west = collect(west, value, r + 1, r + 1, lanes)
    ends = (to_edge(east), to_edge(west))
    for i in range(4):
        position = 1 if i < 2 else ROWS
        corner_edges[i] = jnp.broadcast_to(ends[i % 2][position : position + 1], (8, STATE))
    corner_copies, corner_waits = corners_out(place, corner_edges, corners, corner_send, corner_recv)
    edges[0] = ends[0].astype(BF16)
    edges[1] = ends[1].astype(BF16)
    col_copies = cols_out(place, edges, sides, col_send.at[0], col_recv.at[0])
    pending += row_copies + col_copies + corner_copies

    for load in loads[2:]:
        load.wait()
    wide_grad[...] = hidden_grad[...].astype(F32).reshape(hid * ROWS, COLS)
    bias_cols = jnp.transpose(jnp.broadcast_to(gate_bias[...], (LANES, GATES)))
    read_cols = jnp.transpose(jnp.broadcast_to(readout[...], (LANES, hid)))
    for t in range(9):
        turned[t] = jnp.transpose(weights[t].astype(F32)).astype(BF16)

    def open_windows(position, low, low_side, high_side):
        before, after = spread(low.astype(F32), low_side, high_side, lanes, position)
        windows[position, 0:STATE] = before.astype(BF16)
        windows[position, STATE : 2 * STATE] = low
        windows[position, 2 * STATE : 3 * STATE] = after.astype(BF16)

    for copy in col_copies:
        copy.wait_recv()
    low_side, high_side = from_edge(sides[0]), from_edge(sides[1])
    for position in range(1, PADDED - 1):
        open_windows(position, rows[position], low_side, high_side)

    flat = jnp.concatenate([weights[t] for t in range(9)], axis=1)

    def cells_of(pair, bias_total):
        columns = jnp.concatenate([windows[r : r + 3].reshape(9 * STATE, COLS) for r in pair], axis=1)
        both = jnp.dot(flat, columns, preferred_element_type=F32)
        for k, r in enumerate(pair):
            preact = both[:, k * COLS : (k + 1) * COLS] + bias_cols
            input_gate = jax.nn.sigmoid(preact[0:hid])
            forget_gate = jax.nn.sigmoid(preact[hid : 2 * hid])
            output_gate = jax.nn.sigmoid(preact[2 * hid : 3 * hid])
            candidate = jnp.tanh(preact[3 * hid : 4 * hid])
            land_row = land[r : r + 1, :].astype(F32)
            fire_row = fire[r : r + 1, :].astype(F32)
            prev = cell_prev[pl.ds(r, hid, stride=ROWS), :]
            cell = land_row * (forget_gate * prev + input_gate * candidate)
            squashed = jnp.tanh(cell)
            new_hidden = (output_gate * squashed).astype(BF16).astype(F32)
            predicted = jnp.sum(read_cols * new_hidden, axis=0, keepdims=True)
            miss = 2.0 * (fire_row * (predicted - target[r : r + 1, :]))
            total_grad = wide_grad[pl.ds(r, hid, stride=ROWS), :] + miss * read_cols
            cell_grad = land_row * total_grad * output_gate * (1.0 - squashed * squashed)
            pre_grad = jnp.concatenate(
                [
                    cell_grad * candidate * input_gate * (1.0 - input_gate),
                    cell_grad * prev * forget_gate * (1.0 - forget_gate),
                    total_grad * squashed * output_gate * (1.0 - output_gate),
                    cell_grad * input_gate * (1.0 - candidate * candidate),
                ],
                axis=0,
            )
            cell_next[pl.ds(r, hid, stride=ROWS), :] = cell
            grad_cell[pl.ds(r, hid, stride=ROWS), :] = cell_grad * forget_gate
            wide[pl.ds(r, hid, stride=ROWS), :] = new_hidden
            bias_total = bias_total + pre_grad
            low_rows[r] = pre_grad.astype(BF16)
        return bias_total

    def kernel_terms(cells, rows_in, a):
        seen = jnp.concatenate([windows[r + a] for r in rows_in], axis=1)
        return lax.dot_general(cells, seen, (((1,), (1,)), ((), ())), preferred_element_type=F32)

    bias_total = jnp.zeros((GATES, COLS), F32)
    for pair in EARLY:
        bias_total = cells_of(pair, bias_total)
    cells = jnp.concatenate([low_rows[r] for r in range(1, ROWS - 1)], axis=1)
    for a in range(3):
        kernel_acc[a] = kernel_terms(cells, range(1, ROWS - 1), a)

    for wait in row_waits + corner_waits:
        wait.wait_recv()
    for slot, position in ((0, 0), (1, PADDED - 1)):
        ends = [jnp.transpose(jnp.broadcast_to(corners[slot, side, 0:1], (LANES, STATE))) for side in range(2)]
        open_windows(position, halo[slot], *ends)
    bias_total = cells_of(LATE, bias_total)

    halves = [pl.ds(theirs, HALF), pl.ds(mine, HALF)]
    cells = jnp.concatenate(
        [jnp.concatenate([low_rows[r, half, :] for r in LATE], axis=1) for half in halves], axis=0
    )
    pair_copies = {}
    for a in (2, 0, 1):
        part = kernel_terms(cells, LATE, a)
        given = part[0:HALF] + kernel_acc[a, halves[0], :]
        kept = part[HALF:] + kernel_acc[a, halves[1], :]
        for b in range(3):
            pair_out[a, b] = given[:, b * STATE : (b + 1) * STATE].astype(BF16)
        copy = remote(pair_out.at[a], pair_in.at[a], sends.at[0, a, 0], recvs.at[0, a, 0], partner)
        copy.start()
        pair_copies[a] = copy
        for b in range(3):
            owned[a, b] = kept[:, b * STATE : (b + 1) * STATE]

    first_copies = {}
    for a in (2, 0, 1):
        pair_copies[a].wait_recv()
        total = owned[a] + pair_in[a].astype(F32)
        owned[a] = total
        first_out[a] = total.astype(BF16)
        axis = ORDERS[a][0]
        rows1 = HALF // place.count[axis]
        copies = []
        for k, device, other in reversed(place.peers(axis)):
            start = pl.multiple_of(other * rows1, rows1)
            copy = remote(
                first_out.at[a, :, pl.ds(start, rows1), :],
                first_in[a].at[k],
                sends.at[1, a, k],
                recvs.at[1, a, k],
                device,
            )
            copy.start()
            copies.append(copy)
        first_copies[a] = copies
    pending += pair_copies.values()

    def bias_start(stage, axis, value):
        slot = place.index[axis]
        buf = bias_bufs[stage]
        buf[slot] = value
        copies = []
        for k, device, _ in place.peers(axis):
            copy = remote(buf.at[slot], buf.at[slot], bias_send.at[stage, k], bias_recv.at[stage, k], device)
            copy.start()
            copies.append(copy)
        return copies

    def bias_finish(stage, axis, copies):
        buf = bias_bufs[stage]
        for copy in copies:
            copy.wait_recv()
        pending.extend(copies)
        total = buf[0]
        for k in range(1, place.count[axis]):
            total = total + buf[k]
        return total

    bias = lax.dot_general(
        jnp.ones((8, COLS), F32),
        bias_total,
        (((1,), (1,)), ((), ())),
        precision=lax.Precision.HIGHEST,
        preferred_element_type=F32,
    )
    bias_copies = bias_start(0, "core", bias)

    gate_lanes = lane_ids((GATES, COLS))
    east = jnp.zeros((GATES, COLS), F32)
    west = jnp.zeros((GATES, COLS), F32)
    for r in range(ROWS):
        value = low_rows[r].astype(F32)
        before = jnp.where(gate_lanes == 0, 0.0, pltpu.roll(value, 1, 1))
        after = jnp.where(gate_lanes == COLS - 1, 0.0, pltpu.roll(value, COLS - 1, 1))
        low_windows[r + 1, 0:GATES] = before.astype(BF16)
        low_windows[r + 1, GATES : 2 * GATES] = low_rows[r]
        low_windows[r + 1, 2 * GATES : 3 * GATES] = after.astype(BF16)
        east = collect(east, value, r + 1, r + 2, gate_lanes)
        west = collect(west, value, r + 1, r + 1, gate_lanes)
    for slot, (value, last) in enumerate(((east, 2), (west, 0))):
        shifts = jnp.concatenate([pltpu.roll(value, a % LANES, 1).astype(BF16) for a in (-1, 0, 1)], axis=0)
        taps = jnp.concatenate([turned[3 * a + last] for a in range(3)], axis=1)
        given_cells = to_edge(jnp.dot(taps, shifts, preferred_element_type=F32))
        low_edges[slot] = given_cells.astype(BF16)
        for i, position in ((slot, 0), (slot + 2, PADDED - 1)):
            low_corner_edges[i] = jnp.broadcast_to(given_cells[position : position + 1], (8, STATE))
    low_copies = cols_out(place, low_edges, low_sides, col_send.at[2], col_recv.at[2])
    low_corner_copies, low_corner_waits = corners_out(
        place, low_corner_edges, low_corners, low_corner_send, low_corner_recv
    )

    flipped = jnp.concatenate([turned[8 - q] for q in range(9)], axis=1)
    rims[0] = jnp.dot(flipped[:, 6 * GATES :], low_windows[1], preferred_element_type=F32).astype(BF16)
    rims[1] = jnp.dot(flipped[:, : 3 * GATES], low_windows[ROWS], preferred_element_type=F32).astype(BF16)
    row_copies, row_waits = rows_out(place, rims.at[0], rims.at[1], low_halo, row_send.at[1], row_recv.at[1])
    bias = bias_finish(0, "core", bias_copies)
    bias_copies = bias_start(1, "x", bias)

    second_copies = []

    def second_start(a):
        axis1, axis2, _ = ORDERS[a]
        n1, n2 = place.count[axis1], place.count[axis2]
        rows1 = HALF // n1
        rows2 = rows1 // n2
        for copy in reversed(first_copies[a]):
            copy.wait_recv()
        pending.extend(first_copies[a])
        start = pl.multiple_of(place.index[axis1] * rows1, rows1)
        total = owned[a, :, pl.ds(start, rows1), :]
        for k in range(n1 - 1):
            total = total + first_in[a][k].astype(F32)
        for p in range(n2):
            second_out[a][p] = total[:, p * rows2 : (p + 1) * rows2, :]
        copies = []
        for k, device, other in reversed(place.peers(axis2)):
            copy = remote(second_out[a].at[other], second_in[a].at[k], sends.at[2, a, k], recvs.at[2, a, k], device)
            copy.start()
            copies.append(copy)
        second_copies.append((a, copies))

    second_start(2)
    second_start(0)
    second_start(1)

    bias = bias_finish(1, "x", bias_copies)
    bias_copies = bias_start(2, "y", bias)

    third_copies = []
    for a, copies2 in sorted(second_copies, key=lambda entry: entry[0]):
        _, axis2, axis3 = ORDERS[a]
        for copy in reversed(copies2):
            copy.wait_recv()
        pending += copies2
        total = second_out[a][place.index[axis2]]
        for k in range(place.count[axis2] - 1):
            total = total + second_in[a][k]
        slot = place.index[axis3]
        third[a][slot] = total
        copies = []
        for k, device, _ in reversed(place.peers(axis3)):
            copy = remote(third[a].at[slot], third[a].at[slot], sends.at[3, a, k], recvs.at[3, a, k], device)
            copy.start()
            copies.append(copy)
        third_copies.append((a, copies))

    hidden_next[...] = wide[pl.ds(0, hid * ROWS), :].reshape(hid, ROWS, COLS).astype(BF16)
    low_windows[0] = jnp.zeros((3 * GATES, COLS), BF16)
    low_windows[PADDED - 1] = jnp.zeros((3 * GATES, COLS), BF16)
    for pair in range(ROWS // 2):
        blocks = [low_windows[r : r + 3].reshape(9 * GATES, COLS) for r in (2 * pair, 2 * pair + 1)]
        both = jnp.dot(flipped, jnp.concatenate(blocks, axis=1), preferred_element_type=F32)
        for k in range(2):
            field[2 * pair + k] = both[:, k * COLS : (k + 1) * COLS]
    for copy in low_copies:
        copy.wait_recv()
    low_side, high_side = from_edge(low_sides[0]), from_edge(low_sides[1])

    def arrived(low_side, high_side, position):
        first = jnp.where(lanes == 0, pltpu.roll(low_side, (-position) % LANES, 1), 0.0)
        last = jnp.where(lanes == COLS - 1, pltpu.roll(high_side, (COLS - 1 - position) % LANES, 1), 0.0)
        return first + last

    pending += low_copies + row_copies + low_corner_copies
    for r in range(ROWS):
        field[r] = field[r] + arrived(low_side, high_side, r + 1)
    bias = bias_finish(2, "y", bias_copies)
    bias_copies = bias_start(3, "z", bias)

    fourth_copies = []
    for a, copies3 in third_copies:
        _, axis2, axis3 = ORDERS[a]
        for copy in reversed(copies3):
            copy.wait_recv()
        pending += copies3
        total = third[a][0]
        for k in range(1, place.count[axis3]):
            total = total + third[a][k]
        slot = place.index[axis2]
        gathered[a][slot] = (total * scaling).astype(BF16)
        copies = []
        for k, device, _ in reversed(place.peers(axis2)):
            copy = remote(gathered[a].at[slot], gathered[a].at[slot], sends.at[4, a, k], recvs.at[4, a, k], device)
            copy.start()
            copies.append(copy)
        fourth_copies.append((a, copies))

    def block_of(a, owner):
        rows1 = HALF // place.count[ORDERS[a][0]]
        start = pl.multiple_of(mine + owner * rows1, rows1)
        return kernel_low.at[pl.ds(3 * a, 3), pl.ds(start, rows1), :]

    last_copies = []

    def forward(a, owner, slot):
        block = block_of(a, owner)
        copy = remote(block, block, sends.at[6, a, slot], recvs.at[6, a, slot], partner)
        copy.start()
        last_copies.append(copy)

    fifth_copies = []
    for a, copies4 in fourth_copies:
        axis1, axis2, _ = ORDERS[a]
        n1 = place.count[axis1]
        for copy in reversed(copies4):
            copy.wait_recv()
        pending += copies4
        block = block_of(a, place.index[axis1])
        block[...] = jnp.concatenate(
            [gathered[a][p].astype(F32) for p in range(place.count[axis2])], axis=1
        ).astype(BF16)
        copies = []
        for k, device, _ in reversed(place.peers(axis1)):
            copy = remote(block, block, sends.at[5, a, k], recvs.at[5, a, k], device)
            copy.start()
            copies.append((copy, k, lax.rem(place.index[axis1] + n1 - 1 - k, n1)))
        forward(a, place.index[axis1], n1 - 1)
        fifth_copies.append((a, copies))

    for slot, r in ((0, 0), (1, ROWS - 1)):
        row_waits[slot].wait_recv()
        for wait in low_corner_waits[2 * slot : 2 * slot + 2]:
            wait.wait_recv()
        ends = [jnp.transpose(jnp.broadcast_to(low_corners[slot, side, 0:1], (LANES, STATE))) for side in range(2)]
        given_cells = jnp.where(lanes == 0, ends[0], jnp.where(lanes == COLS - 1, ends[1], 0.0))
        field[r] = field[r] + low_halo[slot].astype(F32) + given_cells
    for r in range(ROWS):
        wide[pl.ds(r, STATE, stride=ROWS), :] = field[r]
    grad_inputs[...] = wide[pl.ds(0, width * ROWS), :].reshape(width, ROWS, COLS).astype(BF16)
    grad_hidden[...] = wide[pl.ds(width * ROWS, hid * ROWS), :].reshape(hid, ROWS, COLS).astype(BF16)

    arrivals = []
    for a, copies5 in fifth_copies:
        count = place.count[ORDERS[a][0]]
        arrivals += [(min(k + 1, count - 1 - k), a, copy, k, sender) for copy, k, sender in copies5]
    for _, a, copy, k, sender in sorted(arrivals, key=lambda entry: entry[:2]):
        copy.wait_recv()
        forward(a, sender, k)
        pending.append(copy)
    bias_sum[...] = bias_finish(3, "z", bias_copies) * scaling
    for copy in last_copies:
        copy.wait_recv()
    pending += last_copies
    for copy in pending:
        copy.wait_send()


def finish_kernel(
    hidden_next,
    cell_next,
    grad_inputs,
    grad_hidden,
    grad_cell,
    kernel_low,
    bias_sum,
    hidden_next_out,
    cell_next_out,
    grad_inputs_out,
    grad_hidden_out,
    grad_cell_out,
    kernel_out,
    bias_out,
    kernel_wide,
    sems,
):
    pairs = (
        (hidden_next, hidden_next_out),
        (cell_next, cell_next_out),
        (grad_inputs, grad_inputs_out),
        (grad_hidden, grad_hidden_out),
        (grad_cell, grad_cell_out),
        (bias_sum.at[0:1], bias_out),
    )
    copies = [pltpu.make_async_copy(source, target, sems.at[i]) for i, (source, target) in enumerate(pairs)]
    for copy in copies:
        copy.start()
    for a in range(3):
        taps = pl.ds(3 * a, 3)
        kernel_wide[taps] = kernel_low[taps].astype(F32)
        copy = pltpu.make_async_copy(kernel_wide.at[taps], kernel_out.at[taps], sems.at[len(pairs) + a])
        copy.start()
        copies.append(copy)
    for copy in copies:
        copy.wait()


def shape_of(shape, dtype):
    return jax.ShapeDtypeStruct(shape, dtype)


def body(
    sizes,
    inputs_below,
    hidden_prev,
    cell_prev,
    kernel_weights,
    gate_bias,
    readout,
    target_field,
    land_mask,
    fire_mask,
    hidden_grad,
):
    nx, ny, zh, zl = sizes
    count = {"x": nx, "y": ny, "z": zh * zl}
    hid = hidden_prev.shape[0]
    dma = pltpu.SemaphoreType.DMA
    scaling = 1.0 / math.sqrt(ROWS * nx * zh * 2 * COLS * ny * zl)
    most = max(nx, ny, zh * zl)
    chunk = []
    for axis1, axis2, axis3 in ORDERS:
        rows1 = HALF // count[axis1]
        chunk.append((count[axis1], rows1, count[axis2], rows1 // count[axis2], count[axis3]))
    cells = shape_of((hid, ROWS, COLS), BF16)
    wide_cells = shape_of((hid * ROWS, COLS), F32)
    inputs = (
        inputs_below,
        hidden_prev,
        cell_prev.reshape(hid * ROWS, COLS),
        kernel_weights,
        gate_bias.reshape(1, GATES),
        readout.reshape(1, hid),
        target_field,
        land_mask,
        fire_mask,
        hidden_grad,
    )
    results = pl.pallas_call(
        functools.partial(step_kernel, sizes, scaling),
        out_shape=[
            cells,
            wide_cells,
            cells,
            cells,
            wide_cells,
            shape_of((9, GATES, STATE), BF16),
            shape_of((8, GATES), F32),
        ],
        in_specs=[pl.BlockSpec(memory_space=pltpu.HBM)] * len(inputs),
        out_specs=[VMEM_SPEC] * 7,
        scratch_shapes=[pltpu.VMEM(value.shape, value.dtype) for value in inputs]
        + [
            pltpu.VMEM((STATE * ROWS, COLS), F32),
            pltpu.VMEM((hid * ROWS, COLS), F32),
            pltpu.VMEM((PADDED, STATE, COLS), BF16),
            pltpu.VMEM((2, STATE, COLS), BF16),
            pltpu.VMEM((2, EDGE, STATE), BF16),
            pltpu.VMEM((2, EDGE, STATE), BF16),
            pltpu.VMEM((4, 8, STATE), F32),
            pltpu.VMEM((2, 2, 8, STATE), F32),
            pltpu.VMEM((PADDED, 3 * STATE, COLS), BF16),
            pltpu.VMEM((3, GATES, 3 * STATE), F32),
            pltpu.VMEM((9, STATE, GATES), BF16),
            pltpu.VMEM((ROWS, GATES, COLS), BF16),
            pltpu.VMEM((ROWS, STATE, COLS), F32),
            pltpu.VMEM((4, 8, STATE), F32),
            pltpu.VMEM((2, 2, 8, STATE), F32),
            pltpu.VMEM((2, STATE, COLS), BF16),
            pltpu.VMEM((2, STATE, COLS), BF16),
            pltpu.VMEM((2, EDGE, STATE), BF16),
            pltpu.VMEM((2, EDGE, STATE), BF16),
            pltpu.VMEM((PADDED, 3 * GATES, COLS), BF16),
            pltpu.VMEM((3, 3, HALF, STATE), BF16),
            pltpu.VMEM((3, 3, HALF, STATE), BF16),
            pltpu.VMEM((3, 3, HALF, STATE), F32),
            pltpu.VMEM((3, 3, HALF, STATE), BF16),
            [pltpu.VMEM((n1 - 1, 3, r1, STATE), BF16) for n1, r1, _, _, _ in chunk],
            [pltpu.VMEM((n2, 3, r2, STATE), F32) for _, _, n2, r2, _ in chunk],
            [pltpu.VMEM((n2 - 1, 3, r2, STATE), F32) for _, _, n2, r2, _ in chunk],
            [pltpu.VMEM((n3, 3, r2, STATE), F32) for _, _, _, r2, n3 in chunk],
            [pltpu.VMEM((n2, 3, r2, STATE), BF16) for _, _, n2, r2, _ in chunk],
            [pltpu.VMEM((n, 8, GATES), F32) for n in (2, nx, ny, zh * zl)],
            dma((len(inputs),)),
            dma((2, 2)),
            dma((2, 2)),
            dma((3, 2)),
            dma((3, 2)),
            dma((4,)),
            dma((2, 2)),
            dma((4,)),
            dma((2, 2)),
            dma((7, 3, most)),
            dma((7, 3, most)),
            dma((4, most)),
            dma((4, most)),
        ],
        compiler_params=pltpu.CompilerParams(
            collective_id=0, has_side_effects=True, vmem_limit_bytes=VMEM_LIMIT
        ),
        name="whole_step",
    )(*[pltpu.with_memory_space_constraint(value, pltpu.HBM) for value in inputs])

    hidden_next, cell_next, grad_inputs, grad_hidden, grad_cell, grad_kernel, grad_bias = pl.pallas_call(
        finish_kernel,
        out_shape=[
            cells,
            wide_cells,
            cells,
            cells,
            wide_cells,
            shape_of((9, GATES, STATE), F32),
            shape_of((1, GATES), F32),
        ],
        in_specs=[VMEM_SPEC] * 7,
        out_specs=[pl.BlockSpec(memory_space=pltpu.HBM)] * 7,
        scratch_shapes=[pltpu.VMEM((9, GATES, STATE), F32), dma((9,))],
        compiler_params=pltpu.CompilerParams(vmem_limit_bytes=VMEM_LIMIT),
        name="results",
    )(*results)
    shape = (hid, ROWS, COLS)
    return (
        hidden_next,
        cell_next.reshape(shape),
        grad_inputs,
        grad_hidden,
        grad_cell.reshape(shape),
        grad_kernel,
        grad_bias.reshape(GATES),
    )


def solution(mesh):
    lat, lon = mesh.shape["lat"], mesh.shape["lon"]
    sizes = {(16, 32): (4, 8, 2, 4), (4, 4): (2, 2, 1, 2)}[(lat, lon)]
    cells = P(None, "lat", "lon")
    flat = P("lat", "lon")
    return jax.shard_map(
        functools.partial(body, sizes),
        mesh=mesh,
        in_specs=(cells, cells, cells, P(), P(), P(), flat, flat, flat, cells),
        out_specs=(cells, cells, cells, cells, cells, P(), P()),
        check_vma=False,
    )
```
